256 devices in a mesh: ax: 32 (over x, z_hi, core), az: 8 (over z_lo, y).
Axes of the slice: x: 4, y: 4, z: 8 (z_hi: 4, z_lo: 2; z = z_hi * 2 + z_lo), core: 2. Of those that a mesh axis runs over, the one named last changes fastest.
Arguments:
- initial: float32 [19, 64, 128, 256], P(None, 'ax', 'az'), as said below
- adjoint_seed: float32 [19, 64, 128, 256], P(None, 'ax', 'az'), may hold values from -6 to 6
- porosity: float32 [64, 128, 256], P('ax', 'az'), may hold values from 0.05 to 0.6
- cell_type: int32 [64, 128, 256], P('ax', 'az'), may hold values from 0 to 3
- region: int32 [64, 128, 256], P('ax', 'az'), may hold values from 0 to 64, as said below
Outputs:
- final_state: float32 [19, 64, 128, 256], P(None, 'ax', 'az')
- adjoint_state: float32 [19, 64, 128, 256], P(None, 'ax', 'az')
- sensitivity: float32 [64, 128, 256], P('ax', 'az')
- region_totals: float32 [64], replicated
The draws below stay inside these ranges and needn't reach their ends.
Inputs may be any that keep to these rules, and one draw needn't show every extreme that they name: `cell_type`: the cells of radial index 0 and 255 are walls. All design cells of one aligned block of 2 x 16 x 256 cells share one region; each region holds four such blocks. `initial`: populations are positive.
All inputs are finite; a program needn't handle non-finite values.
Results may differ from the reference program's by a relative error of at most 0.0003.
Values sent between devices are 32-bit elements; how exact they have to be, the bound alone decides.
A program may use at most 64 MiB of HBM per device.

```python
import jax
import jax.numpy as jnp
from jax import lax

CA = 2
CT = 16
NR = 256
NA = 64
NT = 128
NREG = 64


VELOCITY = [(0, 0, 0), (1, 0, 0), (-1, 0, 0), (0, 1, 0), (0, -1, 0), (0, 0, 1), (0, 0, -1), (1, 1, 0), (-1, -1, 0), (1, -1, 0), (-1, 1, 0), (1, 0, 1), (-1, 0, -1), (1, 0, -1), (-1, 0, 1), (0, 1, 1), (0, -1, -1), (0, 1, -1), (0, -1, 1)]


WEIGHTS = [1.0 / 3.0] + [1.0 / 18.0] * 6 + [1.0 / 36.0] * 12


def draw_initial(key, part):
    keys = jax.random.split(jax.random.fold_in(key, 11), 3)
    cells = (NA, NT, NR)
    density = 1.0 + 0.05 * jnp.clip(jax.random.normal(keys[0], cells, jnp.float32), -3.0, 3.0)
    velocity = jnp.clip(0.04 * jax.random.normal(keys[1], (3,) + cells, jnp.float32), -0.1, 0.1)
    noise = jnp.clip(jax.random.normal(keys[2], (19,) + cells, jnp.float32), -3.0, 3.0)
    speed_sq = velocity[0] * velocity[0] + velocity[1] * velocity[1] + velocity[2] * velocity[2]
    result = []
    for index_q in range(19):
        direc = VELOCITY[index_q]
        projected = direc[0] * velocity[0] + direc[1] * velocity[1] + direc[2] * velocity[2]
        balance = WEIGHTS[index_q] * density * (1.0 + 3.0 * projected + 4.5 * projected * projected - 1.5 * speed_sq)
        result.append(balance + 0.1 * WEIGHTS[index_q] * density * noise[index_q])
    return jnp.stack(result).astype(jnp.float32)


def draw_cell_type(key, part):
    rolls = jax.random.randint(jax.random.fold_in(key, 23), (NA, NT, NR), 0, 100)
    types = jnp.where(rolls < 10, 1, jnp.where(rolls < 13, 2, jnp.where(rolls < 16, 3, 0)))
    radial = jnp.arange(NR)[None, None, :]
    types = jnp.where((radial == 0) | (radial == NR - 1), 1, types)
    return types.astype(jnp.int32)


def draw_region(key, part):
    blocks_a = NA // CA
    blocks_t = NT // CT
    order = jax.random.permutation(jax.random.fold_in(key, 31), blocks_a * blocks_t)
    labels = (1 + order % NREG).reshape(blocks_a, blocks_t)
    labels = jnp.repeat(jnp.repeat(labels, CA, axis=0), CT, axis=1)
    chosen = jax.random.randint(jax.random.fold_in(key, 37), (NA, NT, NR), 0, 2)
    return (labels[:, :, None] * chosen).astype(jnp.int32)


def shard_levels(rng, dims, pieces, least, top_value):
    factor_of, own = 1.0, jax.random.fold_in(rng, 6)
    for position, blocks in pieces:
        steps = jnp.exp(jax.random.uniform(jax.random.fold_in(own, position), (blocks,), jnp.float32, least / len(pieces), top_value / len(pieces)))
        factor_of = factor_of * jnp.repeat(steps, dims[position] // blocks).reshape([-1 if axis == position else 1 for axis in range(len(dims))])
    return factor_of


def gaussian(rng, dims, width, most, cuts=(), dtype=jnp.bfloat16):
    drawn = jax.random.normal(rng, dims, jnp.float32) * width
    if len(cuts) > 0:
        drawn = shard_levels(rng, dims, cuts, -0.22, 0.18) * drawn
    return jnp.clip(drawn, min=-most, max=most).astype(dtype)


def setup_inputs(seed: int = 0) -> dict:
    seeds = jax.random.split(jax.random.key(seed), 6)
    initial = draw_initial(jax.random.fold_in(seeds[5], 71), 0)
    adjoint_seed = gaussian(seeds[1], (19, NA, NT, NR), 1.0, 6.0, ((1, 32), (2, 8)), jnp.float32)
    porosity = jnp.clip(0.05 + 0.55 * jax.random.uniform(seeds[2], (NA, NT, NR), jnp.float32) ** shard_levels(seeds[2], (NA, NT, NR), ((0, 32), (1, 8)), -0.2, 0.2), 0.05, 0.6)
    cell_type = draw_cell_type(jax.random.fold_in(seeds[5], 71), 0)
    region = draw_region(jax.random.fold_in(seeds[5], 71), 0)
    return dict(initial=initial, adjoint_seed=adjoint_seed, porosity=porosity, cell_type=cell_type, region=region)


VELOCITY = [(0, 0, 0), (1, 0, 0), (-1, 0, 0), (0, 1, 0), (0, -1, 0), (0, 0, 1), (0, 0, -1), (1, 1, 0), (-1, -1, 0), (1, -1, 0), (-1, 1, 0), (1, 0, 1), (-1, 0, -1), (1, 0, -1), (-1, 0, 1), (0, 1, 1), (0, -1, -1), (0, 1, -1), (0, -1, 1)]
OPPOSITE = [0, 2, 1, 4, 3, 6, 5, 8, 7, 10, 9, 12, 11, 14, 13, 16, 15, 18, 17]
WEIGHTS = [1.0 / 3.0] + [1.0 / 18.0] * 6 + [1.0 / 36.0] * 12
INLET_SPEED = (0.05, 0.05, 0.0)
HIGH = lax.Precision.HIGHEST

def equilibrium(density, velocity):
    table = jnp.array(VELOCITY, jnp.float32)
    weights = jnp.array(WEIGHTS, jnp.float32).reshape((19,) + (1,) * density.ndim)
    projected = jnp.einsum('qk,k...->q...', table, velocity, precision=HIGH)
    speed_sq = lax.optimization_barrier(jnp.sum(velocity * velocity, axis=0))
    return weights * density * (1.0 + 3.0 * projected + 4.5 * projected * projected - 1.5 * speed_sq)

def collide(pops, porous, types, regions):
    table = jnp.array(VELOCITY, jnp.float32)
    weights = jnp.array(WEIGHTS, jnp.float32).reshape((19,) + (1,) * (pops.ndim - 1))
    density = lax.optimization_barrier(jnp.sum(pops, axis=0))
    momentum = jnp.einsum('qk,q...->k...', table, pops, precision=HIGH)
    velocity = momentum / density
    balance = equilibrium(density, velocity)
    departure = pops - balance
    moments = []
    for first_k, second_k in ((0, 0), (1, 1), (2, 2), (0, 1), (0, 2), (1, 2)):
        factors = table[:, first_k] * table[:, second_k]
        moments.append(jnp.einsum('q,q...->...', factors, departure, precision=HIGH))
    stress_sq = moments[0] ** 2 + moments[1] ** 2 + moments[2] ** 2 + 2.0 * (moments[3] ** 2 + moments[4] ** 2 + moments[5] ** 2)
    shear = 1.5 * jnp.sqrt(stress_sq + 0.0001) / density
    viscous = 0.02 * (shear + 0.01) ** (0.7 - 1.0)
    relax = 0.5 + 3.0 * viscous
    design = (regions > 0).astype(jnp.float32)
    relaxed = pops - departure / relax - porous * design * (balance - weights * density)
    unity = jnp.ones_like(density)
    inlet_vel = jnp.array(INLET_SPEED, jnp.float32).reshape((3,) + (1,) * density.ndim) * unity
    inflow = equilibrium(unity, inlet_vel)
    outflow = equilibrium(unity, velocity)
    return jnp.where(types == 2, inflow, jnp.where(types == 3, outflow, relaxed))

def displaced(field, shift_a, shift_t, shift_r):
    rolled = jnp.roll(field, -shift_t, axis=1)
    padded = jnp.pad(rolled, ((1, 1), (0, 0), (1, 1)))
    rows_a, rows_r = (field.shape[0], field.shape[2])
    return padded[1 + shift_a:1 + shift_a + rows_a, :, 1 + shift_r:1 + shift_r + rows_r]

def stream(post, flags):
    result = []
    for index_q in range(19):
        direc = VELOCITY[index_q]
        source_ok = displaced(flags, -direc[0], -direc[1], -direc[2]) > 0
        moved = displaced(post[index_q], -direc[0], -direc[1], -direc[2])
        result.append(jnp.where(source_ok, moved, post[OPPOSITE[index_q]]))
    return jnp.stack(result)

def stream_adjoint(adjoint, flags):
    result = []
    for index_q in range(19):
        direc = VELOCITY[index_q]
        ahead = displaced(adjoint[index_q], direc[0], direc[1], direc[2])
        blocked = 1.0 - displaced(flags, direc[0], direc[1], direc[2])
        result.append(flags * ahead + blocked * adjoint[OPPOSITE[index_q]])
    return jnp.stack(result)

def collide_all(pops, porous, types, regions):

    def one_row(entries):
        return collide(entries[0], entries[1], entries[2], entries[3])
    mapped = lax.map(one_row, (jnp.moveaxis(pops, 1, 0), porous, types, regions))
    return jnp.moveaxis(mapped, 0, 1)

def adjoint_all(upstream, pops, porous, types, regions):

    def one_row(entries):
        row_types, row_regions = (entries[3], entries[4])
        primal, pullback = jax.vjp(lambda current, coefficient: collide(current, coefficient, row_types, row_regions), entries[1], entries[2])
        return pullback(entries[0])
    back_pops, back_porous = lax.map(one_row, (jnp.moveaxis(upstream, 1, 0), jnp.moveaxis(pops, 1, 0), porous, types, regions))
    return (jnp.moveaxis(back_pops, 0, 1), back_porous)

def reference(initial, adjoint_seed, porosity, cell_type, region):
    flags = (cell_type != 1).astype(jnp.float32)
    state_one = stream(collide_all(initial, porosity, cell_type, region), flags)
    final_state = stream(collide_all(state_one, porosity, cell_type, region), flags)
    adjoint = adjoint_seed
    sensitivity = jnp.zeros(porosity.shape, jnp.float32)
    for recorded in (state_one, initial):
        upstream = stream_adjoint(adjoint, flags)
        adjoint, partial_sens = adjoint_all(upstream, recorded, porosity, cell_type, region)
        sensitivity = sensitivity + partial_sens
    totals = jax.ops.segment_sum(sensitivity.reshape(-1), region.reshape(-1), num_segments=NREG + 1)[1:]
    return (final_state, adjoint, sensitivity, totals)
```

```python
import functools

import jax
import jax.numpy as jnp
from jax import lax
from jax.experimental import pallas as pl
from jax.experimental.pallas import tpu as pltpu
from jax.sharding import PartitionSpec as P

MESH = pl.DeviceIdType.MESH

VELOCITY = [
    (0, 0, 0),
    (1, 0, 0),
    (-1, 0, 0),
    (0, 1, 0),
    (0, -1, 0),
    (0, 0, 1),
    (0, 0, -1),
    (1, 1, 0),
    (-1, -1, 0),
    (1, -1, 0),
    (-1, 1, 0),
    (1, 0, 1),
    (-1, 0, -1),
    (1, 0, -1),
    (-1, 0, 1),
    (0, 1, 1),
    (0, -1, -1),
    (0, 1, -1),
    (0, -1, 1),
]
OPPOSITE = [0, 2, 1, 4, 3, 6, 5, 8, 7, 10, 9, 12, 11, 14, 13, 16, 15, 18, 17]
WEIGHTS = [1.0 / 3.0] + [1.0 / 18.0] * 6 + [1.0 / 36.0] * 12
INLET_SPEED = (0.05, 0.05, 0.0)
HIGH = lax.Precision.HIGHEST


def extended_2(x, sides, width):
    for axis, dim in sides:
        peers, length = (lax.axis_size(axis), x.shape[dim])
        up = [(i, (i + 1) % peers) for i in range(peers)]
        down = [(j, i) for i, j in up]
        last = lax.slice_in_dim(x, length - width, length, axis=dim)
        leading = lax.slice_in_dim(x, 0, width, axis=dim)
        before = lax.ppermute(last, axis, up)
        after = lax.ppermute(leading, axis, down)
        x = jnp.concatenate([before, x, after], axis=dim)
    return x


def equilibrium(density, velocity):
    table = jnp.array(VELOCITY, jnp.float32)
    weights = jnp.array(WEIGHTS, jnp.float32).reshape((19,) + (1,) * density.ndim)
    projected = jnp.einsum("qk,k...->q...", table, velocity, precision=HIGH)
    speed_sq = jnp.sum(velocity * velocity, axis=0)
    return (
        weights * density * (1.0 + 3.0 * projected + 4.5 * projected * projected - 1.5 * speed_sq)
    )


def collide(pops, porous, types, regions):
    table = jnp.array(VELOCITY, jnp.float32)
    weights = jnp.array(WEIGHTS, jnp.float32).reshape((19,) + (1,) * (pops.ndim - 1))
    density = jnp.sum(pops, axis=0)
    momentum = jnp.einsum("qk,q...->k...", table, pops, precision=HIGH)
    velocity = momentum / density
    balance = equilibrium(density, velocity)
    departure = pops - balance
    moments = []
    for first_k, second_k in ((0, 0), (1, 1), (2, 2), (0, 1), (0, 2), (1, 2)):
        factors = table[:, first_k] * table[:, second_k]
        moments.append(jnp.einsum("q,q...->...", factors, departure, precision=HIGH))
    stress_sq = (
        moments[0] ** 2
        + moments[1] ** 2
        + moments[2] ** 2
        + 2.0 * (moments[3] ** 2 + moments[4] ** 2 + moments[5] ** 2)
    )
    shear = 1.5 * jnp.sqrt(stress_sq + 0.0001) / density
    viscous = 0.02 * (shear + 0.01) ** (0.7 - 1.0)
    relax = 0.5 + 3.0 * viscous
    design = (regions > 0).astype(jnp.float32)
    relaxed = pops - departure / relax - porous * design * (balance - weights * density)
    unity = jnp.ones_like(density)
    inlet_vel = jnp.array(INLET_SPEED, jnp.float32).reshape((3,) + (1,) * density.ndim) * unity
    inflow = equilibrium(unity, inlet_vel)
    outflow = equilibrium(unity, velocity)
    return jnp.where(types == 2, inflow, jnp.where(types == 3, outflow, relaxed))


def clipped(extended, shift_a, shift_t, shift_r):
    leading = extended.ndim - 3
    padded = jnp.pad(extended, [(0, 0)] * leading + [(0, 0), (0, 0), (1, 1)])
    rows_a, rows_t, rows_r = (extended.shape[-3], extended.shape[-2], extended.shape[-1])
    return padded[
        ...,
        1 + shift_a : rows_a - 1 + shift_a,
        1 + shift_t : rows_t - 1 + shift_t,
        1 + shift_r : 1 + shift_r + rows_r,
    ]


def stream(post_ext, flag_ext):
    result = []
    for index_q in range(19):
        direc = VELOCITY[index_q]
        source_ok = clipped(flag_ext, -direc[0], -direc[1], -direc[2]) > 0
        moved = clipped(post_ext[index_q], -direc[0], -direc[1], -direc[2])
        result.append(jnp.where(source_ok, moved, clipped(post_ext[OPPOSITE[index_q]], 0, 0, 0)))
    return jnp.stack(result)


def stream_adjoint(adjoint_ext, flag_ext):
    centre_flag = clipped(flag_ext, 0, 0, 0)
    result = []
    for index_q in range(19):
        direc = VELOCITY[index_q]
        ahead = clipped(adjoint_ext[index_q], direc[0], direc[1], direc[2])
        blocked = 1.0 - clipped(flag_ext, direc[0], direc[1], direc[2])
        result.append(
            centre_flag * ahead + blocked * clipped(adjoint_ext[OPPOSITE[index_q]], 0, 0, 0)
        )
    return jnp.stack(result)


def forward_extend(post_own):
    return extended_2(post_own, (("ax", 1), ("az", 2)), 1)


def adjoint_extend(adjoint):
    return extended_2(adjoint, (("ax", 1), ("az", 2)), 1)


def shards(initial, adjoint_seed, porosity, cell_type, region):
    rows_a = cell_type.shape[0]
    types_wide, region_wide = (
        extended_2(cell_type, (("ax", 0), ("az", 1)), 2),
        extended_2(region, (("ax", 0), ("az", 1)), 2),
    )
    global_row = lax.axis_index("ax") * rows_a - 2 + jnp.arange(rows_a + 4, dtype=jnp.int32)
    inside = ((global_row >= 0) & (global_row < rows_a * lax.axis_size("ax"))).astype(jnp.float32)[
        :, None, None
    ]
    flag_wide = (types_wide != 1).astype(jnp.float32) * inside
    flag_near = flag_wide[1:-1, 1:-1]
    inside_near = inside[1:-1]
    current = initial
    recorded = []
    for step_no in range(2):
        post_own = collide(current, porosity, cell_type, region)
        post_ext = forward_extend(post_own)
        current = stream(post_ext, flag_near)
        recorded.append(current)
    state_one = recorded[0]
    adjoint = adjoint_seed
    sensitivity = jnp.zeros(porosity.shape, jnp.float32)
    for linear_at in (state_one, initial):
        adjoint_ext = adjoint_extend(adjoint) * inside_near
        upstream = stream_adjoint(adjoint_ext, flag_near)
        primal, pullback = jax.vjp(
            lambda current_f, coefficient: collide(current_f, coefficient, cell_type, region),
            linear_at,
            porosity,
        )
        adjoint, partial_sens = pullback(upstream)
        sensitivity = sensitivity + partial_sens
    region_count = lax.axis_size("ax") * lax.axis_size("az") // 4
    labels = jnp.arange(1, region_count + 1, dtype=jnp.int32)
    selector = (region.reshape(1, -1) == labels[:, None]).astype(jnp.float32)
    partial_tot = jnp.dot(selector, sensitivity.reshape(-1), precision=HIGH)
    totals = total_over_mesh(partial_tot)
    return (current, adjoint, sensitivity, totals)


def _total_kernel(n_ax, n_az, x_ref, o_ref, row_a, row_b, mid, send_a, recv_a, send_b, recv_b, local):
    me_ax, me_az = lax.axis_index("ax"), lax.axis_index("az")
    barrier = pltpu.get_barrier_semaphore()
    for k in range(1, n_az):
        pl.semaphore_signal(barrier, 1, device_id=(me_ax, lax.rem(me_az + k, n_az)), device_id_type=MESH)
    for k in range(1, n_ax):
        pl.semaphore_signal(barrier, 1, device_id=(lax.rem(me_ax + k, n_ax), me_az), device_id_type=MESH)
    pl.semaphore_wait(barrier, n_az - 1 + n_ax - 1)

    own = pltpu.make_async_copy(x_ref, row_a.at[me_az], local.at[0])
    own.start()
    sends = []
    for k in range(1, n_az):
        copy = pltpu.make_async_remote_copy(
            src_ref=x_ref,
            dst_ref=row_a.at[me_az],
            send_sem=send_a.at[k],
            recv_sem=recv_a.at[me_az],
            device_id=(me_ax, lax.rem(me_az + k, n_az)),
            device_id_type=MESH,
        )
        copy.start()
        sends.append(copy)
    own.wait()
    for k in range(1, n_az):
        source = lax.rem(me_az + n_az - k, n_az)
        pltpu.make_async_remote_copy(
            src_ref=x_ref,
            dst_ref=row_a.at[source],
            send_sem=send_a.at[k],
            recv_sem=recv_a.at[source],
            device_id=(me_ax, source),
            device_id_type=MESH,
        ).wait_recv()
    acc = row_a[0]
    for j in range(1, n_az):
        acc = acc + row_a[j]
    mid[...] = acc

    own = pltpu.make_async_copy(mid, row_b.at[me_ax], local.at[1])
    own.start()
    own.wait()
    for k in range(1, n_ax):
        copy = pltpu.make_async_remote_copy(
            src_ref=row_b.at[me_ax],
            dst_ref=row_b.at[me_ax],
            send_sem=send_b.at[k],
            recv_sem=recv_b.at[me_ax],
            device_id=(lax.rem(me_ax + k, n_ax), me_az),
            device_id_type=MESH,
        )
        copy.start()
        sends.append(copy)
    for k in range(1, n_ax):
        source = lax.rem(me_ax + n_ax - k, n_ax)
        pltpu.make_async_remote_copy(
            src_ref=row_b.at[me_ax],
            dst_ref=row_b.at[source],
            send_sem=send_b.at[k],
            recv_sem=recv_b.at[source],
            device_id=(source, me_az),
            device_id_type=MESH,
        ).wait_recv()
    acc = row_b[0]
    for j in range(1, n_ax):
        acc = acc + row_b[j]
    o_ref[...] = acc
    for copy in sends:
        copy.wait_send()


def total_over_mesh(partial):
    n_ax, n_az = lax.axis_size("ax"), lax.axis_size("az")
    row = partial.reshape(1, -1)
    out = pl.pallas_call(
        functools.partial(_total_kernel, n_ax, n_az),
        out_shape=jax.ShapeDtypeStruct(row.shape, row.dtype),
        in_specs=[pl.BlockSpec(memory_space=pltpu.VMEM)],
        out_specs=pl.BlockSpec(memory_space=pltpu.VMEM),
        scratch_shapes=[
            pltpu.VMEM((n_az,) + row.shape, row.dtype),
            pltpu.VMEM((n_ax,) + row.shape, row.dtype),
            pltpu.VMEM(row.shape, row.dtype),
            pltpu.SemaphoreType.DMA((n_az,)),
            pltpu.SemaphoreType.DMA((n_az,)),
            pltpu.SemaphoreType.DMA((n_ax,)),
            pltpu.SemaphoreType.DMA((n_ax,)),
            pltpu.SemaphoreType.DMA((2,)),
        ],
        compiler_params=pltpu.CompilerParams(collective_id=0, has_side_effects=True),
    )(row)
    return out.reshape(partial.shape)


def solution(mesh):
    return jax.shard_map(
        shards,
        mesh=mesh,
        in_specs=(
            P(None, "ax", "az", None),
            P(None, "ax", "az", None),
            P("ax", "az", None),
            P("ax", "az", None),
            P("ax", "az", None),
        ),
        out_specs=(P(None, "ax", "az", None), P(None, "ax", "az", None), P("ax", "az", None), P()),
        check_vma=False,
    )
```

```python
import functools

import numpy as np

import jax
import jax.numpy as jnp
from jax import lax
from jax.experimental import pallas as pl
from jax.experimental.pallas import tpu as pltpu
from jax.sharding import PartitionSpec as P

MESH = pl.DeviceIdType.MESH

VELOCITY = [
    (0, 0, 0),
    (1, 0, 0),
    (-1, 0, 0),
    (0, 1, 0),
    (0, -1, 0),
    (0, 0, 1),
    (0, 0, -1),
    (1, 1, 0),
    (-1, -1, 0),
    (1, -1, 0),
    (-1, 1, 0),
    (1, 0, 1),
    (-1, 0, -1),
    (1, 0, -1),
    (-1, 0, 1),
    (0, 1, 1),
    (0, -1, -1),
    (0, 1, -1),
    (0, -1, 1),
]
OPPOSITE = [0, 2, 1, 4, 3, 6, 5, 8, 7, 10, 9, 12, 11, 14, 13, 16, 15, 18, 17]
WEIGHTS = [1.0 / 3.0] + [1.0 / 18.0] * 6 + [1.0 / 36.0] * 12
INLET_SPEED = (0.05, 0.05, 0.0)
NQ = 19
TILE = 8


def _inflow_constants():
    w = np.array(WEIGHTS, np.float32)
    u = np.array(INLET_SPEED, np.float32)
    c = np.array(VELOCITY, np.float32)
    proj = (c * u[None, :]).sum(1, dtype=np.float32).astype(np.float32)
    usq = np.float32((u * u).sum(dtype=np.float32))
    one = np.float32(1.0)
    val = w * one * (one + np.float32(3.0) * proj + np.float32(4.5) * proj * proj - np.float32(1.5) * usq)
    return [float(v) for v in val.astype(np.float32)]


INFLOW = _inflow_constants()


def _combo(values, coeffs):
    acc = None
    for v, c in zip(values, coeffs):
        if c == 0:
            continue
        term = v if c == 1 else (-v if c == -1 else c * v)
        acc = term if acc is None else acc + term
    return acc


def _equilibrium(rho, u):
    usq = u[0] * u[0] + u[1] * u[1] + u[2] * u[2]
    out = []
    for q in range(NQ):
        p = _combo(u, VELOCITY[q])
        if p is None:
            inner = 1.0 - 1.5 * usq
        else:
            inner = 1.0 + 3.0 * p + 4.5 * p * p - 1.5 * usq
        out.append(WEIGHTS[q] * rho * inner)
    return out


def _collide(f, porous, types, regions):
    rho = f[0]
    for q in range(1, NQ):
        rho = rho + f[q]
    u = [_combo(f, [VELOCITY[q][k] for q in range(NQ)]) / rho for k in range(3)]
    feq = _equilibrium(rho, u)
    g = [f[q] - feq[q] for q in range(NQ)]
    moments = []
    for a, b in ((0, 0), (1, 1), (2, 2), (0, 1), (0, 2), (1, 2)):
        moments.append(_combo(g, [VELOCITY[q][a] * VELOCITY[q][b] for q in range(NQ)]))
    stress_sq = (
        moments[0] * moments[0]
        + moments[1] * moments[1]
        + moments[2] * moments[2]
        + 2.0 * (moments[3] * moments[3] + moments[4] * moments[4] + moments[5] * moments[5])
    )
    shear = 1.5 * jnp.sqrt(stress_sq + 0.0001) / rho
    viscous = 0.02 * (shear + 0.01) ** (0.7 - 1.0)
    relax = 0.5 + 3.0 * viscous
    design = jnp.where(regions > 0, 1.0, 0.0).astype(jnp.float32)
    damp = porous * design
    outflow = _equilibrium(jnp.ones_like(rho), u)
    inlet = types == 2
    outlet = types == 3
    out = []
    for q in range(NQ):
        relaxed = f[q] - g[q] / relax - damp * (feq[q] - WEIGHTS[q] * rho)
        out.append(jnp.where(inlet, INFLOW[q], jnp.where(outlet, outflow[q], relaxed)))
    return out


def _pieces(sign):
    out = []
    for q in range(NQ):
        oa, ot = sign * VELOCITY[q][0], sign * VELOCITY[q][1]
        if oa != 0:
            out.append((q, "a", oa, ot))
        if ot != 0:
            out.append((q, "t", oa, ot))
        if oa != 0 and ot != 0:
            out.append((q, "c", oa, ot))
    return out


FLAG_PIECES = [
    (0, "a", 1, 0),
    (0, "a", -1, 0),
    (0, "t", 0, 1),
    (0, "t", 0, -1),
    (0, "c", 1, 1),
    (0, "c", 1, -1),
    (0, "c", -1, 1),
    (0, "c", -1, -1),
]
NPIECE = 24


class Halo:
    def __init__(self, a_lo, a_hi, t_lo, t_hi):
        self.a_lo, self.a_hi, self.t_lo, self.t_hi = a_lo, a_hi, t_lo, t_hi


def _piece_refs(piece, field, halo, ca, ct):
    q, kind, oa, ot = piece
    a_face = ca - 1 if oa == -1 else 0
    t_face = ct - 1 if ot == -1 else 0
    if kind == "a":
        src = field.at[q, pl.ds(a_face, 1)]
        dst = (halo.a_lo if oa == -1 else halo.a_hi).at[q]
        move = (-oa, 0)
    elif kind == "t":
        src = field.at[q, :, pl.ds(t_face, 1)]
        dst = (halo.t_lo if ot == -1 else halo.t_hi).at[q, pl.ds(1, ca)]
        move = (0, -ot)
    else:
        src = field.at[q, pl.ds(a_face, 1), pl.ds(t_face, 1)]
        slot = 0 if oa == -1 else ca + 1
        dst = (halo.t_lo if ot == -1 else halo.t_hi).at[q, pl.ds(slot, 1)]
        move = (-oa, -ot)
    return src, dst, move


class Exchange:
    def __init__(self, pieces, field, halo, send_sem, recv_sem, pos, sizes, ca, ct):
        self.items = []
        me_ax, me_az = pos
        n_ax, n_az = sizes
        for i, piece in enumerate(pieces):
            src, dst, (da, dt) = _piece_refs(piece, field, halo, ca, ct)
            to_ax = me_ax + da
            from_ax = me_ax - da
            to_dev = (to_ax, lax.rem(me_az + dt + n_az, n_az))
            from_dev = (from_ax, lax.rem(me_az - dt + n_az, n_az))
            send = pltpu.make_async_remote_copy(
                src_ref=src, dst_ref=dst, send_sem=send_sem.at[i], recv_sem=recv_sem.at[i],
                device_id=to_dev, device_id_type=MESH)
            recv = pltpu.make_async_remote_copy(
                src_ref=src, dst_ref=dst, send_sem=send_sem.at[i], recv_sem=recv_sem.at[i],
                device_id=from_dev, device_id_type=MESH)
            send_ok = jnp.logical_and(to_ax >= 0, to_ax < n_ax) if da != 0 else None
            recv_ok = jnp.logical_and(from_ax >= 0, from_ax < n_ax) if da != 0 else None
            self.items.append((send, recv, send_ok, recv_ok))

    @staticmethod
    def _maybe(ok, fn):
        if ok is None:
            fn()
        else:
            pl.when(ok)(fn)

    def start(self):
        for send, _, ok, _ in self.items:
            self._maybe(ok, send.start)

    def wait_recv(self):
        for _, recv, _, ok in self.items:
            self._maybe(ok, recv.wait_recv)

    def wait_send(self):
        for send, _, ok, _ in self.items:
            self._maybe(ok, send.wait_send)


def _shift(own, halo, q, a, oa, ot, orr, lo_ok, hi_ok, ca, ct, nr, zero_r):
    ae = a + oa
    ok = None
    if ae < 0:
        slab = halo.a_lo[q, 0]
        ok = lo_ok
    elif ae >= ca:
        slab = halo.a_hi[q, 0]
        ok = hi_ok
    else:
        slab = own[q, ae]
    if ot != 0:
        rows = lax.broadcasted_iota(jnp.int32, (ct, nr), 0)
        if ot == -1:
            edge = halo.t_lo[q, ae + 1]
            slab = jnp.where(rows == 0, edge, pltpu.roll(slab, 1, 0))
        else:
            edge = halo.t_hi[q, ae + 1]
            slab = jnp.where(rows == ct - 1, edge, pltpu.roll(slab, ct - 1, 0))
    if orr != 0:
        lanes = lax.broadcasted_iota(jnp.int32, (ct, nr), 1)
        if orr == -1:
            slab = jnp.where(lanes == 0, zero_r, pltpu.roll(slab, 1, 1))
        else:
            slab = jnp.where(lanes == nr - 1, zero_r, pltpu.roll(slab, nr - 1, 1))
    if ok is not None:
        slab = jnp.where(ok, slab, zero_r)
    return slab


def _window_kernel(
    n_ax, n_az,
    init_ref, seed_ref, por_ref, type_ref, reg_ref,
    final_ref, adj_ref, sens_ref, part_ref,
    post0, state1, back1, post1, adj1, back0, sens1,
    pop_a_lo, pop_a_hi, pop_t_lo, pop_t_hi,
    ty_a_lo, ty_a_hi, ty_t_lo, ty_t_hi,
    send_sem, recv_sem, ty_send, ty_recv,
):
    _, ca, ct, nr = init_ref.shape
    me_ax, me_az = lax.axis_index("ax"), lax.axis_index("az")
    lo_ok = me_ax > 0
    hi_ok = me_ax < n_ax - 1
    pos, sizes = (me_ax, me_az), (n_ax, n_az)

    barrier = pltpu.get_barrier_semaphore()
    up_az, dn_az = lax.rem(me_az + 1, n_az), lax.rem(me_az + n_az - 1, n_az)
    for dz in (up_az, dn_az):
        pl.semaphore_signal(barrier, 1, device_id=(me_ax, dz), device_id_type=MESH)
    for ok, other in ((lo_ok, me_ax - 1), (hi_ok, me_ax + 1)):
        @pl.when(ok)
        def _():
            for dz in (me_az, up_az, dn_az):
                pl.semaphore_signal(barrier, 1, device_id=(other, dz), device_id_type=MESH)
    count = 2 + 3 * (lo_ok.astype(jnp.int32) + hi_ok.astype(jnp.int32))
    pl.semaphore_wait(barrier, count)

    def halo(k):
        return Halo(pop_a_lo.at[k], pop_a_hi.at[k], pop_t_lo.at[k], pop_t_hi.at[k])

    ty_halo = Halo(ty_a_lo, ty_a_hi, ty_t_lo, ty_t_hi)
    ex_types = Exchange(FLAG_PIECES, type_ref, ty_halo, ty_send, ty_recv, pos, sizes, ca, ct)
    ex_seed = Exchange(_pieces(1), seed_ref, halo(0), send_sem.at[0], recv_sem.at[0], pos, sizes, ca, ct)
    ex_types.start()
    ex_seed.start()

    steps = ca * (ct // TILE)

    def tile_at(i):
        a = i // (ct // TILE)
        t0 = pl.multiple_of((i % (ct // TILE)) * TILE, TILE)
        return a, pl.ds(t0, TILE)

    def load(ref, a, ts):
        return [ref[q, a, ts, :] for q in range(NQ)]

    def store(ref, a, ts, vals):
        for q in range(NQ):
            ref[q, a, ts, :] = vals[q]

    def collide_loop(src, dst):
        def body(i, carry):
            a, ts = tile_at(i)
            out = _collide(load(src, a, ts), por_ref[a, ts, :], type_ref[0, a, ts, :], reg_ref[a, ts, :])
            store(dst, a, ts, out)
            return carry
        lax.fori_loop(0, steps, body, 0)

    def vjp_loop(at, upstream, primal_dst, grad_dst, sens_dst, sens_add):
        def body(i, carry):
            a, ts = tile_at(i)
            types = type_ref[0, a, ts, :]
            regions = reg_ref[a, ts, :]
            out, pullback = jax.vjp(
                lambda f, p: _collide(f, p, types, regions), load(at, a, ts), por_ref[a, ts, :])
            if primal_dst is not None:
                store(primal_dst, a, ts, out)
            d_f, d_p = pullback(load(upstream, a, ts))
            store(grad_dst, a, ts, d_f)
            if sens_add is not None:
                d_p = d_p + sens_add[a, ts, :]
            sens_dst[a, ts, :] = d_p
            return carry
        lax.fori_loop(0, steps, body, 0)

    zero = jnp.zeros((ct, nr), jnp.float32)

    def flag_shift(a, oa, ot, orr):
        if oa == 0 and ot == 0 and orr == 0:
            own = type_ref[0, a]
            return jnp.where(own != 1, 1.0, 0.0).astype(jnp.float32)
        ty = _shift(type_ref, ty_halo, 0, a, oa, ot, orr, lo_ok, hi_ok, ca, ct, nr, jnp.ones((ct, nr), jnp.int32))
        return jnp.where(ty != 1, 1.0, 0.0).astype(jnp.float32)

    def stream(post, hal, dst):
        for a in range(ca):
            for q in range(NQ):
                c = VELOCITY[q]
                moved = _shift(post, hal, q, a, -c[0], -c[1], -c[2], lo_ok, hi_ok, ca, ct, nr, zero)
                ok = flag_shift(a, -c[0], -c[1], -c[2]) > 0
                dst[q, a] = jnp.where(ok, moved, post[OPPOSITE[q], a])

    def stream_adjoint(adj, hal, dst):
        for a in range(ca):
            centre = flag_shift(a, 0, 0, 0)
            for q in range(NQ):
                c = VELOCITY[q]
                ahead = _shift(adj, hal, q, a, c[0], c[1], c[2], lo_ok, hi_ok, ca, ct, nr, zero)
                blocked = 1.0 - flag_shift(a, c[0], c[1], c[2])
                dst[q, a] = centre * ahead + blocked * adj[OPPOSITE[q], a]

    collide_loop(init_ref, post0)
    ex_post0 = Exchange(_pieces(-1), post0, halo(1), send_sem.at[1], recv_sem.at[1], pos, sizes, ca, ct)
    ex_post0.start()
    ex_types.wait_recv()
    ex_post0.wait_recv()
    stream(post0, halo(1), state1)
    ex_seed.wait_recv()
    stream_adjoint(seed_ref, halo(0), back1)
    vjp_loop(state1, back1, post1, adj1, sens1, None)
    ex_post1 = Exchange(_pieces(-1), post1, halo(2), send_sem.at[2], recv_sem.at[2], pos, sizes, ca, ct)
    ex_adj1 = Exchange(_pieces(1), adj1, halo(3), send_sem.at[3], recv_sem.at[3], pos, sizes, ca, ct)
    ex_adj1.start()
    ex_post1.start()
    ex_adj1.wait_recv()
    stream_adjoint(adj1, halo(3), back0)
    vjp_loop(init_ref, back0, None, adj_ref, sens_ref, sens1)
    ex_post1.wait_recv()
    stream(post1, halo(2), final_ref)

    total = jnp.zeros((1, 1), jnp.float32)
    rid = jnp.zeros((1, 1), jnp.int32)
    for a in range(ca):
        reg = reg_ref[a]
        total = total + jnp.sum(jnp.where(reg > 0, sens_ref[a], 0.0), keepdims=True)
        rid = jnp.maximum(rid, jnp.max(reg, keepdims=True))
    labels = lax.broadcasted_iota(jnp.int32, part_ref.shape, 1) + 1
    part_ref[...] = jnp.where(labels == rid, total, 0.0)

    for ex in (ex_types, ex_seed, ex_post0, ex_post1, ex_adj1):
        ex.wait_send()


def window(initial, adjoint_seed, porosity, cell_type, region, n_regions):
    n_ax, n_az = lax.axis_size("ax"), lax.axis_size("az")
    nq, ca, ct, nr = initial.shape
    pop = jax.ShapeDtypeStruct(initial.shape, jnp.float32)
    cells = jax.ShapeDtypeStruct(porosity.shape, jnp.float32)
    vmem = pltpu.VMEM
    f32, i32 = jnp.float32, jnp.int32
    scratch = (
        [vmem((nq, ca, ct, nr), f32) for _ in range(6)]
        + [vmem((ca, ct, nr), f32)]
        + [vmem((4, nq, 1, ct, nr), f32), vmem((4, nq, 1, ct, nr), f32),
           vmem((4, nq, ca + 2, 1, nr), f32), vmem((4, nq, ca + 2, 1, nr), f32)]
        + [vmem((1, 1, ct, nr), i32), vmem((1, 1, ct, nr), i32),
           vmem((1, ca + 2, 1, nr), i32), vmem((1, ca + 2, 1, nr), i32)]
        + [pltpu.SemaphoreType.DMA((4, NPIECE)), pltpu.SemaphoreType.DMA((4, NPIECE)),
           pltpu.SemaphoreType.DMA((len(FLAG_PIECES),)), pltpu.SemaphoreType.DMA((len(FLAG_PIECES),))]
    )
    any_spec = pl.BlockSpec(memory_space=vmem)
    final, adj, sens, part = pl.pallas_call(
        functools.partial(_window_kernel, n_ax, n_az),
        out_shape=(pop, pop, cells, jax.ShapeDtypeStruct((1, n_regions), f32)),
        in_specs=[any_spec] * 5,
        out_specs=(any_spec,) * 4,
        scratch_shapes=scratch,
        compiler_params=pltpu.CompilerParams(collective_id=1, has_side_effects=True,
                                             vmem_limit_bytes=48 * 1024 * 1024),
    )(initial, adjoint_seed, porosity, cell_type.reshape((1,) + cell_type.shape), region)
    return final, adj, sens, part


def _total_kernel(n_ax, n_az, x_ref, o_ref, row_a, row_b, mid, send_a, recv_a, send_b, recv_b, local):
    me_ax, me_az = lax.axis_index("ax"), lax.axis_index("az")
    barrier = pltpu.get_barrier_semaphore()
    for k in range(1, n_az):
        pl.semaphore_signal(barrier, 1, device_id=(me_ax, lax.rem(me_az + k, n_az)), device_id_type=MESH)
    for k in range(1, n_ax):
        pl.semaphore_signal(barrier, 1, device_id=(lax.rem(me_ax + k, n_ax), me_az), device_id_type=MESH)
    pl.semaphore_wait(barrier, n_az - 1 + n_ax - 1)

    own = pltpu.make_async_copy(x_ref, row_a.at[me_az], local.at[0])
    own.start()
    sends = []
    for k in range(1, n_az):
        copy = pltpu.make_async_remote_copy(
            src_ref=x_ref,
            dst_ref=row_a.at[me_az],
            send_sem=send_a.at[k],
            recv_sem=recv_a.at[me_az],
            device_id=(me_ax, lax.rem(me_az + k, n_az)),
            device_id_type=MESH,
        )
        copy.start()
        sends.append(copy)
    own.wait()
    for k in range(1, n_az):
        source = lax.rem(me_az + n_az - k, n_az)
        pltpu.make_async_remote_copy(
            src_ref=x_ref,
            dst_ref=row_a.at[source],
            send_sem=send_a.at[k],
            recv_sem=recv_a.at[source],
            device_id=(me_ax, source),
            device_id_type=MESH,
        ).wait_recv()
    acc = row_a[0]
    for j in range(1, n_az):
        acc = acc + row_a[j]
    mid[...] = acc

    own = pltpu.make_async_copy(mid, row_b.at[me_ax], local.at[1])
    own.start()
    own.wait()
    for k in range(1, n_ax):
        copy = pltpu.make_async_remote_copy(
            src_ref=row_b.at[me_ax],
            dst_ref=row_b.at[me_ax],
            send_sem=send_b.at[k],
            recv_sem=recv_b.at[me_ax],
            device_id=(lax.rem(me_ax + k, n_ax), me_az),
            device_id_type=MESH,
        )
        copy.start()
        sends.append(copy)
    for k in range(1, n_ax):
        source = lax.rem(me_ax + n_ax - k, n_ax)
        pltpu.make_async_remote_copy(
            src_ref=row_b.at[me_ax],
            dst_ref=row_b.at[source],
            send_sem=send_b.at[k],
            recv_sem=recv_b.at[source],
            device_id=(source, me_az),
            device_id_type=MESH,
        ).wait_recv()
    acc = row_b[0]
    for j in range(1, n_ax):
        acc = acc + row_b[j]
    o_ref[...] = acc
    for copy in sends:
        copy.wait_send()


def total_over_mesh(partial):
    n_ax, n_az = lax.axis_size("ax"), lax.axis_size("az")
    row = partial.reshape(1, -1)
    out = pl.pallas_call(
        functools.partial(_total_kernel, n_ax, n_az),
        out_shape=jax.ShapeDtypeStruct(row.shape, row.dtype),
        in_specs=[pl.BlockSpec(memory_space=pltpu.VMEM)],
        out_specs=pl.BlockSpec(memory_space=pltpu.VMEM),
        scratch_shapes=[
            pltpu.VMEM((n_az,) + row.shape, row.dtype),
            pltpu.VMEM((n_ax,) + row.shape, row.dtype),
            pltpu.VMEM(row.shape, row.dtype),
            pltpu.SemaphoreType.DMA((n_az,)),
            pltpu.SemaphoreType.DMA((n_az,)),
            pltpu.SemaphoreType.DMA((n_ax,)),
            pltpu.SemaphoreType.DMA((n_ax,)),
            pltpu.SemaphoreType.DMA((2,)),
        ],
        compiler_params=pltpu.CompilerParams(collective_id=0, has_side_effects=True),
    )(row)
    return out.reshape(partial.shape)


def shards(initial, adjoint_seed, porosity, cell_type, region):
    n_regions = lax.axis_size("ax") * lax.axis_size("az") // 4
    final, adjoint, sensitivity, partial = window(
        initial, adjoint_seed, porosity, cell_type, region, n_regions)
    totals = total_over_mesh(partial.reshape(-1))
    return (final, adjoint, sensitivity, totals)


def solution(mesh):
    return jax.shard_map(
        shards,
        mesh=mesh,
        in_specs=(
            P(None, "ax", "az", None),
            P(None, "ax", "az", None),
            P("ax", "az", None),
            P("ax", "az", None),
            P("ax", "az", None),
        ),
        out_specs=(P(None, "ax", "az", None), P(None, "ax", "az", None), P("ax", "az", None), P()),
        check_vma=False,
    )
```

```python
import functools

import numpy as np

import jax
import jax.numpy as jnp
from jax import lax
from jax.experimental import pallas as pl
from jax.experimental.pallas import tpu as pltpu
from jax.sharding import PartitionSpec as P

MESH = pl.DeviceIdType.MESH

VELOCITY = [
    (0, 0, 0),
    (1, 0, 0),
    (-1, 0, 0),
    (0, 1, 0),
    (0, -1, 0),
    (0, 0, 1),
    (0, 0, -1),
    (1, 1, 0),
    (-1, -1, 0),
    (1, -1, 0),
    (-1, 1, 0),
    (1, 0, 1),
    (-1, 0, -1),
    (1, 0, -1),
    (-1, 0, 1),
    (0, 1, 1),
    (0, -1, -1),
    (0, 1, -1),
    (0, -1, 1),
]
OPPOSITE = [0, 2, 1, 4, 3, 6, 5, 8, 7, 10, 9, 12, 11, 14, 13, 16, 15, 18, 17]
WEIGHTS = [1.0 / 3.0] + [1.0 / 18.0] * 6 + [1.0 / 36.0] * 12
INLET_SPEED = (0.05, 0.05, 0.0)
NQ = 19
TILE = 8


def _inflow_constants():
    w = np.array(WEIGHTS, np.float32)
    u = np.array(INLET_SPEED, np.float32)
    c = np.array(VELOCITY, np.float32)
    proj = (c * u[None, :]).sum(1, dtype=np.float32).astype(np.float32)
    usq = np.float32((u * u).sum(dtype=np.float32))
    one = np.float32(1.0)
    val = w * one * (one + np.float32(3.0) * proj + np.float32(4.5) * proj * proj - np.float32(1.5) * usq)
    return [float(v) for v in val.astype(np.float32)]


INFLOW = _inflow_constants()


def _combo(values, coeffs):
    acc = None
    for v, c in zip(values, coeffs):
        if c == 0:
            continue
        term = v if c == 1 else (-v if c == -1 else c * v)
        acc = term if acc is None else acc + term
    return acc


def _equilibrium(rho, u):
    usq = u[0] * u[0] + u[1] * u[1] + u[2] * u[2]
    out = []
    for q in range(NQ):
        p = _combo(u, VELOCITY[q])
        if p is None:
            inner = 1.0 - 1.5 * usq
        else:
            inner = 1.0 + 3.0 * p + 4.5 * p * p - 1.5 * usq
        out.append(WEIGHTS[q] * rho * inner)
    return out


def _collide(f, porous, types, regions):
    rho = f[0]
    for q in range(1, NQ):
        rho = rho + f[q]
    u = [_combo(f, [VELOCITY[q][k] for q in range(NQ)]) / rho for k in range(3)]
    feq = _equilibrium(rho, u)
    g = [f[q] - feq[q] for q in range(NQ)]
    moments = []
    for a, b in ((0, 0), (1, 1), (2, 2), (0, 1), (0, 2), (1, 2)):
        moments.append(_combo(g, [VELOCITY[q][a] * VELOCITY[q][b] for q in range(NQ)]))
    stress_sq = (
        moments[0] * moments[0]
        + moments[1] * moments[1]
        + moments[2] * moments[2]
        + 2.0 * (moments[3] * moments[3] + moments[4] * moments[4] + moments[5] * moments[5])
    )
    shear = 1.5 * jnp.sqrt(stress_sq + 0.0001) / rho
    viscous = 0.02 * (shear + 0.01) ** (0.7 - 1.0)
    relax = 0.5 + 3.0 * viscous
    design = jnp.where(regions > 0, 1.0, 0.0).astype(jnp.float32)
    damp = porous * design
    outflow = _equilibrium(jnp.ones_like(rho), u)
    inlet = types == 2
    outlet = types == 3
    out = []
    for q in range(NQ):
        relaxed = f[q] - g[q] / relax - damp * (feq[q] - WEIGHTS[q] * rho)
        out.append(jnp.where(inlet, INFLOW[q], jnp.where(outlet, outflow[q], relaxed)))
    return out


def _pieces(sign):
    out = []
    for q in range(NQ):
        oa, ot = sign * VELOCITY[q][0], sign * VELOCITY[q][1]
        if oa != 0:
            out.append((q, "a", oa, ot))
        if ot != 0:
            out.append((q, "t", oa, ot))
        if oa != 0 and ot != 0:
            out.append((q, "c", oa, ot))
    return out


FLAG_PIECES = [
    (0, "a", 1, 0),
    (0, "a", -1, 0),
    (0, "t", 0, 1),
    (0, "t", 0, -1),
    (0, "c", 1, 1),
    (0, "c", 1, -1),
    (0, "c", -1, 1),
    (0, "c", -1, -1),
]
NPIECE = 24


class Halo:
    def __init__(self, a_lo, a_hi, t_lo, t_hi):
        self.a_lo, self.a_hi, self.t_lo, self.t_hi = a_lo, a_hi, t_lo, t_hi


def _piece_refs(piece, field, halo, ca, ct):
    q, kind, oa, ot = piece
    a_face = ca - 1 if oa == -1 else 0
    t_face = ct - 1 if ot == -1 else 0
    if kind == "a":
        src = field.at[q, pl.ds(a_face, 1)]
        dst = (halo.a_lo if oa == -1 else halo.a_hi).at[q]
        move = (-oa, 0)
    elif kind == "t":
        src = field.at[q, :, pl.ds(t_face, 1)]
        dst = (halo.t_lo if ot == -1 else halo.t_hi).at[q, pl.ds(1, ca)]
        move = (0, -ot)
    else:
        src = field.at[q, pl.ds(a_face, 1), pl.ds(t_face, 1)]
        slot = 0 if oa == -1 else ca + 1
        dst = (halo.t_lo if ot == -1 else halo.t_hi).at[q, pl.ds(slot, 1)]
        move = (-oa, -ot)
    return src, dst, move


class Exchange:
    def __init__(self, pieces, field, halo, send_sem, recv_sem, pos, sizes, ca, ct):
        self.items = []
        me_ax, me_az = pos
        n_ax, n_az = sizes
        for i, piece in enumerate(pieces):
            src, dst, (da, dt) = _piece_refs(piece, field, halo, ca, ct)
            to_ax = me_ax + da
            from_ax = me_ax - da
            to_dev = (to_ax, lax.rem(me_az + dt + n_az, n_az))
            from_dev = (from_ax, lax.rem(me_az - dt + n_az, n_az))
            send = pltpu.make_async_remote_copy(
                src_ref=src, dst_ref=dst, send_sem=send_sem.at[i], recv_sem=recv_sem.at[i],
                device_id=to_dev, device_id_type=MESH)
            recv = pltpu.make_async_remote_copy(
                src_ref=src, dst_ref=dst, send_sem=send_sem.at[i], recv_sem=recv_sem.at[i],
                device_id=from_dev, device_id_type=MESH)
            send_ok = jnp.logical_and(to_ax >= 0, to_ax < n_ax) if da != 0 else None
            recv_ok = jnp.logical_and(from_ax >= 0, from_ax < n_ax) if da != 0 else None
            self.items.append((send, recv, send_ok, recv_ok))

    @staticmethod
    def _maybe(ok, fn):
        if ok is None:
            fn()
        else:
            pl.when(ok)(fn)

    def start(self):
        for send, _, ok, _ in self.items:
            self._maybe(ok, send.start)

    def wait_recv(self):
        for _, recv, _, ok in self.items:
            self._maybe(ok, recv.wait_recv)

    def wait_send(self):
        for send, _, ok, _ in self.items:
            self._maybe(ok, send.wait_send)


def _shift(own, halo, q, a, oa, ot, orr, lo_ok, hi_ok, ca, ct, nr, zero_r):
    ae = a + oa
    ok = None
    if ae < 0:
        slab = halo.a_lo[q, 0]
        ok = lo_ok
    elif ae >= ca:
        slab = halo.a_hi[q, 0]
        ok = hi_ok
    else:
        slab = own[q, ae]
    if ot != 0:
        rows = lax.broadcasted_iota(jnp.int32, (ct, nr), 0)
        if ot == -1:
            edge = halo.t_lo[q, ae + 1]
            slab = jnp.where(rows == 0, edge, pltpu.roll(slab, 1, 0))
        else:
            edge = halo.t_hi[q, ae + 1]
            slab = jnp.where(rows == ct - 1, edge, pltpu.roll(slab, ct - 1, 0))
    if orr != 0:
        lanes = lax.broadcasted_iota(jnp.int32, (ct, nr), 1)
        if orr == -1:
            slab = jnp.where(lanes == 0, zero_r, pltpu.roll(slab, 1, 1))
        else:
            slab = jnp.where(lanes == nr - 1, zero_r, pltpu.roll(slab, nr - 1, 1))
    if ok is not None:
        slab = jnp.where(ok, slab, zero_r)
    return slab


def _window_kernel(
    n_ax, n_az,
    init_hbm, seed_hbm, por_hbm, type_hbm, reg_hbm,
    final_ref, adj_ref, sens_ref, tot_ref,
    init_ref, seed_ref, por_ref, type_ref, reg_ref, load_sem,
    post0, state1, back1, post1, adj1, back0, sens1,
    pop_a_lo, pop_a_hi, pop_t_lo, pop_t_hi,
    ty_a_lo, ty_a_hi, ty_t_lo, ty_t_hi,
    send_sem, recv_sem, ty_send, ty_recv,
    part_ref, row_a, row_b, send_a, recv_a, send_b, recv_b, local,
):
    loads = [
        pltpu.make_async_copy(src, dst, load_sem.at[i])
        for i, (src, dst) in enumerate(
            ((type_hbm, type_ref), (seed_hbm, seed_ref), (init_hbm, init_ref),
             (por_hbm, por_ref), (reg_hbm, reg_ref)))
    ]
    for copy in loads:
        copy.start()
    _, ca, ct, nr = init_ref.shape
    me_ax, me_az = lax.axis_index("ax"), lax.axis_index("az")
    lo_ok = me_ax > 0
    hi_ok = me_ax < n_ax - 1
    pos, sizes = (me_ax, me_az), (n_ax, n_az)

    barrier = pltpu.get_barrier_semaphore()
    up_az, dn_az = lax.rem(me_az + 1, n_az), lax.rem(me_az + n_az - 1, n_az)
    for k in range(1, n_az):
        pl.semaphore_signal(barrier, 1, device_id=(me_ax, lax.rem(me_az + k, n_az)), device_id_type=MESH)
    for k in range(1, n_ax):
        pl.semaphore_signal(barrier, 1, device_id=(lax.rem(me_ax + k, n_ax), me_az), device_id_type=MESH)
    for ok, other in ((lo_ok, me_ax - 1), (hi_ok, me_ax + 1)):
        @pl.when(ok)
        def _():
            for dz in (up_az, dn_az):
                pl.semaphore_signal(barrier, 1, device_id=(other, dz), device_id_type=MESH)
    count = (n_az - 1) + (n_ax - 1) + 2 * (lo_ok.astype(jnp.int32) + hi_ok.astype(jnp.int32))
    pl.semaphore_wait(barrier, count)
    for copy in loads:
        copy.wait()

    def halo(k):
        return Halo(pop_a_lo.at[k], pop_a_hi.at[k], pop_t_lo.at[k], pop_t_hi.at[k])

    ty_halo = Halo(ty_a_lo, ty_a_hi, ty_t_lo, ty_t_hi)
    ex_types = Exchange(FLAG_PIECES, type_ref, ty_halo, ty_send, ty_recv, pos, sizes, ca, ct)
    ex_seed = Exchange(_pieces(1), seed_ref, halo(0), send_sem.at[0], recv_sem.at[0], pos, sizes, ca, ct)
    ex_types.start()
    ex_seed.start()

    steps = ca * (ct // TILE)

    def tile_at(i):
        a = i // (ct // TILE)
        t0 = pl.multiple_of((i % (ct // TILE)) * TILE, TILE)
        return a, pl.ds(t0, TILE)

    def load(ref, a, ts):
        return [ref[q, a, ts, :] for q in range(NQ)]

    def store(ref, a, ts, vals):
        for q in range(NQ):
            ref[q, a, ts, :] = vals[q]

    def collide_loop(src, dst):
        def body(i, carry):
            a, ts = tile_at(i)
            out = _collide(load(src, a, ts), por_ref[a, ts, :], type_ref[0, a, ts, :], reg_ref[a, ts, :])
            store(dst, a, ts, out)
            return carry
        lax.fori_loop(0, steps, body, 0)

    def vjp_loop(at, upstream, primal_dst, grad_dst, sens_dst, sens_add):
        def body(i, carry):
            a, ts = tile_at(i)
            types = type_ref[0, a, ts, :]
            regions = reg_ref[a, ts, :]
            out, pullback = jax.vjp(
                lambda f, p: _collide(f, p, types, regions), load(at, a, ts), por_ref[a, ts, :])
            if primal_dst is not None:
                store(primal_dst, a, ts, out)
            d_f, d_p = pullback(load(upstream, a, ts))
            store(grad_dst, a, ts, d_f)
            if sens_add is not None:
                d_p = d_p + sens_add[a, ts, :]
            sens_dst[a, ts, :] = d_p
            return carry
        lax.fori_loop(0, steps, body, 0)

    zero = jnp.zeros((ct, nr), jnp.float32)

    def flag_shift(a, oa, ot, orr):
        if oa == 0 and ot == 0 and orr == 0:
            own = type_ref[0, a]
            return jnp.where(own != 1, 1.0, 0.0).astype(jnp.float32)
        ty = _shift(type_ref, ty_halo, 0, a, oa, ot, orr, lo_ok, hi_ok, ca, ct, nr, jnp.ones((ct, nr), jnp.int32))
        return jnp.where(ty != 1, 1.0, 0.0).astype(jnp.float32)

    def stream(post, hal, dst):
        for a in range(ca):
            for q in range(NQ):
                c = VELOCITY[q]
                moved = _shift(post, hal, q, a, -c[0], -c[1], -c[2], lo_ok, hi_ok, ca, ct, nr, zero)
                ok = flag_shift(a, -c[0], -c[1], -c[2]) > 0
                dst[q, a] = jnp.where(ok, moved, post[OPPOSITE[q], a])

    def stream_adjoint(adj, hal, dst):
        for a in range(ca):
            centre = flag_shift(a, 0, 0, 0)
            for q in range(NQ):
                c = VELOCITY[q]
                ahead = _shift(adj, hal, q, a, c[0], c[1], c[2], lo_ok, hi_ok, ca, ct, nr, zero)
                blocked = 1.0 - flag_shift(a, c[0], c[1], c[2])
                dst[q, a] = centre * ahead + blocked * adj[OPPOSITE[q], a]

    collide_loop(init_ref, post0)
    ex_post0 = Exchange(_pieces(-1), post0, halo(1), send_sem.at[1], recv_sem.at[1], pos, sizes, ca, ct)
    ex_post0.start()
    ex_types.wait_recv()
    ex_post0.wait_recv()
    stream(post0, halo(1), state1)
    ex_seed.wait_recv()
    stream_adjoint(seed_ref, halo(0), back1)
    vjp_loop(state1, back1, post1, adj1, sens1, None)
    ex_post1 = Exchange(_pieces(-1), post1, halo(2), send_sem.at[2], recv_sem.at[2], pos, sizes, ca, ct)
    ex_adj1 = Exchange(_pieces(1), adj1, halo(3), send_sem.at[3], recv_sem.at[3], pos, sizes, ca, ct)
    ex_adj1.start()
    ex_post1.start()
    ex_adj1.wait_recv()
    stream_adjoint(adj1, halo(3), back0)
    vjp_loop(init_ref, back0, None, adj_ref, sens_ref, sens1)
    ex_post1.wait_recv()
    stream(post1, halo(2), final_ref)

    total = jnp.zeros((1, 1), jnp.float32)
    rid = jnp.zeros((1, 1), jnp.int32)
    for a in range(ca):
        reg = reg_ref[a]
        total = total + jnp.sum(jnp.where(reg > 0, sens_ref[a], 0.0), keepdims=True)
        rid = jnp.maximum(rid, jnp.max(reg, keepdims=True))
    labels = lax.broadcasted_iota(jnp.int32, part_ref.shape, 1) + 1
    part_ref[...] = jnp.where(labels == rid, total, 0.0)
    sends = _reduce_totals(part_ref, tot_ref, row_a, row_b, send_a, recv_a, send_b, recv_b, local, pos, sizes)

    for ex in (ex_types, ex_seed, ex_post0, ex_post1, ex_adj1):
        ex.wait_send()
    for copy in sends:
        copy.wait_send()


def window(initial, adjoint_seed, porosity, cell_type, region, n_regions):
    n_ax, n_az = lax.axis_size("ax"), lax.axis_size("az")
    nq, ca, ct, nr = initial.shape
    pop = jax.ShapeDtypeStruct(initial.shape, jnp.float32)
    cells = jax.ShapeDtypeStruct(porosity.shape, jnp.float32)
    vmem = pltpu.VMEM
    f32, i32 = jnp.float32, jnp.int32
    scratch = (
        [vmem(initial.shape, f32), vmem(initial.shape, f32), vmem(porosity.shape, f32),
         vmem((1,) + cell_type.shape, i32), vmem(region.shape, i32), pltpu.SemaphoreType.DMA((5,))]
        + [vmem((nq, ca, ct, nr), f32) for _ in range(6)]
        + [vmem((ca, ct, nr), f32)]
        + [vmem((4, nq, 1, ct, nr), f32), vmem((4, nq, 1, ct, nr), f32),
           vmem((4, nq, ca + 2, 1, nr), f32), vmem((4, nq, ca + 2, 1, nr), f32)]
        + [vmem((1, 1, ct, nr), i32), vmem((1, 1, ct, nr), i32),
           vmem((1, ca + 2, 1, nr), i32), vmem((1, ca + 2, 1, nr), i32)]
        + [pltpu.SemaphoreType.DMA((4, NPIECE)), pltpu.SemaphoreType.DMA((4, NPIECE)),
           pltpu.SemaphoreType.DMA((len(FLAG_PIECES),)), pltpu.SemaphoreType.DMA((len(FLAG_PIECES),))]
        + [vmem((1, n_regions), f32), vmem((n_az, 1, n_regions), f32), vmem((n_ax, 1, n_regions), f32),
           pltpu.SemaphoreType.DMA((n_az,)), pltpu.SemaphoreType.DMA((n_az,)),
           pltpu.SemaphoreType.DMA((n_ax,)), pltpu.SemaphoreType.DMA((n_ax,)),
           pltpu.SemaphoreType.DMA((2,))]
    )
    any_spec = pl.BlockSpec(memory_space=vmem)
    final, adj, sens, tot = pl.pallas_call(
        functools.partial(_window_kernel, n_ax, n_az),
        out_shape=(pop, pop, cells, jax.ShapeDtypeStruct((1, n_regions), f32)),
        in_specs=[pl.BlockSpec(memory_space=pl.ANY)] * 5,
        out_specs=(any_spec,) * 4,
        scratch_shapes=scratch,
        compiler_params=pltpu.CompilerParams(collective_id=1, has_side_effects=True,
                                             vmem_limit_bytes=48 * 1024 * 1024),
    )(initial, adjoint_seed, porosity, cell_type.reshape((1,) + cell_type.shape), region)
    return final, adj, sens, tot


def _reduce_totals(x_ref, o_ref, row_a, row_b, send_a, recv_a, send_b, recv_b, local, pos, sizes):
    me_ax, me_az = pos
    n_ax, n_az = sizes
    own = pltpu.make_async_copy(x_ref, row_a.at[me_az], local.at[0])
    own.start()
    sends = []
    for k in range(1, n_az):
        copy = pltpu.make_async_remote_copy(
            src_ref=x_ref,
            dst_ref=row_a.at[me_az],
            send_sem=send_a.at[k],
            recv_sem=recv_a.at[me_az],
            device_id=(me_ax, lax.rem(me_az + k, n_az)),
            device_id_type=MESH,
        )
        copy.start()
        sends.append(copy)
    own.wait()
    for k in range(1, n_az):
        source = lax.rem(me_az + n_az - k, n_az)
        pltpu.make_async_remote_copy(
            src_ref=x_ref,
            dst_ref=row_a.at[source],
            send_sem=send_a.at[k],
            recv_sem=recv_a.at[source],
            device_id=(me_ax, source),
            device_id_type=MESH,
        ).wait_recv()
    acc = row_a[0]
    for j in range(1, n_az):
        acc = acc + row_a[j]
    for copy in sends:
        copy.wait_send()
    sends = []
    x_ref[...] = acc

    own = pltpu.make_async_copy(x_ref, row_b.at[me_ax], local.at[1])
    own.start()
    own.wait()
    for k in range(1, n_ax):
        copy = pltpu.make_async_remote_copy(
            src_ref=row_b.at[me_ax],
            dst_ref=row_b.at[me_ax],
            send_sem=send_b.at[k],
            recv_sem=recv_b.at[me_ax],
            device_id=(lax.rem(me_ax + k, n_ax), me_az),
            device_id_type=MESH,
        )
        copy.start()
        sends.append(copy)
    for k in range(1, n_ax):
        source = lax.rem(me_ax + n_ax - k, n_ax)
        pltpu.make_async_remote_copy(
            src_ref=row_b.at[me_ax],
            dst_ref=row_b.at[source],
            send_sem=send_b.at[k],
            recv_sem=recv_b.at[source],
            device_id=(source, me_az),
            device_id_type=MESH,
        ).wait_recv()
    acc = row_b[0]
    for j in range(1, n_ax):
        acc = acc + row_b[j]
    o_ref[...] = acc
    return sends


def shards(initial, adjoint_seed, porosity, cell_type, region):
    n_regions = lax.axis_size("ax") * lax.axis_size("az") // 4
    final, adjoint, sensitivity, totals = window(
        initial, adjoint_seed, porosity, cell_type, region, n_regions)
    totals = totals.reshape(-1)
    return (final, adjoint, sensitivity, totals)


def solution(mesh):
    return jax.shard_map(
        shards,
        mesh=mesh,
        in_specs=(
            P(None, "ax", "az", None),
            P(None, "ax", "az", None),
            P("ax", "az", None),
            P("ax", "az", None),
            P("ax", "az", None),
        ),
        out_specs=(P(None, "ax", "az", None), P(None, "ax", "az", None), P("ax", "az", None), P()),
        check_vma=False,
    )
```

```python
import functools

import numpy as np

import jax
import jax.numpy as jnp
from jax import lax
from jax.experimental import pallas as pl
from jax.experimental.pallas import tpu as pltpu
from jax.sharding import PartitionSpec as P

MESH = pl.DeviceIdType.MESH

VELOCITY = [
    (0, 0, 0),
    (1, 0, 0),
    (-1, 0, 0),
    (0, 1, 0),
    (0, -1, 0),
    (0, 0, 1),
    (0, 0, -1),
    (1, 1, 0),
    (-1, -1, 0),
    (1, -1, 0),
    (-1, 1, 0),
    (1, 0, 1),
    (-1, 0, -1),
    (1, 0, -1),
    (-1, 0, 1),
    (0, 1, 1),
    (0, -1, -1),
    (0, 1, -1),
    (0, -1, 1),
]
OPPOSITE = [0, 2, 1, 4, 3, 6, 5, 8, 7, 10, 9, 12, 11, 14, 13, 16, 15, 18, 17]
WEIGHTS = [1.0 / 3.0] + [1.0 / 18.0] * 6 + [1.0 / 36.0] * 12
INLET_SPEED = (0.05, 0.05, 0.0)
NQ = 19
TILE = 8


def _inflow_constants():
    w = np.array(WEIGHTS, np.float32)
    u = np.array(INLET_SPEED, np.float32)
    c = np.array(VELOCITY, np.float32)
    proj = (c * u[None, :]).sum(1, dtype=np.float32).astype(np.float32)
    usq = np.float32((u * u).sum(dtype=np.float32))
    one = np.float32(1.0)
    val = w * one * (one + np.float32(3.0) * proj + np.float32(4.5) * proj * proj - np.float32(1.5) * usq)
    return [float(v) for v in val.astype(np.float32)]


INFLOW = _inflow_constants()


def _combo(values, coeffs):
    acc = None
    for v, c in zip(values, coeffs):
        if c == 0:
            continue
        term = v if c == 1 else (-v if c == -1 else c * v)
        acc = term if acc is None else acc + term
    return acc


def _equilibrium(rho, u):
    usq = u[0] * u[0] + u[1] * u[1] + u[2] * u[2]
    out = []
    for q in range(NQ):
        p = _combo(u, VELOCITY[q])
        if p is None:
            inner = 1.0 - 1.5 * usq
        else:
            inner = 1.0 + 3.0 * p + 4.5 * p * p - 1.5 * usq
        out.append(WEIGHTS[q] * rho * inner)
    return out


def _collide(f, porous, types, regions):
    rho = f[0]
    for q in range(1, NQ):
        rho = rho + f[q]
    u = [_combo(f, [VELOCITY[q][k] for q in range(NQ)]) / rho for k in range(3)]
    feq = _equilibrium(rho, u)
    g = [f[q] - feq[q] for q in range(NQ)]
    moments = []
    for a, b in ((0, 0), (1, 1), (2, 2), (0, 1), (0, 2), (1, 2)):
        moments.append(_combo(g, [VELOCITY[q][a] * VELOCITY[q][b] for q in range(NQ)]))
    stress_sq = (
        moments[0] * moments[0]
        + moments[1] * moments[1]
        + moments[2] * moments[2]
        + 2.0 * (moments[3] * moments[3] + moments[4] * moments[4] + moments[5] * moments[5])
    )
    shear = 1.5 * jnp.sqrt(stress_sq + 0.0001) / rho
    viscous = 0.02 * (shear + 0.01) ** (0.7 - 1.0)
    relax = 0.5 + 3.0 * viscous
    design = jnp.where(regions > 0, 1.0, 0.0).astype(jnp.float32)
    damp = porous * design
    outflow = _equilibrium(jnp.ones_like(rho), u)
    inlet = types == 2
    outlet = types == 3
    out = []
    for q in range(NQ):
        relaxed = f[q] - g[q] / relax - damp * (feq[q] - WEIGHTS[q] * rho)
        out.append(jnp.where(inlet, INFLOW[q], jnp.where(outlet, outflow[q], relaxed)))
    return out


def _pieces(sign):
    out = []
    for q in range(NQ):
        oa, ot = sign * VELOCITY[q][0], sign * VELOCITY[q][1]
        if oa != 0:
            out.append((q, "a", oa, ot))
        if ot != 0:
            out.append((q, "t", oa, ot))
        if oa != 0 and ot != 0:
            out.append((q, "c", oa, ot))
    return out


FLAG_PIECES = [
    (0, "a", 1, 0),
    (0, "a", -1, 0),
    (0, "t", 0, 1),
    (0, "t", 0, -1),
    (0, "c", 1, 1),
    (0, "c", 1, -1),
    (0, "c", -1, 1),
    (0, "c", -1, -1),
]
NPIECE = 24


class Halo:
    def __init__(self, a_lo, a_hi, t_lo, t_hi):
        self.a_lo, self.a_hi, self.t_lo, self.t_hi = a_lo, a_hi, t_lo, t_hi


def _piece_refs(piece, field, halo, ca, ct):
    q, kind, oa, ot = piece
    a_face = ca - 1 if oa == -1 else 0
    t_face = ct - 1 if ot == -1 else 0
    if kind == "a":
        src = field.at[q, pl.ds(a_face, 1)]
        dst = (halo.a_lo if oa == -1 else halo.a_hi).at[q]
        move = (-oa, 0)
    elif kind == "t":
        src = field.at[q, :, pl.ds(t_face, 1)]
        dst = (halo.t_lo if ot == -1 else halo.t_hi).at[q, pl.ds(1, ca)]
        move = (0, -ot)
    else:
        src = field.at[q, pl.ds(a_face, 1), pl.ds(t_face, 1)]
        slot = 0 if oa == -1 else ca + 1
        dst = (halo.t_lo if ot == -1 else halo.t_hi).at[q, pl.ds(slot, 1)]
        move = (-oa, -ot)
    return src, dst, move


class Exchange:
    def __init__(self, pieces, field, halo, send_sem, recv_sem, pos, sizes, ca, ct):
        self.items = []
        me_ax, me_az = pos
        n_ax, n_az = sizes
        for i, piece in enumerate(pieces):
            src, dst, (da, dt) = _piece_refs(piece, field, halo, ca, ct)
            to_ax = me_ax + da
            from_ax = me_ax - da
            to_dev = (to_ax, lax.rem(me_az + dt + n_az, n_az))
            from_dev = (from_ax, lax.rem(me_az - dt + n_az, n_az))
            send = pltpu.make_async_remote_copy(
                src_ref=src, dst_ref=dst, send_sem=send_sem.at[i], recv_sem=recv_sem.at[i],
                device_id=to_dev, device_id_type=MESH)
            recv = pltpu.make_async_remote_copy(
                src_ref=src, dst_ref=dst, send_sem=send_sem.at[i], recv_sem=recv_sem.at[i],
                device_id=from_dev, device_id_type=MESH)
            send_ok = jnp.logical_and(to_ax >= 0, to_ax < n_ax) if da != 0 else None
            recv_ok = jnp.logical_and(from_ax >= 0, from_ax < n_ax) if da != 0 else None
            self.items.append((send, recv, send_ok, recv_ok))

    @staticmethod
    def _maybe(ok, fn):
        if ok is None:
            fn()
        else:
            pl.when(ok)(fn)

    def start(self):
        for send, _, ok, _ in self.items:
            self._maybe(ok, send.start)

    def wait_recv(self):
        for _, recv, _, ok in self.items:
            self._maybe(ok, recv.wait_recv)

    def wait_send(self):
        for send, _, ok, _ in self.items:
            self._maybe(ok, send.wait_send)


def _shift(own, halo, q, a, oa, ot, orr, lo_ok, hi_ok, ca, ct, nr, zero_r):
    ae = a + oa
    ok = None
    if ae < 0:
        slab = halo.a_lo[q, 0]
        ok = lo_ok
    elif ae >= ca:
        slab = halo.a_hi[q, 0]
        ok = hi_ok
    else:
        slab = own[q, ae]
    if ot != 0:
        rows = lax.broadcasted_iota(jnp.int32, (ct, nr), 0)
        if ot == -1:
            edge = halo.t_lo[q, ae + 1]
            slab = jnp.where(rows == 0, edge, pltpu.roll(slab, 1, 0))
        else:
            edge = halo.t_hi[q, ae + 1]
            slab = jnp.where(rows == ct - 1, edge, pltpu.roll(slab, ct - 1, 0))
    if orr != 0:
        lanes = lax.broadcasted_iota(jnp.int32, (ct, nr), 1)
        if orr == -1:
            slab = jnp.where(lanes == 0, zero_r, pltpu.roll(slab, 1, 1))
        else:
            slab = jnp.where(lanes == nr - 1, zero_r, pltpu.roll(slab, nr - 1, 1))
    if ok is not None:
        slab = jnp.where(ok, slab, zero_r)
    return slab


def _window_kernel(
    n_ax, n_az,
    init_hbm, seed_hbm, por_hbm, type_hbm, reg_hbm,
    final_ref, adj_ref, sens_ref, tot_ref,
    init_ref, seed_ref, por_ref, type_ref, reg_ref, load_sem,
    post0, state1, back1, post1, adj1, back0, sens1,
    pop_a_lo, pop_a_hi, pop_t_lo, pop_t_hi,
    ty_a_lo, ty_a_hi, ty_t_lo, ty_t_hi,
    send_sem, recv_sem, ty_send, ty_recv,
    part_ref, row_a, row_b, send_a, recv_a, send_b, recv_b, local,
):
    loads = [
        pltpu.make_async_copy(src, dst, load_sem.at[i])
        for i, (src, dst) in enumerate(
            ((type_hbm, type_ref), (seed_hbm, seed_ref), (init_hbm, init_ref),
             (por_hbm, por_ref), (reg_hbm, reg_ref)))
    ]
    for copy in loads:
        copy.start()
    _, ca, ct, nr = init_ref.shape
    me_ax, me_az = lax.axis_index("ax"), lax.axis_index("az")
    lo_ok = me_ax > 0
    hi_ok = me_ax < n_ax - 1
    pos, sizes = (me_ax, me_az), (n_ax, n_az)

    barrier = pltpu.get_barrier_semaphore()
    up_az, dn_az = lax.rem(me_az + 1, n_az), lax.rem(me_az + n_az - 1, n_az)
    for k in range(1, n_az):
        pl.semaphore_signal(barrier, 1, device_id=(me_ax, lax.rem(me_az + k, n_az)), device_id_type=MESH)
    for k in range(1, n_ax):
        pl.semaphore_signal(barrier, 1, device_id=(lax.rem(me_ax + k, n_ax), me_az), device_id_type=MESH)
    for ok, other in ((lo_ok, me_ax - 1), (hi_ok, me_ax + 1)):
        @pl.when(ok)
        def _():
            for dz in (up_az, dn_az):
                pl.semaphore_signal(barrier, 1, device_id=(other, dz), device_id_type=MESH)
    count = (n_az - 1) + (n_ax - 1) + 2 * (lo_ok.astype(jnp.int32) + hi_ok.astype(jnp.int32))
    pl.semaphore_wait(barrier, count)
    for copy in loads:
        copy.wait()

    def halo(k):
        return Halo(pop_a_lo.at[k], pop_a_hi.at[k], pop_t_lo.at[k], pop_t_hi.at[k])

    ty_halo = Halo(ty_a_lo, ty_a_hi, ty_t_lo, ty_t_hi)
    ex_types = Exchange(FLAG_PIECES, type_ref, ty_halo, ty_send, ty_recv, pos, sizes, ca, ct)
    ex_seed = Exchange(_pieces(1), seed_ref, halo(0), send_sem.at[0], recv_sem.at[0], pos, sizes, ca, ct)
    ex_types.start()
    ex_seed.start()

    steps = ca * (ct // TILE)

    def tile_at(i):
        a = i // (ct // TILE)
        t0 = pl.multiple_of((i % (ct // TILE)) * TILE, TILE)
        return a, pl.ds(t0, TILE)

    def load(ref, a, ts):
        return [ref[q, a, ts, :] for q in range(NQ)]

    def store(ref, a, ts, vals):
        for q in range(NQ):
            ref[q, a, ts, :] = vals[q]

    def collide_loop(src, dst):
        def body(i, carry):
            a, ts = tile_at(i)
            out = _collide(load(src, a, ts), por_ref[a, ts, :], type_ref[0, a, ts, :], reg_ref[a, ts, :])
            store(dst, a, ts, out)
            return carry
        lax.fori_loop(0, steps, body, 0)

    def vjp_loop(at, upstream, primal_dst, grad_dst, sens_dst, sens_add):
        def body(i, carry):
            a, ts = tile_at(i)
            types = type_ref[0, a, ts, :]
            regions = reg_ref[a, ts, :]
            out, pullback = jax.vjp(
                lambda f, p: _collide(f, p, types, regions), load(at, a, ts), por_ref[a, ts, :])
            if primal_dst is not None:
                store(primal_dst, a, ts, out)
            d_f, d_p = pullback(load(upstream, a, ts))
            store(grad_dst, a, ts, d_f)
            if sens_add is not None:
                d_p = d_p + sens_add[a, ts, :]
            sens_dst[a, ts, :] = d_p
            return carry
        lax.fori_loop(0, steps, body, 0)

    zero = jnp.zeros((ct, nr), jnp.float32)

    def flag_shift(a, oa, ot, orr):
        if oa == 0 and ot == 0 and orr == 0:
            own = type_ref[0, a]
            return jnp.where(own != 1, 1.0, 0.0).astype(jnp.float32)
        ty = _shift(type_ref, ty_halo, 0, a, oa, ot, orr, lo_ok, hi_ok, ca, ct, nr, jnp.ones((ct, nr), jnp.int32))
        return jnp.where(ty != 1, 1.0, 0.0).astype(jnp.float32)

    def stream(post, hal, dst):
        for a in range(ca):
            for q in range(NQ):
                c = VELOCITY[q]
                moved = _shift(post, hal, q, a, -c[0], -c[1], -c[2], lo_ok, hi_ok, ca, ct, nr, zero)
                ok = flag_shift(a, -c[0], -c[1], -c[2]) > 0
                dst[q, a] = jnp.where(ok, moved, post[OPPOSITE[q], a])

    def stream_adjoint(adj, hal, dst):
        for a in range(ca):
            centre = flag_shift(a, 0, 0, 0)
            for q in range(NQ):
                c = VELOCITY[q]
                ahead = _shift(adj, hal, q, a, c[0], c[1], c[2], lo_ok, hi_ok, ca, ct, nr, zero)
                blocked = 1.0 - flag_shift(a, c[0], c[1], c[2])
                dst[q, a] = centre * ahead + blocked * adj[OPPOSITE[q], a]

    collide_loop(init_ref, post0)
    ex_post0 = Exchange(_pieces(-1), post0, halo(1), send_sem.at[1], recv_sem.at[1], pos, sizes, ca, ct)
    ex_post0.start()
    ex_types.wait_recv()
    ex_post0.wait_recv()
    stream(post0, halo(1), state1)
    ex_seed.wait_recv()
    stream_adjoint(seed_ref, halo(0), back1)
    vjp_loop(state1, back1, post1, adj1, sens1, None)
    ex_post1 = Exchange(_pieces(-1), post1, halo(2), send_sem.at[2], recv_sem.at[2], pos, sizes, ca, ct)
    ex_adj1 = Exchange(_pieces(1), adj1, halo(3), send_sem.at[3], recv_sem.at[3], pos, sizes, ca, ct)
    ex_adj1.start()
    ex_post1.start()
    ex_adj1.wait_recv()
    stream_adjoint(adj1, halo(3), back0)
    vjp_loop(init_ref, back0, None, adj_ref, sens_ref, sens1)

    total = jnp.zeros((1, 1), jnp.float32)
    rid = jnp.zeros((1, 1), jnp.int32)
    for a in range(ca):
        reg = reg_ref[a]
        total = total + jnp.sum(jnp.where(reg > 0, sens_ref[a], 0.0), keepdims=True)
        rid = jnp.maximum(rid, jnp.max(reg, keepdims=True))
    labels = lax.broadcasted_iota(jnp.int32, part_ref.shape, 1) + 1
    part_ref[...] = jnp.where(labels == rid, total, 0.0)
    first = _TotalsStage(part_ref, row_a, send_a, recv_a, local.at[0], me_az, n_az,
                         lambda j: (me_ax, j))
    first.start()

    ex_post1.wait_recv()
    stream(post1, halo(2), final_ref)

    first.finish(part_ref)
    own = pltpu.make_async_copy(part_ref, row_b.at[me_ax], local.at[1])
    own.start()
    own.wait()
    second = _TotalsStage(row_b.at[me_ax], row_b, send_b, recv_b, None, me_ax, n_ax,
                          lambda j: (j, me_az))
    second.start()
    second.finish(tot_ref)

    for ex in (ex_types, ex_seed, ex_post0, ex_post1, ex_adj1):
        ex.wait_send()


class _TotalsStage:
    def __init__(self, src, rows, send, recv, own_sem, me, n, device):
        self.src, self.rows, self.own_sem, self.me, self.n = src, rows, own_sem, me, n
        self.sends, self.recvs = [], []
        for k in range(1, n):
            to, frm = lax.rem(me + k, n), lax.rem(me + n - k, n)
            self.sends.append(pltpu.make_async_remote_copy(
                src_ref=src, dst_ref=rows.at[me], send_sem=send.at[k], recv_sem=recv.at[me],
                device_id=device(to), device_id_type=MESH))
            self.recvs.append(pltpu.make_async_remote_copy(
                src_ref=src, dst_ref=rows.at[frm], send_sem=send.at[k], recv_sem=recv.at[frm],
                device_id=device(frm), device_id_type=MESH))

    def start(self):
        self.own = None
        if self.own_sem is not None:
            self.own = pltpu.make_async_copy(self.src, self.rows.at[self.me], self.own_sem)
            self.own.start()
        for copy in self.sends:
            copy.start()

    def finish(self, out):
        if self.own is not None:
            self.own.wait()
        for copy in self.recvs:
            copy.wait_recv()
        acc = self.rows[0]
        for j in range(1, self.n):
            acc = acc + self.rows[j]
        for copy in self.sends:
            copy.wait_send()
        out[...] = acc


def window(initial, adjoint_seed, porosity, cell_type, region, n_regions):
    n_ax, n_az = lax.axis_size("ax"), lax.axis_size("az")
    nq, ca, ct, nr = initial.shape
    pop = jax.ShapeDtypeStruct(initial.shape, jnp.float32)
    cells = jax.ShapeDtypeStruct(porosity.shape, jnp.float32)
    vmem = pltpu.VMEM
    f32, i32 = jnp.float32, jnp.int32
    scratch = (
        [vmem(initial.shape, f32), vmem(initial.shape, f32), vmem(porosity.shape, f32),
         vmem((1,) + cell_type.shape, i32), vmem(region.shape, i32), pltpu.SemaphoreType.DMA((5,))]

        + [vmem((nq, ca, ct, nr), f32) for _ in range(6)]
        + [vmem((ca, ct, nr), f32)]
        + [vmem((4, nq, 1, ct, nr), f32), vmem((4, nq, 1, ct, nr), f32),
           vmem((4, nq, ca + 2, 1, nr), f32), vmem((4, nq, ca + 2, 1, nr), f32)]
        + [vmem((1, 1, ct, nr), i32), vmem((1, 1, ct, nr), i32),
           vmem((1, ca + 2, 1, nr), i32), vmem((1, ca + 2, 1, nr), i32)]
        + [pltpu.SemaphoreType.DMA((4, NPIECE)), pltpu.SemaphoreType.DMA((4, NPIECE)),
           pltpu.SemaphoreType.DMA((len(FLAG_PIECES),)), pltpu.SemaphoreType.DMA((len(FLAG_PIECES),))]
        + [vmem((1, n_regions), f32), vmem((n_az, 1, n_regions), f32), vmem((n_ax, 1, n_regions), f32),
           pltpu.SemaphoreType.DMA((n_az,)), pltpu.SemaphoreType.DMA((n_az,)),
           pltpu.SemaphoreType.DMA((n_ax,)), pltpu.SemaphoreType.DMA((n_ax,)),
           pltpu.SemaphoreType.DMA((2,))]
    )
    final, adj, sens, tot = pl.pallas_call(
        functools.partial(_window_kernel, n_ax, n_az),
        out_shape=(pop, pop, cells, jax.ShapeDtypeStruct((1, n_regions), f32)),
        in_specs=[pl.BlockSpec(memory_space=pltpu.HBM)] * 5,
        out_specs=(pl.BlockSpec(memory_space=vmem),) * 4,
        scratch_shapes=scratch,
        compiler_params=pltpu.CompilerParams(collective_id=1, has_side_effects=True,
                                             vmem_limit_bytes=67043328),
    )(initial, adjoint_seed, porosity, cell_type.reshape((1,) + cell_type.shape), region)
    return final, adj, sens, tot


def shards(initial, adjoint_seed, porosity, cell_type, region):
    n_regions = lax.axis_size("ax") * lax.axis_size("az") // 4
    final, adjoint, sensitivity, totals = window(
        initial, adjoint_seed, porosity, cell_type, region, n_regions)
    totals = totals.reshape(-1)
    return (final, adjoint, sensitivity, totals)


def solution(mesh):
    return jax.shard_map(
        shards,
        mesh=mesh,
        in_specs=(
            P(None, "ax", "az", None),
            P(None, "ax", "az", None),
            P("ax", "az", None),
            P("ax", "az", None),
            P("ax", "az", None),
        ),
        out_specs=(P(None, "ax", "az", None), P(None, "ax", "az", None), P("ax", "az", None), P()),
        check_vma=False,
    )
```

```python
import functools

import numpy as np

import jax
import jax.numpy as jnp
from jax import lax
from jax.experimental import pallas as pl
from jax.experimental.pallas import tpu as pltpu
from jax.sharding import PartitionSpec as P

MESH = pl.DeviceIdType.MESH

VELOCITY = [
    (0, 0, 0),
    (1, 0, 0),
    (-1, 0, 0),
    (0, 1, 0),
    (0, -1, 0),
    (0, 0, 1),
    (0, 0, -1),
    (1, 1, 0),
    (-1, -1, 0),
    (1, -1, 0),
    (-1, 1, 0),
    (1, 0, 1),
    (-1, 0, -1),
    (1, 0, -1),
    (-1, 0, 1),
    (0, 1, 1),
    (0, -1, -1),
    (0, 1, -1),
    (0, -1, 1),
]
OPPOSITE = [0, 2, 1, 4, 3, 6, 5, 8, 7, 10, 9, 12, 11, 14, 13, 16, 15, 18, 17]
WEIGHTS = [1.0 / 3.0] + [1.0 / 18.0] * 6 + [1.0 / 36.0] * 12
INLET_SPEED = (0.05, 0.05, 0.0)
NQ = 19
TILE = 8


def _inflow_constants():
    w = np.array(WEIGHTS, np.float32)
    u = np.array(INLET_SPEED, np.float32)
    c = np.array(VELOCITY, np.float32)
    proj = (c * u[None, :]).sum(1, dtype=np.float32).astype(np.float32)
    usq = np.float32((u * u).sum(dtype=np.float32))
    one = np.float32(1.0)
    val = w * one * (one + np.float32(3.0) * proj + np.float32(4.5) * proj * proj - np.float32(1.5) * usq)
    return [float(v) for v in val.astype(np.float32)]


INFLOW = _inflow_constants()


def _combo(values, coeffs):
    acc = None
    for v, c in zip(values, coeffs):
        if c == 0:
            continue
        term = v if c == 1 else (-v if c == -1 else c * v)
        acc = term if acc is None else acc + term
    return acc


def _equilibrium(rho, u):
    usq = u[0] * u[0] + u[1] * u[1] + u[2] * u[2]
    out = []
    for q in range(NQ):
        p = _combo(u, VELOCITY[q])
        if p is None:
            inner = 1.0 - 1.5 * usq
        else:
            inner = 1.0 + 3.0 * p + 4.5 * p * p - 1.5 * usq
        out.append(WEIGHTS[q] * rho * inner)
    return out


def _collide(f, porous, types, regions, with_grad=False):
    rho = f[0]
    for q in range(1, NQ):
        rho = rho + f[q]
    u = [_combo(f, [VELOCITY[q][k] for q in range(NQ)]) / rho for k in range(3)]
    feq = _equilibrium(rho, u)
    g = [f[q] - feq[q] for q in range(NQ)]
    moments = []
    for a, b in ((0, 0), (1, 1), (2, 2), (0, 1), (0, 2), (1, 2)):
        moments.append(_combo(g, [VELOCITY[q][a] * VELOCITY[q][b] for q in range(NQ)]))
    stress_sq = (
        moments[0] * moments[0]
        + moments[1] * moments[1]
        + moments[2] * moments[2]
        + 2.0 * (moments[3] * moments[3] + moments[4] * moments[4] + moments[5] * moments[5])
    )
    shear = 1.5 * jnp.sqrt(stress_sq + 0.0001) / rho
    viscous = 0.02 * (shear + 0.01) ** (0.7 - 1.0)
    relax = 0.5 + 3.0 * viscous
    design = jnp.where(regions > 0, 1.0, 0.0).astype(jnp.float32)
    damp = porous * design
    outflow = _equilibrium(jnp.ones_like(rho), u)
    inlet = types == 2
    outlet = types == 3
    out = []
    for q in range(NQ):
        relaxed = f[q] - g[q] / relax - damp * (feq[q] - WEIGHTS[q] * rho)
        out.append(jnp.where(inlet, INFLOW[q], jnp.where(outlet, outflow[q], relaxed)))
    if not with_grad:
        return out
    fixed = jnp.logical_or(inlet, outlet)
    grad = [jnp.where(fixed, 0.0, -design * (feq[q] - WEIGHTS[q] * rho)) for q in range(NQ)]
    return out, grad


def _pieces(sign):
    out = []
    for q in range(NQ):
        oa, ot = sign * VELOCITY[q][0], sign * VELOCITY[q][1]
        if oa != 0:
            out.append((q, "a", oa, ot))
        if ot != 0:
            out.append((q, "t", oa, ot))
        if oa != 0 and ot != 0:
            out.append((q, "c", oa, ot))
    return out


FLAG_PIECES = [
    (0, "a", 1, 0),
    (0, "a", -1, 0),
    (0, "t", 0, 1),
    (0, "t", 0, -1),
    (0, "c", 1, 1),
    (0, "c", 1, -1),
    (0, "c", -1, 1),
    (0, "c", -1, -1),
]
NPIECE = 24


class Halo:
    def __init__(self, a_lo, a_hi, t_lo, t_hi):
        self.a_lo, self.a_hi, self.t_lo, self.t_hi = a_lo, a_hi, t_lo, t_hi


def _piece_refs(piece, field, halo, ca, ct):
    q, kind, oa, ot = piece
    a_face = ca - 1 if oa == -1 else 0
    t_face = ct - 1 if ot == -1 else 0
    if kind == "a":
        src = field.at[q, pl.ds(a_face, 1)]
        dst = (halo.a_lo if oa == -1 else halo.a_hi).at[q]
        move = (-oa, 0)
    elif kind == "t":
        src = field.at[q, :, pl.ds(t_face, 1)]
        dst = (halo.t_lo if ot == -1 else halo.t_hi).at[q, pl.ds(1, ca)]
        move = (0, -ot)
    else:
        src = field.at[q, pl.ds(a_face, 1), pl.ds(t_face, 1)]
        slot = 0 if oa == -1 else ca + 1
        dst = (halo.t_lo if ot == -1 else halo.t_hi).at[q, pl.ds(slot, 1)]
        move = (-oa, -ot)
    return src, dst, move


class Exchange:
    def __init__(self, pieces, field, halo, send_sem, recv_sem, pos, sizes, ca, ct):
        self.items = []
        me_ax, me_az = pos
        n_ax, n_az = sizes
        for i, piece in enumerate(pieces):
            src, dst, (da, dt) = _piece_refs(piece, field, halo, ca, ct)
            to_ax = me_ax + da
            from_ax = me_ax - da
            to_dev = (to_ax, lax.rem(me_az + dt + n_az, n_az))
            from_dev = (from_ax, lax.rem(me_az - dt + n_az, n_az))
            send = pltpu.make_async_remote_copy(
                src_ref=src, dst_ref=dst, send_sem=send_sem.at[i], recv_sem=recv_sem.at[i],
                device_id=to_dev, device_id_type=MESH)
            recv = pltpu.make_async_remote_copy(
                src_ref=src, dst_ref=dst, send_sem=send_sem.at[i], recv_sem=recv_sem.at[i],
                device_id=from_dev, device_id_type=MESH)
            send_ok = jnp.logical_and(to_ax >= 0, to_ax < n_ax) if da != 0 else None
            recv_ok = jnp.logical_and(from_ax >= 0, from_ax < n_ax) if da != 0 else None
            self.items.append((send, recv, send_ok, recv_ok))

    @staticmethod
    def _maybe(ok, fn):
        if ok is None:
            fn()
        else:
            pl.when(ok)(fn)

    def start(self):
        for send, _, ok, _ in self.items:
            self._maybe(ok, send.start)

    def wait_recv(self):
        for _, recv, _, ok in self.items:
            self._maybe(ok, recv.wait_recv)

    def wait_send(self):
        for send, _, ok, _ in self.items:
            self._maybe(ok, send.wait_send)


def _shift(own, halo, q, a, oa, ot, orr, lo_ok, hi_ok, ca, ct, nr, zero_r):
    ae = a + oa
    ok = None
    if ae < 0:
        slab = halo.a_lo[q, 0]
        ok = lo_ok
    elif ae >= ca:
        slab = halo.a_hi[q, 0]
        ok = hi_ok
    else:
        slab = own[q, ae]
    if ot != 0:
        rows = lax.broadcasted_iota(jnp.int32, (ct, nr), 0)
        if ot == -1:
            edge = halo.t_lo[q, ae + 1]
            slab = jnp.where(rows == 0, edge, pltpu.roll(slab, 1, 0))
        else:
            edge = halo.t_hi[q, ae + 1]
            slab = jnp.where(rows == ct - 1, edge, pltpu.roll(slab, ct - 1, 0))
    if orr != 0:
        lanes = lax.broadcasted_iota(jnp.int32, (ct, nr), 1)
        if orr == -1:
            slab = jnp.where(lanes == 0, zero_r, pltpu.roll(slab, 1, 1))
        else:
            slab = jnp.where(lanes == nr - 1, zero_r, pltpu.roll(slab, nr - 1, 1))
    if ok is not None:
        slab = jnp.where(ok, slab, zero_r)
    return slab


def _window_kernel(
    n_ax, n_az,
    init_hbm, seed_hbm, por_hbm, type_hbm, reg_hbm,
    final_ref, adj_ref, sens_ref, tot_ref,
    init_ref, seed_ref, por_ref, type_ref, reg_ref, load_sem,
    post0, state1, back1, post1, adj1, back0, gpor, sens1,
    pop_a_lo, pop_a_hi, pop_t_lo, pop_t_hi,
    ty_a_lo, ty_a_hi, ty_t_lo, ty_t_hi,
    send_sem, recv_sem, ty_send, ty_recv,
    part_ref, row_a, row_b, send_a, recv_a, send_b, recv_b, local,
):
    loads = [
        pltpu.make_async_copy(src, dst, load_sem.at[i])
        for i, (src, dst) in enumerate(
            ((type_hbm, type_ref), (seed_hbm, seed_ref), (init_hbm, init_ref),
             (por_hbm, por_ref), (reg_hbm, reg_ref)))
    ]
    for copy in loads:
        copy.start()
    _, ca, ct, nr = init_ref.shape
    me_ax, me_az = lax.axis_index("ax"), lax.axis_index("az")
    lo_ok = me_ax > 0
    hi_ok = me_ax < n_ax - 1
    pos, sizes = (me_ax, me_az), (n_ax, n_az)

    barrier = pltpu.get_barrier_semaphore()
    up_az, dn_az = lax.rem(me_az + 1, n_az), lax.rem(me_az + n_az - 1, n_az)
    for k in range(1, n_az):
        pl.semaphore_signal(barrier, 1, device_id=(me_ax, lax.rem(me_az + k, n_az)), device_id_type=MESH)
    for k in range(1, n_ax):
        pl.semaphore_signal(barrier, 1, device_id=(lax.rem(me_ax + k, n_ax), me_az), device_id_type=MESH)
    for ok, other in ((lo_ok, me_ax - 1), (hi_ok, me_ax + 1)):
        @pl.when(ok)
        def _():
            for dz in (up_az, dn_az):
                pl.semaphore_signal(barrier, 1, device_id=(other, dz), device_id_type=MESH)
    count = (n_az - 1) + (n_ax - 1) + 2 * (lo_ok.astype(jnp.int32) + hi_ok.astype(jnp.int32))
    for copy in loads:
        copy.wait()

    def halo(k):
        return Halo(pop_a_lo.at[k], pop_a_hi.at[k], pop_t_lo.at[k], pop_t_hi.at[k])

    ty_halo = Halo(ty_a_lo, ty_a_hi, ty_t_lo, ty_t_hi)
    ex_types = Exchange(FLAG_PIECES, type_ref, ty_halo, ty_send, ty_recv, pos, sizes, ca, ct)
    ex_seed = Exchange(_pieces(1), seed_ref, halo(0), send_sem.at[0], recv_sem.at[0], pos, sizes, ca, ct)

    steps = ca * (ct // TILE)

    def tile_at(i):
        a = i // (ct // TILE)
        t0 = pl.multiple_of((i % (ct // TILE)) * TILE, TILE)
        return a, pl.ds(t0, TILE)

    def load(ref, a, ts):
        return [ref[q, a, ts, :] for q in range(NQ)]

    def store(ref, a, ts, vals):
        for q in range(NQ):
            ref[q, a, ts, :] = vals[q]

    def collide_loop(src, dst, grad_dst):
        def body(i, carry):
            a, ts = tile_at(i)
            out, grad = _collide(load(src, a, ts), por_ref[a, ts, :], type_ref[0, a, ts, :],
                                 reg_ref[a, ts, :], with_grad=True)
            store(dst, a, ts, out)
            store(grad_dst, a, ts, grad)
            return carry
        lax.fori_loop(0, steps, body, 0)

    def vjp_loop(at, upstream, primal_dst, grad_dst, sens_dst):
        def body(i, carry):
            a, ts = tile_at(i)
            types = type_ref[0, a, ts, :]
            regions = reg_ref[a, ts, :]
            out, pullback = jax.vjp(
                lambda f, p: _collide(f, p, types, regions), load(at, a, ts), por_ref[a, ts, :])
            if primal_dst is not None:
                store(primal_dst, a, ts, out)
            d_f, d_p = pullback(load(upstream, a, ts))
            store(grad_dst, a, ts, d_f)
            if sens_dst is not None:
                sens_dst[a, ts, :] = d_p
            return carry
        lax.fori_loop(0, steps, body, 0)

    zero = jnp.zeros((ct, nr), jnp.float32)

    def flag_shift(a, oa, ot, orr):
        if oa == 0 and ot == 0 and orr == 0:
            own = type_ref[0, a]
            return jnp.where(own != 1, 1.0, 0.0).astype(jnp.float32)
        ty = _shift(type_ref, ty_halo, 0, a, oa, ot, orr, lo_ok, hi_ok, ca, ct, nr, jnp.ones((ct, nr), jnp.int32))
        return jnp.where(ty != 1, 1.0, 0.0).astype(jnp.float32)

    def stream(post, hal, dst):
        for a in range(ca):
            for q in range(NQ):
                c = VELOCITY[q]
                moved = _shift(post, hal, q, a, -c[0], -c[1], -c[2], lo_ok, hi_ok, ca, ct, nr, zero)
                ok = flag_shift(a, -c[0], -c[1], -c[2]) > 0
                dst[q, a] = jnp.where(ok, moved, post[OPPOSITE[q], a])

    def stream_adjoint(adj, hal, dst):
        for a in range(ca):
            centre = flag_shift(a, 0, 0, 0)
            for q in range(NQ):
                c = VELOCITY[q]
                ahead = _shift(adj, hal, q, a, c[0], c[1], c[2], lo_ok, hi_ok, ca, ct, nr, zero)
                blocked = 1.0 - flag_shift(a, c[0], c[1], c[2])
                dst[q, a] = centre * ahead + blocked * adj[OPPOSITE[q], a]

    collide_loop(init_ref, post0, gpor)
    pl.semaphore_wait(barrier, count)
    ex_post0 = Exchange(_pieces(-1), post0, halo(1), send_sem.at[1], recv_sem.at[1], pos, sizes, ca, ct)
    ex_post0.start()
    ex_types.start()
    ex_seed.start()
    ex_types.wait_recv()
    ex_post0.wait_recv()
    stream(post0, halo(1), state1)
    ex_seed.wait_recv()
    stream_adjoint(seed_ref, halo(0), back1)
    vjp_loop(state1, back1, post1, adj1, sens1)
    ex_post1 = Exchange(_pieces(-1), post1, halo(2), send_sem.at[2], recv_sem.at[2], pos, sizes, ca, ct)
    ex_adj1 = Exchange(_pieces(1), adj1, halo(3), send_sem.at[3], recv_sem.at[3], pos, sizes, ca, ct)
    ex_adj1.start()
    ex_post1.start()
    ex_adj1.wait_recv()
    stream_adjoint(adj1, halo(3), back0)
    for a in range(ca):
        sens0 = back0[0, a] * gpor[0, a]
        for q in range(1, NQ):
            sens0 = sens0 + back0[q, a] * gpor[q, a]
        sens_ref[a] = sens1[a] + sens0

    total = jnp.zeros((1, 1), jnp.float32)
    rid = jnp.zeros((1, 1), jnp.int32)
    for a in range(ca):
        reg = reg_ref[a]
        total = total + jnp.sum(jnp.where(reg > 0, sens_ref[a], 0.0), keepdims=True)
        rid = jnp.maximum(rid, jnp.max(reg, keepdims=True))
    labels = lax.broadcasted_iota(jnp.int32, part_ref.shape, 1) + 1
    part_ref[...] = jnp.where(labels == rid, total, 0.0)
    first = _TotalsStage(part_ref, row_a, send_a, recv_a, local.at[0], me_az, n_az,
                         lambda j: (me_ax, j))
    first.start()

    vjp_loop(init_ref, back0, None, adj_ref, None)
    ex_post1.wait_recv()
    stream(post1, halo(2), final_ref)

    first.finish(part_ref)
    own = pltpu.make_async_copy(part_ref, row_b.at[me_ax], local.at[1])
    own.start()
    own.wait()
    second = _TotalsStage(row_b.at[me_ax], row_b, send_b, recv_b, None, me_ax, n_ax,
                          lambda j: (j, me_az))
    second.start()
    second.finish(tot_ref)

    for ex in (ex_types, ex_seed, ex_post0, ex_post1, ex_adj1):
        ex.wait_send()


class _TotalsStage:
    def __init__(self, src, rows, send, recv, own_sem, me, n, device):
        self.src, self.rows, self.own_sem, self.me, self.n = src, rows, own_sem, me, n
        self.sends, self.recvs = [], []
        for k in range(1, n):
            to, frm = lax.rem(me + k, n), lax.rem(me + n - k, n)
            self.sends.append(pltpu.make_async_remote_copy(
                src_ref=src, dst_ref=rows.at[me], send_sem=send.at[k], recv_sem=recv.at[me],
                device_id=device(to), device_id_type=MESH))
            self.recvs.append(pltpu.make_async_remote_copy(
                src_ref=src, dst_ref=rows.at[frm], send_sem=send.at[k], recv_sem=recv.at[frm],
                device_id=device(frm), device_id_type=MESH))

    def start(self):
        self.own = None
        if self.own_sem is not None:
            self.own = pltpu.make_async_copy(self.src, self.rows.at[self.me], self.own_sem)
            self.own.start()
        for copy in self.sends:
            copy.start()

    def finish(self, out):
        if self.own is not None:
            self.own.wait()
        for copy in self.recvs:
            copy.wait_recv()
        acc = self.rows[0]
        for j in range(1, self.n):
            acc = acc + self.rows[j]
        for copy in self.sends:
            copy.wait_send()
        out[...] = acc


def window(initial, adjoint_seed, porosity, cell_type, region, n_regions):
    n_ax, n_az = lax.axis_size("ax"), lax.axis_size("az")
    nq, ca, ct, nr = initial.shape
    pop = jax.ShapeDtypeStruct(initial.shape, jnp.float32)
    cells = jax.ShapeDtypeStruct(porosity.shape, jnp.float32)
    vmem = pltpu.VMEM
    f32, i32 = jnp.float32, jnp.int32
    scratch = (
        [vmem(initial.shape, f32), vmem(initial.shape, f32), vmem(porosity.shape, f32),
         vmem((1,) + cell_type.shape, i32), vmem(region.shape, i32), pltpu.SemaphoreType.DMA((5,))]

        + [vmem((nq, ca, ct, nr), f32) for _ in range(7)]
        + [vmem((ca, ct, nr), f32)]
        + [vmem((4, nq, 1, ct, nr), f32), vmem((4, nq, 1, ct, nr), f32),
           vmem((4, nq, ca + 2, 1, nr), f32), vmem((4, nq, ca + 2, 1, nr), f32)]
        + [vmem((1, 1, ct, nr), i32), vmem((1, 1, ct, nr), i32),
           vmem((1, ca + 2, 1, nr), i32), vmem((1, ca + 2, 1, nr), i32)]
        + [pltpu.SemaphoreType.DMA((4, NPIECE)), pltpu.SemaphoreType.DMA((4, NPIECE)),
           pltpu.SemaphoreType.DMA((len(FLAG_PIECES),)), pltpu.SemaphoreType.DMA((len(FLAG_PIECES),))]
        + [vmem((1, n_regions), f32), vmem((n_az, 1, n_regions), f32), vmem((n_ax, 1, n_regions), f32),
           pltpu.SemaphoreType.DMA((n_az,)), pltpu.SemaphoreType.DMA((n_az,)),
           pltpu.SemaphoreType.DMA((n_ax,)), pltpu.SemaphoreType.DMA((n_ax,)),
           pltpu.SemaphoreType.DMA((2,))]
    )
    final, adj, sens, tot = pl.pallas_call(
        functools.partial(_window_kernel, n_ax, n_az),
        out_shape=(pop, pop, cells, jax.ShapeDtypeStruct((1, n_regions), f32)),
        in_specs=[pl.BlockSpec(memory_space=pltpu.HBM)] * 5,
        out_specs=(pl.BlockSpec(memory_space=vmem),) * 4,
        scratch_shapes=scratch,
        compiler_params=pltpu.CompilerParams(collective_id=1, has_side_effects=True,
                                             vmem_limit_bytes=67043328),
    )(initial, adjoint_seed, porosity, cell_type.reshape((1,) + cell_type.shape), region)
    return final, adj, sens, tot


def shards(initial, adjoint_seed, porosity, cell_type, region):
    n_regions = lax.axis_size("ax") * lax.axis_size("az") // 4
    final, adjoint, sensitivity, totals = window(
        initial, adjoint_seed, porosity, cell_type, region, n_regions)
    totals = totals.reshape(-1)
    return (final, adjoint, sensitivity, totals)


def solution(mesh):
    return jax.shard_map(
        shards,
        mesh=mesh,
        in_specs=(
            P(None, "ax", "az", None),
            P(None, "ax", "az", None),
            P("ax", "az", None),
            P("ax", "az", None),
            P("ax", "az", None),
        ),
        out_specs=(P(None, "ax", "az", None), P(None, "ax", "az", None), P("ax", "az", None), P()),
        check_vma=False,
    )
```

```python
import functools

import numpy as np

import jax
import jax.numpy as jnp
from jax import lax
from jax.experimental import pallas as pl
from jax.experimental.pallas import tpu as pltpu
from jax.sharding import PartitionSpec as P

MESH = pl.DeviceIdType.MESH

VELOCITY = [
    (0, 0, 0),
    (1, 0, 0),
    (-1, 0, 0),
    (0, 1, 0),
    (0, -1, 0),
    (0, 0, 1),
    (0, 0, -1),
    (1, 1, 0),
    (-1, -1, 0),
    (1, -1, 0),
    (-1, 1, 0),
    (1, 0, 1),
    (-1, 0, -1),
    (1, 0, -1),
    (-1, 0, 1),
    (0, 1, 1),
    (0, -1, -1),
    (0, 1, -1),
    (0, -1, 1),
]
OPPOSITE = [0, 2, 1, 4, 3, 6, 5, 8, 7, 10, 9, 12, 11, 14, 13, 16, 15, 18, 17]
WEIGHTS = [1.0 / 3.0] + [1.0 / 18.0] * 6 + [1.0 / 36.0] * 12
INLET_SPEED = (0.05, 0.05, 0.0)
NQ = 19
TILE = 8


def _inflow_constants():
    w = np.array(WEIGHTS, np.float32)
    u = np.array(INLET_SPEED, np.float32)
    c = np.array(VELOCITY, np.float32)
    proj = (c * u[None, :]).sum(1, dtype=np.float32).astype(np.float32)
    usq = np.float32((u * u).sum(dtype=np.float32))
    one = np.float32(1.0)
    val = w * one * (one + np.float32(3.0) * proj + np.float32(4.5) * proj * proj - np.float32(1.5) * usq)
    return [float(v) for v in val.astype(np.float32)]


INFLOW = _inflow_constants()


def _combo(values, coeffs):
    acc = None
    for v, c in zip(values, coeffs):
        if c == 0:
            continue
        term = v if c == 1 else (-v if c == -1 else c * v)
        acc = term if acc is None else acc + term
    return acc


def _equilibrium(rho, u):
    usq = u[0] * u[0] + u[1] * u[1] + u[2] * u[2]
    out = []
    for q in range(NQ):
        p = _combo(u, VELOCITY[q])
        if p is None:
            inner = 1.0 - 1.5 * usq
        else:
            inner = 1.0 + 3.0 * p + 4.5 * p * p - 1.5 * usq
        out.append(WEIGHTS[q] * rho * inner)
    return out


def _collide(f, porous, types, regions, with_grad=False):
    rho = f[0]
    for q in range(1, NQ):
        rho = rho + f[q]
    u = [_combo(f, [VELOCITY[q][k] for q in range(NQ)]) / rho for k in range(3)]
    feq = _equilibrium(rho, u)
    g = [f[q] - feq[q] for q in range(NQ)]
    moments = []
    for a, b in ((0, 0), (1, 1), (2, 2), (0, 1), (0, 2), (1, 2)):
        moments.append(_combo(g, [VELOCITY[q][a] * VELOCITY[q][b] for q in range(NQ)]))
    stress_sq = (
        moments[0] * moments[0]
        + moments[1] * moments[1]
        + moments[2] * moments[2]
        + 2.0 * (moments[3] * moments[3] + moments[4] * moments[4] + moments[5] * moments[5])
    )
    shear = 1.5 * jnp.sqrt(stress_sq + 0.0001) / rho
    viscous = 0.02 * (shear + 0.01) ** (0.7 - 1.0)
    relax = 0.5 + 3.0 * viscous
    design = jnp.where(regions > 0, 1.0, 0.0).astype(jnp.float32)
    damp = porous * design
    outflow = _equilibrium(jnp.ones_like(rho), u)
    inlet = types == 2
    outlet = types == 3
    out = []
    for q in range(NQ):
        relaxed = f[q] - g[q] / relax - damp * (feq[q] - WEIGHTS[q] * rho)
        out.append(jnp.where(inlet, INFLOW[q], jnp.where(outlet, outflow[q], relaxed)))
    if not with_grad:
        return out
    fixed = jnp.logical_or(inlet, outlet)
    grad = [jnp.where(fixed, 0.0, -design * (feq[q] - WEIGHTS[q] * rho)) for q in range(NQ)]
    return out, grad


def _pieces(sign):
    out = []
    for q in range(NQ):
        oa, ot = sign * VELOCITY[q][0], sign * VELOCITY[q][1]
        if oa != 0:
            out.append((q, "a", oa, ot))
        if ot != 0:
            out.append((q, "t", oa, ot))
        if oa != 0 and ot != 0:
            out.append((q, "c", oa, ot))
    return out


FLAG_PIECES = [
    (0, "a", 1, 0),
    (0, "a", -1, 0),
    (0, "t", 0, 1),
    (0, "t", 0, -1),
    (0, "c", 1, 1),
    (0, "c", 1, -1),
    (0, "c", -1, 1),
    (0, "c", -1, -1),
]
NPIECE = 24


class Halo:
    def __init__(self, a_lo, a_hi, t_lo, t_hi):
        self.a_lo, self.a_hi, self.t_lo, self.t_hi = a_lo, a_hi, t_lo, t_hi


def _piece_refs(piece, field, halo, ca, ct):
    q, kind, oa, ot = piece
    a_face = ca - 1 if oa == -1 else 0
    t_face = ct - 1 if ot == -1 else 0
    if kind == "a":
        src = field.at[q, pl.ds(a_face, 1)]
        dst = (halo.a_lo if oa == -1 else halo.a_hi).at[q]
        move = (-oa, 0)
    elif kind == "t":
        src = field.at[q, :, pl.ds(t_face, 1)]
        dst = (halo.t_lo if ot == -1 else halo.t_hi).at[q, pl.ds(1, ca)]
        move = (0, -ot)
    else:
        src = field.at[q, pl.ds(a_face, 1), pl.ds(t_face, 1)]
        slot = 0 if oa == -1 else ca + 1
        dst = (halo.t_lo if ot == -1 else halo.t_hi).at[q, pl.ds(slot, 1)]
        move = (-oa, -ot)
    return src, dst, move


class Exchange:
    def __init__(self, pieces, field, halo, send_sem, recv_sem, pos, sizes, ca, ct):
        self.items = []
        me_ax, me_az = pos
        n_ax, n_az = sizes
        for i, piece in enumerate(pieces):
            src, dst, (da, dt) = _piece_refs(piece, field, halo, ca, ct)
            to_ax = me_ax + da
            from_ax = me_ax - da
            to_dev = (to_ax, lax.rem(me_az + dt + n_az, n_az))
            from_dev = (from_ax, lax.rem(me_az - dt + n_az, n_az))
            send = pltpu.make_async_remote_copy(
                src_ref=src, dst_ref=dst, send_sem=send_sem.at[i], recv_sem=recv_sem.at[i],
                device_id=to_dev, device_id_type=MESH)
            recv = pltpu.make_async_remote_copy(
                src_ref=src, dst_ref=dst, send_sem=send_sem.at[i], recv_sem=recv_sem.at[i],
                device_id=from_dev, device_id_type=MESH)
            send_ok = jnp.logical_and(to_ax >= 0, to_ax < n_ax) if da != 0 else None
            recv_ok = jnp.logical_and(from_ax >= 0, from_ax < n_ax) if da != 0 else None
            self.items.append((send, recv, send_ok, recv_ok))

    @staticmethod
    def _maybe(ok, fn):
        if ok is None:
            fn()
        else:
            pl.when(ok)(fn)

    def start(self):
        for send, _, ok, _ in self.items:
            self._maybe(ok, send.start)

    def wait_recv(self):
        for _, recv, _, ok in self.items:
            self._maybe(ok, recv.wait_recv)

    def wait_send(self):
        for send, _, ok, _ in self.items:
            self._maybe(ok, send.wait_send)


def _shift(own, halo, q, a, oa, ot, orr, lo_ok, hi_ok, ca, ct, nr, zero_r):
    ae = a + oa
    ok = None
    if ae < 0:
        slab = halo.a_lo[q, 0]
        ok = lo_ok
    elif ae >= ca:
        slab = halo.a_hi[q, 0]
        ok = hi_ok
    else:
        slab = own[q, ae]
    if ot != 0:
        rows = lax.broadcasted_iota(jnp.int32, (ct, nr), 0)
        if ot == -1:
            edge = halo.t_lo[q, ae + 1]
            slab = jnp.where(rows == 0, edge, pltpu.roll(slab, 1, 0))
        else:
            edge = halo.t_hi[q, ae + 1]
            slab = jnp.where(rows == ct - 1, edge, pltpu.roll(slab, ct - 1, 0))
    if orr != 0:
        lanes = lax.broadcasted_iota(jnp.int32, (ct, nr), 1)
        if orr == -1:
            slab = jnp.where(lanes == 0, zero_r, pltpu.roll(slab, 1, 1))
        else:
            slab = jnp.where(lanes == nr - 1, zero_r, pltpu.roll(slab, nr - 1, 1))
    if ok is not None:
        slab = jnp.where(ok, slab, zero_r)
    return slab


def _window_kernel(
    n_ax, n_az,
    init_hbm, seed_hbm, por_hbm, type_hbm, reg_hbm,
    final_ref, adj_ref, sens_ref, tot_ref,
    init_ref, seed_ref, por_ref, type_ref, reg_ref, load_sem,
    post0, state1, back1, post1, adj1, back0, gpor, sens1,
    pop_a_lo, pop_a_hi, pop_t_lo, pop_t_hi,
    ty_a_lo, ty_a_hi, ty_t_lo, ty_t_hi,
    send_sem, recv_sem, ty_send, ty_recv,
    part_ref, row_a, row_b, send_a, recv_a, send_b, recv_b, local,
    row_c, send_c, recv_c,
):
    loads = [
        pltpu.make_async_copy(src, dst, load_sem.at[i])
        for i, (src, dst) in enumerate(
            ((type_hbm, type_ref), (seed_hbm, seed_ref), (init_hbm, init_ref),
             (por_hbm, por_ref), (reg_hbm, reg_ref)))
    ]
    for copy in loads:
        copy.start()
    _, ca, ct, nr = init_ref.shape
    me_ax, me_az = lax.axis_index("ax"), lax.axis_index("az")
    n_lo = max(d for d in range(1, 9) if n_ax % d == 0)
    lo_ok = me_ax > 0
    hi_ok = me_ax < n_ax - 1
    pos, sizes = (me_ax, me_az), (n_ax, n_az)

    barrier = pltpu.get_barrier_semaphore()
    up_az, dn_az = lax.rem(me_az + 1, n_az), lax.rem(me_az + n_az - 1, n_az)
    for k in range(1, n_az):
        pl.semaphore_signal(barrier, 1, device_id=(me_ax, lax.rem(me_az + k, n_az)), device_id_type=MESH)
    for k in range(1, n_ax):
        pl.semaphore_signal(barrier, 1, device_id=(lax.rem(me_ax + k, n_ax), me_az), device_id_type=MESH)
    for ok, other in ((lo_ok, me_ax - 1), (hi_ok, me_ax + 1)):
        @pl.when(ok)
        def _():
            for dz in (up_az, dn_az):
                pl.semaphore_signal(barrier, 1, device_id=(other, dz), device_id_type=MESH)
    count = (n_az - 1) + (n_ax - 1) + 2 * (lo_ok.astype(jnp.int32) + hi_ok.astype(jnp.int32))
    for copy in loads:
        copy.wait()

    def halo(k):
        return Halo(pop_a_lo.at[k], pop_a_hi.at[k], pop_t_lo.at[k], pop_t_hi.at[k])

    ty_halo = Halo(ty_a_lo, ty_a_hi, ty_t_lo, ty_t_hi)
    ex_types = Exchange(FLAG_PIECES, type_ref, ty_halo, ty_send, ty_recv, pos, sizes, ca, ct)
    ex_seed = Exchange(_pieces(1), seed_ref, halo(0), send_sem.at[0], recv_sem.at[0], pos, sizes, ca, ct)

    steps = ca * (ct // TILE)

    def tile_at(i):
        a = i // (ct // TILE)
        t0 = pl.multiple_of((i % (ct // TILE)) * TILE, TILE)
        return a, pl.ds(t0, TILE)

    def load(ref, a, ts):
        return [ref[q, a, ts, :] for q in range(NQ)]

    def store(ref, a, ts, vals):
        for q in range(NQ):
            ref[q, a, ts, :] = vals[q]

    def collide_loop(src, dst, grad_dst):
        def body(i, carry):
            a, ts = tile_at(i)
            out, grad = _collide(load(src, a, ts), por_ref[a, ts, :], type_ref[0, a, ts, :],
                                 reg_ref[a, ts, :], with_grad=True)
            store(dst, a, ts, out)
            store(grad_dst, a, ts, grad)
            return carry
        lax.fori_loop(0, steps, body, 0)

    def vjp_loop(at, upstream, primal_dst, grad_dst, sens_dst):
        def body(i, carry):
            a, ts = tile_at(i)
            types = type_ref[0, a, ts, :]
            regions = reg_ref[a, ts, :]
            out, pullback = jax.vjp(
                lambda f, p: _collide(f, p, types, regions), load(at, a, ts), por_ref[a, ts, :])
            if primal_dst is not None:
                store(primal_dst, a, ts, out)
            d_f, d_p = pullback(load(upstream, a, ts))
            store(grad_dst, a, ts, d_f)
            if sens_dst is not None:
                sens_dst[a, ts, :] = d_p
            return carry
        lax.fori_loop(0, steps, body, 0)

    zero = jnp.zeros((ct, nr), jnp.float32)

    def flag_shift(a, oa, ot, orr):
        if oa == 0 and ot == 0 and orr == 0:
            own = type_ref[0, a]
            return jnp.where(own != 1, 1.0, 0.0).astype(jnp.float32)
        ty = _shift(type_ref, ty_halo, 0, a, oa, ot, orr, lo_ok, hi_ok, ca, ct, nr, jnp.ones((ct, nr), jnp.int32))
        return jnp.where(ty != 1, 1.0, 0.0).astype(jnp.float32)

    def stream(post, hal, dst):
        for a in range(ca):
            for q in range(NQ):
                c = VELOCITY[q]
                moved = _shift(post, hal, q, a, -c[0], -c[1], -c[2], lo_ok, hi_ok, ca, ct, nr, zero)
                ok = flag_shift(a, -c[0], -c[1], -c[2]) > 0
                dst[q, a] = jnp.where(ok, moved, post[OPPOSITE[q], a])

    def stream_adjoint(adj, hal, dst):
        for a in range(ca):
            centre = flag_shift(a, 0, 0, 0)
            for q in range(NQ):
                c = VELOCITY[q]
                ahead = _shift(adj, hal, q, a, c[0], c[1], c[2], lo_ok, hi_ok, ca, ct, nr, zero)
                blocked = 1.0 - flag_shift(a, c[0], c[1], c[2])
                dst[q, a] = centre * ahead + blocked * adj[OPPOSITE[q], a]

    collide_loop(init_ref, post0, gpor)
    pl.semaphore_wait(barrier, count)
    ex_post0 = Exchange(_pieces(-1), post0, halo(1), send_sem.at[1], recv_sem.at[1], pos, sizes, ca, ct)
    ex_post0.start()
    ex_types.start()
    ex_seed.start()
    ex_types.wait_recv()
    ex_post0.wait_recv()
    stream(post0, halo(1), state1)
    ex_seed.wait_recv()
    stream_adjoint(seed_ref, halo(0), back1)
    vjp_loop(state1, back1, post1, adj1, sens1)
    ex_post1 = Exchange(_pieces(-1), post1, halo(2), send_sem.at[2], recv_sem.at[2], pos, sizes, ca, ct)
    ex_adj1 = Exchange(_pieces(1), adj1, halo(3), send_sem.at[3], recv_sem.at[3], pos, sizes, ca, ct)
    ex_adj1.start()
    ex_post1.start()
    ex_adj1.wait_recv()
    stream_adjoint(adj1, halo(3), back0)
    for a in range(ca):
        sens0 = back0[0, a] * gpor[0, a]
        for q in range(1, NQ):
            sens0 = sens0 + back0[q, a] * gpor[q, a]
        sens_ref[a] = sens1[a] + sens0

    total = jnp.zeros((1, 1), jnp.float32)
    rid = jnp.zeros((1, 1), jnp.int32)
    for a in range(ca):
        reg = reg_ref[a]
        total = total + jnp.sum(jnp.where(reg > 0, sens_ref[a], 0.0), keepdims=True)
        rid = jnp.maximum(rid, jnp.max(reg, keepdims=True))
    labels = lax.broadcasted_iota(jnp.int32, part_ref.shape, 1) + 1
    part_ref[...] = jnp.where(labels == rid, total, 0.0)
    first = _TotalsStage(part_ref, row_a, send_a, recv_a, local.at[0], me_az, n_az,
                         lambda j: (me_ax, j))
    first.start()

    vjp_loop(init_ref, back0, None, adj_ref, None)
    ex_post1.wait_recv()
    stream(post1, halo(2), final_ref)

    first.finish(part_ref)
    ax_lo, ax_hi = lax.rem(me_ax, n_lo), me_ax // n_lo
    own = pltpu.make_async_copy(part_ref, row_b.at[ax_lo], local.at[1])
    own.start()
    own.wait()
    second = _TotalsStage(row_b.at[ax_lo], row_b, send_b, recv_b, None, ax_lo, n_lo,
                          lambda j: (ax_hi * n_lo + j, me_az))
    second.start()
    second.finish(part_ref)
    own = pltpu.make_async_copy(part_ref, row_c.at[ax_hi], local.at[2])
    own.start()
    own.wait()
    third = _TotalsStage(row_c.at[ax_hi], row_c, send_c, recv_c, None, ax_hi, n_ax // n_lo,
                         lambda j: (j * n_lo + ax_lo, me_az))
    third.start()
    third.finish(tot_ref)

    for ex in (ex_types, ex_seed, ex_post0, ex_post1, ex_adj1):
        ex.wait_send()


class _TotalsStage:
    def __init__(self, src, rows, send, recv, own_sem, me, n, device):
        self.src, self.rows, self.own_sem, self.me, self.n = src, rows, own_sem, me, n
        self.sends, self.recvs = [], []
        for k in range(1, n):
            to, frm = lax.rem(me + k, n), lax.rem(me + n - k, n)
            self.sends.append(pltpu.make_async_remote_copy(
                src_ref=src, dst_ref=rows.at[me], send_sem=send.at[k], recv_sem=recv.at[me],
                device_id=device(to), device_id_type=MESH))
            self.recvs.append(pltpu.make_async_remote_copy(
                src_ref=src, dst_ref=rows.at[frm], send_sem=send.at[k], recv_sem=recv.at[frm],
                device_id=device(frm), device_id_type=MESH))

    def start(self):
        self.own = None
        if self.own_sem is not None:
            self.own = pltpu.make_async_copy(self.src, self.rows.at[self.me], self.own_sem)
            self.own.start()
        for copy in self.sends:
            copy.start()

    def finish(self, out):
        if self.own is not None:
            self.own.wait()
        for copy in self.recvs:
            copy.wait_recv()
        acc = self.rows[0]
        for j in range(1, self.n):
            acc = acc + self.rows[j]
        for copy in self.sends:
            copy.wait_send()
        out[...] = acc


def window(initial, adjoint_seed, porosity, cell_type, region, n_regions):
    n_ax, n_az = lax.axis_size("ax"), lax.axis_size("az")
    nq, ca, ct, nr = initial.shape
    pop = jax.ShapeDtypeStruct(initial.shape, jnp.float32)
    cells = jax.ShapeDtypeStruct(porosity.shape, jnp.float32)
    vmem = pltpu.VMEM
    f32, i32 = jnp.float32, jnp.int32
    scratch = (
        [vmem(initial.shape, f32), vmem(initial.shape, f32), vmem(porosity.shape, f32),
         vmem((1,) + cell_type.shape, i32), vmem(region.shape, i32), pltpu.SemaphoreType.DMA((5,))]

        + [vmem((nq, ca, ct, nr), f32) for _ in range(7)]
        + [vmem((ca, ct, nr), f32)]
        + [vmem((4, nq, 1, ct, nr), f32), vmem((4, nq, 1, ct, nr), f32),
           vmem((4, nq, ca + 2, 1, nr), f32), vmem((4, nq, ca + 2, 1, nr), f32)]
        + [vmem((1, 1, ct, nr), i32), vmem((1, 1, ct, nr), i32),
           vmem((1, ca + 2, 1, nr), i32), vmem((1, ca + 2, 1, nr), i32)]
        + [pltpu.SemaphoreType.DMA((4, NPIECE)), pltpu.SemaphoreType.DMA((4, NPIECE)),
           pltpu.SemaphoreType.DMA((len(FLAG_PIECES),)), pltpu.SemaphoreType.DMA((len(FLAG_PIECES),))]
        + [vmem((1, n_regions), f32), vmem((n_az, 1, n_regions), f32), vmem((n_ax, 1, n_regions), f32),
           pltpu.SemaphoreType.DMA((n_az,)), pltpu.SemaphoreType.DMA((n_az,)),
           pltpu.SemaphoreType.DMA((n_ax,)), pltpu.SemaphoreType.DMA((n_ax,)),
           pltpu.SemaphoreType.DMA((3,))]
        + [vmem((n_ax, 1, n_regions), f32),
           pltpu.SemaphoreType.DMA((n_ax,)), pltpu.SemaphoreType.DMA((n_ax,))]
    )
    final, adj, sens, tot = pl.pallas_call(
        functools.partial(_window_kernel, n_ax, n_az),
        out_shape=(pop, pop, cells, jax.ShapeDtypeStruct((1, n_regions), f32)),
        in_specs=[pl.BlockSpec(memory_space=pltpu.HBM)] * 5,
        out_specs=(pl.BlockSpec(memory_space=vmem),) * 4,
        scratch_shapes=scratch,
        compiler_params=pltpu.CompilerParams(collective_id=1, has_side_effects=True,
                                             vmem_limit_bytes=67043328),
    )(initial, adjoint_seed, porosity, cell_type.reshape((1,) + cell_type.shape), region)
    return final, adj, sens, tot


def shards(initial, adjoint_seed, porosity, cell_type, region):
    n_regions = lax.axis_size("ax") * lax.axis_size("az") // 4
    final, adjoint, sensitivity, totals = window(
        initial, adjoint_seed, porosity, cell_type, region, n_regions)
    totals = totals.reshape(-1)
    return (final, adjoint, sensitivity, totals)


def solution(mesh):
    return jax.shard_map(
        shards,
        mesh=mesh,
        in_specs=(
            P(None, "ax", "az", None),
            P(None, "ax", "az", None),
            P("ax", "az", None),
            P("ax", "az", None),
            P("ax", "az", None),
        ),
        out_specs=(P(None, "ax", "az", None), P(None, "ax", "az", None), P("ax", "az", None), P()),
        check_vma=False,
    )
```

```python
import functools

import numpy as np

import jax
import jax.numpy as jnp
from jax import lax
from jax.experimental import pallas as pl
from jax.experimental.pallas import tpu as pltpu
from jax.sharding import PartitionSpec as P

MESH = pl.DeviceIdType.MESH

VELOCITY = [
    (0, 0, 0),
    (1, 0, 0),
    (-1, 0, 0),
    (0, 1, 0),
    (0, -1, 0),
    (0, 0, 1),
    (0, 0, -1),
    (1, 1, 0),
    (-1, -1, 0),
    (1, -1, 0),
    (-1, 1, 0),
    (1, 0, 1),
    (-1, 0, -1),
    (1, 0, -1),
    (-1, 0, 1),
    (0, 1, 1),
    (0, -1, -1),
    (0, 1, -1),
    (0, -1, 1),
]
OPPOSITE = [0, 2, 1, 4, 3, 6, 5, 8, 7, 10, 9, 12, 11, 14, 13, 16, 15, 18, 17]
WEIGHTS = [1.0 / 3.0] + [1.0 / 18.0] * 6 + [1.0 / 36.0] * 12
INLET_SPEED = (0.05, 0.05, 0.0)
NQ = 19
TILE = 8


def _inflow_constants():
    w = np.array(WEIGHTS, np.float32)
    u = np.array(INLET_SPEED, np.float32)
    c = np.array(VELOCITY, np.float32)
    proj = (c * u[None, :]).sum(1, dtype=np.float32).astype(np.float32)
    usq = np.float32((u * u).sum(dtype=np.float32))
    one = np.float32(1.0)
    val = w * one * (one + np.float32(3.0) * proj + np.float32(4.5) * proj * proj - np.float32(1.5) * usq)
    return [float(v) for v in val.astype(np.float32)]


INFLOW = _inflow_constants()


def _combo(values, coeffs):
    acc = None
    for v, c in zip(values, coeffs):
        if c == 0:
            continue
        term = v if c == 1 else (-v if c == -1 else c * v)
        acc = term if acc is None else acc + term
    return acc


def _equilibrium(rho, u):
    usq = u[0] * u[0] + u[1] * u[1] + u[2] * u[2]
    out = []
    for q in range(NQ):
        p = _combo(u, VELOCITY[q])
        if p is None:
            inner = 1.0 - 1.5 * usq
        else:
            inner = 1.0 + 3.0 * p + 4.5 * p * p - 1.5 * usq
        out.append(WEIGHTS[q] * rho * inner)
    return out


def _collide(f, porous, types, regions, with_grad=False):
    rho = f[0]
    for q in range(1, NQ):
        rho = rho + f[q]
    u = [_combo(f, [VELOCITY[q][k] for q in range(NQ)]) / rho for k in range(3)]
    feq = _equilibrium(rho, u)
    g = [f[q] - feq[q] for q in range(NQ)]
    moments = []
    for a, b in ((0, 0), (1, 1), (2, 2), (0, 1), (0, 2), (1, 2)):
        moments.append(_combo(g, [VELOCITY[q][a] * VELOCITY[q][b] for q in range(NQ)]))
    stress_sq = (
        moments[0] * moments[0]
        + moments[1] * moments[1]
        + moments[2] * moments[2]
        + 2.0 * (moments[3] * moments[3] + moments[4] * moments[4] + moments[5] * moments[5])
    )
    shear = 1.5 * jnp.sqrt(stress_sq + 0.0001) / rho
    viscous = 0.02 * (shear + 0.01) ** (0.7 - 1.0)
    relax = 0.5 + 3.0 * viscous
    design = jnp.where(regions > 0, 1.0, 0.0).astype(jnp.float32)
    damp = porous * design
    outflow = _equilibrium(jnp.ones_like(rho), u)
    inlet = types == 2
    outlet = types == 3
    out = []
    for q in range(NQ):
        relaxed = f[q] - g[q] / relax - damp * (feq[q] - WEIGHTS[q] * rho)
        out.append(jnp.where(inlet, INFLOW[q], jnp.where(outlet, outflow[q], relaxed)))
    if not with_grad:
        return out
    fixed = jnp.logical_or(inlet, outlet)
    grad = [jnp.where(fixed, 0.0, -design * (feq[q] - WEIGHTS[q] * rho)) for q in range(NQ)]
    return out, grad


def _pieces(sign):
    out = []
    for q in range(NQ):
        oa, ot = sign * VELOCITY[q][0], sign * VELOCITY[q][1]
        if oa != 0:
            out.append((q, "a", oa, ot))
        if ot != 0:
            out.append((q, "t", oa, ot))
        if oa != 0 and ot != 0:
            out.append((q, "c", oa, ot))
    return out


FLAG_PIECES = [
    (0, "a", 1, 0),
    (0, "a", -1, 0),
    (0, "t", 0, 1),
    (0, "t", 0, -1),
    (0, "c", 1, 1),
    (0, "c", 1, -1),
    (0, "c", -1, 1),
    (0, "c", -1, -1),
]
NPIECE = 24


class Halo:
    def __init__(self, a_lo, a_hi, t_lo, t_hi):
        self.a_lo, self.a_hi, self.t_lo, self.t_hi = a_lo, a_hi, t_lo, t_hi


def _piece_refs(piece, field, halo, ca, ct):
    q, kind, oa, ot = piece
    a_face = ca - 1 if oa == -1 else 0
    t_face = ct - 1 if ot == -1 else 0
    if kind == "a":
        src = field.at[q, pl.ds(a_face, 1)]
        dst = (halo.a_lo if oa == -1 else halo.a_hi).at[q]
        move = (-oa, 0)
    elif kind == "t":
        src = field.at[q, :, pl.ds(t_face, 1)]
        dst = (halo.t_lo if ot == -1 else halo.t_hi).at[q, pl.ds(1, ca)]
        move = (0, -ot)
    else:
        src = field.at[q, pl.ds(a_face, 1), pl.ds(t_face, 1)]
        slot = 0 if oa == -1 else ca + 1
        dst = (halo.t_lo if ot == -1 else halo.t_hi).at[q, pl.ds(slot, 1)]
        move = (-oa, -ot)
    return src, dst, move


class Exchange:
    def __init__(self, pieces, field, halo, send_sem, recv_sem, pos, sizes, ca, ct):
        self.items = []
        me_ax, me_az = pos
        n_ax, n_az = sizes
        for i, piece in enumerate(pieces):
            src, dst, (da, dt) = _piece_refs(piece, field, halo, ca, ct)
            to_ax = me_ax + da
            from_ax = me_ax - da
            to_dev = (to_ax, lax.rem(me_az + dt + n_az, n_az))
            from_dev = (from_ax, lax.rem(me_az - dt + n_az, n_az))
            send = pltpu.make_async_remote_copy(
                src_ref=src, dst_ref=dst, send_sem=send_sem.at[i], recv_sem=recv_sem.at[i],
                device_id=to_dev, device_id_type=MESH)
            recv = pltpu.make_async_remote_copy(
                src_ref=src, dst_ref=dst, send_sem=send_sem.at[i], recv_sem=recv_sem.at[i],
                device_id=from_dev, device_id_type=MESH)
            send_ok = jnp.logical_and(to_ax >= 0, to_ax < n_ax) if da != 0 else None
            recv_ok = jnp.logical_and(from_ax >= 0, from_ax < n_ax) if da != 0 else None
            self.items.append((send, recv, send_ok, recv_ok))

    @staticmethod
    def _maybe(ok, fn):
        if ok is None:
            fn()
        else:
            pl.when(ok)(fn)

    def start(self):
        for send, _, ok, _ in self.items:
            self._maybe(ok, send.start)

    def wait_recv(self):
        for _, recv, _, ok in self.items:
            self._maybe(ok, recv.wait_recv)

    def wait_send(self):
        for send, _, ok, _ in self.items:
            self._maybe(ok, send.wait_send)


def _shift(own, halo, q, a, oa, ot, orr, lo_ok, hi_ok, ca, ct, nr, zero_r):
    ae = a + oa
    ok = None
    if ae < 0:
        slab = halo.a_lo[q, 0]
        ok = lo_ok
    elif ae >= ca:
        slab = halo.a_hi[q, 0]
        ok = hi_ok
    else:
        slab = own[q, ae]
    if ot != 0:
        rows = lax.broadcasted_iota(jnp.int32, (ct, nr), 0)
        if ot == -1:
            edge = halo.t_lo[q, ae + 1]
            slab = jnp.where(rows == 0, edge, pltpu.roll(slab, 1, 0))
        else:
            edge = halo.t_hi[q, ae + 1]
            slab = jnp.where(rows == ct - 1, edge, pltpu.roll(slab, ct - 1, 0))
    if orr != 0:
        lanes = lax.broadcasted_iota(jnp.int32, (ct, nr), 1)
        if orr == -1:
            slab = jnp.where(lanes == 0, zero_r, pltpu.roll(slab, 1, 1))
        else:
            slab = jnp.where(lanes == nr - 1, zero_r, pltpu.roll(slab, nr - 1, 1))
    if ok is not None:
        slab = jnp.where(ok, slab, zero_r)
    return slab


def _window_kernel(
    n_ax, n_az,
    init_hbm, seed_hbm, por_hbm, type_hbm, reg_hbm,
    final_ref, adj_ref, sens_ref, tot_ref,
    init_ref, seed_ref, por_ref, type_ref, reg_ref, load_sem,
    post0, state1, back1, post1, adj1, back0, gpor, fmask, sens1,
    pop_a_lo, pop_a_hi, pop_t_lo, pop_t_hi,
    ty_a_lo, ty_a_hi, ty_t_lo, ty_t_hi,
    send_sem, recv_sem, ty_send, ty_recv,
    part_ref, row_a, row_b, send_a, recv_a, send_b, recv_b, local,
):
    loads = [
        pltpu.make_async_copy(src, dst, load_sem.at[i])
        for i, (src, dst) in enumerate(
            ((type_hbm, type_ref), (seed_hbm, seed_ref), (init_hbm, init_ref),
             (por_hbm, por_ref), (reg_hbm, reg_ref)))
    ]
    for copy in loads:
        copy.start()
    _, ca, ct, nr = init_ref.shape
    me_ax, me_az = lax.axis_index("ax"), lax.axis_index("az")
    lo_ok = me_ax > 0
    hi_ok = me_ax < n_ax - 1
    pos, sizes = (me_ax, me_az), (n_ax, n_az)

    barrier = pltpu.get_barrier_semaphore()
    up_az, dn_az = lax.rem(me_az + 1, n_az), lax.rem(me_az + n_az - 1, n_az)
    for k in range(1, n_az):
        pl.semaphore_signal(barrier, 1, device_id=(me_ax, lax.rem(me_az + k, n_az)), device_id_type=MESH)
    for k in range(1, n_ax):
        pl.semaphore_signal(barrier, 1, device_id=(lax.rem(me_ax + k, n_ax), me_az), device_id_type=MESH)
    for ok, other in ((lo_ok, me_ax - 1), (hi_ok, me_ax + 1)):
        @pl.when(ok)
        def _():
            for dz in (up_az, dn_az):
                pl.semaphore_signal(barrier, 1, device_id=(other, dz), device_id_type=MESH)
    count = (n_az - 1) + (n_ax - 1) + 2 * (lo_ok.astype(jnp.int32) + hi_ok.astype(jnp.int32))
    for copy in loads:
        copy.wait()

    def halo(k):
        return Halo(pop_a_lo.at[k], pop_a_hi.at[k], pop_t_lo.at[k], pop_t_hi.at[k])

    ty_halo = Halo(ty_a_lo, ty_a_hi, ty_t_lo, ty_t_hi)
    ex_types = Exchange(FLAG_PIECES, type_ref, ty_halo, ty_send, ty_recv, pos, sizes, ca, ct)
    ex_seed = Exchange(_pieces(1), seed_ref, halo(0), send_sem.at[0], recv_sem.at[0], pos, sizes, ca, ct)

    steps = ca * (ct // TILE)

    def tile_at(i):
        a = i // (ct // TILE)
        t0 = pl.multiple_of((i % (ct // TILE)) * TILE, TILE)
        return a, pl.ds(t0, TILE)

    def load(ref, a, ts):
        return [ref[q, a, ts, :] for q in range(NQ)]

    def store(ref, a, ts, vals):
        for q in range(NQ):
            ref[q, a, ts, :] = vals[q]

    def collide_loop(src, dst, grad_dst):
        def body(i, carry):
            a, ts = tile_at(i)
            out, grad = _collide(load(src, a, ts), por_ref[a, ts, :], type_ref[0, a, ts, :],
                                 reg_ref[a, ts, :], with_grad=True)
            store(dst, a, ts, out)
            store(grad_dst, a, ts, grad)
            return carry
        lax.fori_loop(0, steps, body, 0)

    def vjp_loop(at, upstream, primal_dst, grad_dst, sens_dst):
        def body(i, carry):
            a, ts = tile_at(i)
            types = type_ref[0, a, ts, :]
            regions = reg_ref[a, ts, :]
            out, pullback = jax.vjp(
                lambda f, p: _collide(f, p, types, regions), load(at, a, ts), por_ref[a, ts, :])
            if primal_dst is not None:
                store(primal_dst, a, ts, out)
            d_f, d_p = pullback(load(upstream, a, ts))
            store(grad_dst, a, ts, d_f)
            if sens_dst is not None:
                sens_dst[a, ts, :] = d_p
            return carry
        lax.fori_loop(0, steps, body, 0)

    zero = jnp.zeros((ct, nr), jnp.float32)

    def flag_shift(a, oa, ot, orr):
        if oa == 0 and ot == 0 and orr == 0:
            own = type_ref[0, a]
            return jnp.where(own != 1, 1.0, 0.0).astype(jnp.float32)
        ty = _shift(type_ref, ty_halo, 0, a, oa, ot, orr, lo_ok, hi_ok, ca, ct, nr, jnp.ones((ct, nr), jnp.int32))
        return jnp.where(ty != 1, 1.0, 0.0).astype(jnp.float32)

    def fill_masks():
        for a in range(ca):
            for q in range(NQ):
                c = VELOCITY[q]
                fmask[q, a] = flag_shift(a, -c[0], -c[1], -c[2])

    def stream(post, hal, dst):
        for a in range(ca):
            for q in range(NQ):
                c = VELOCITY[q]
                moved = _shift(post, hal, q, a, -c[0], -c[1], -c[2], lo_ok, hi_ok, ca, ct, nr, zero)
                ok = fmask[q, a] > 0
                dst[q, a] = jnp.where(ok, moved, post[OPPOSITE[q], a])

    def stream_adjoint(adj, hal, dst):
        for a in range(ca):
            centre = fmask[0, a]
            for q in range(NQ):
                c = VELOCITY[q]
                ahead = _shift(adj, hal, q, a, c[0], c[1], c[2], lo_ok, hi_ok, ca, ct, nr, zero)
                blocked = 1.0 - fmask[OPPOSITE[q], a]
                dst[q, a] = centre * ahead + blocked * adj[OPPOSITE[q], a]

    collide_loop(init_ref, post0, gpor)
    pl.semaphore_wait(barrier, count)
    ex_post0 = Exchange(_pieces(-1), post0, halo(1), send_sem.at[1], recv_sem.at[1], pos, sizes, ca, ct)
    ex_types.start()
    ex_post0.start()
    ex_seed.start()
    ex_types.wait_recv()
    fill_masks()
    ex_post0.wait_recv()
    stream(post0, halo(1), state1)
    ex_seed.wait_recv()
    stream_adjoint(seed_ref, halo(0), back1)
    vjp_loop(state1, back1, post1, adj1, sens1)
    ex_post1 = Exchange(_pieces(-1), post1, halo(2), send_sem.at[2], recv_sem.at[2], pos, sizes, ca, ct)
    ex_adj1 = Exchange(_pieces(1), adj1, halo(3), send_sem.at[3], recv_sem.at[3], pos, sizes, ca, ct)
    ex_adj1.start()
    ex_post1.start()
    ex_adj1.wait_recv()
    stream_adjoint(adj1, halo(3), back0)
    for a in range(ca):
        sens0 = back0[0, a] * gpor[0, a]
        for q in range(1, NQ):
            sens0 = sens0 + back0[q, a] * gpor[q, a]
        sens_ref[a] = sens1[a] + sens0

    total = jnp.zeros((1, 1), jnp.float32)
    rid = jnp.zeros((1, 1), jnp.int32)
    for a in range(ca):
        reg = reg_ref[a]
        total = total + jnp.sum(jnp.where(reg > 0, sens_ref[a], 0.0), keepdims=True)
        rid = jnp.maximum(rid, jnp.max(reg, keepdims=True))
    labels = lax.broadcasted_iota(jnp.int32, part_ref.shape, 1) + 1
    part_ref[...] = jnp.where(labels == rid, total, 0.0)
    first = _TotalsStage(part_ref, row_a, send_a, recv_a, local.at[0], me_az, n_az,
                         lambda j: (me_ax, j))
    first.start()

    vjp_loop(init_ref, back0, None, adj_ref, None)
    ex_post1.wait_recv()
    stream(post1, halo(2), final_ref)

    first.finish(part_ref)
    own = pltpu.make_async_copy(part_ref, row_b.at[me_ax], local.at[1])
    own.start()
    own.wait()
    second = _TotalsStage(row_b.at[me_ax], row_b, send_b, recv_b, None, me_ax, n_ax,
                          lambda j: (j, me_az))
    second.start()
    second.finish(tot_ref)

    for ex in (ex_types, ex_seed, ex_post0, ex_post1, ex_adj1):
        ex.wait_send()


class _TotalsStage:
    def __init__(self, src, rows, send, recv, own_sem, me, n, device):
        self.src, self.rows, self.own_sem, self.me, self.n = src, rows, own_sem, me, n
        self.sends, self.recvs = [], []
        for k in range(1, n):
            to, frm = lax.rem(me + k, n), lax.rem(me + n - k, n)
            self.sends.append(pltpu.make_async_remote_copy(
                src_ref=src, dst_ref=rows.at[me], send_sem=send.at[k], recv_sem=recv.at[me],
                device_id=device(to), device_id_type=MESH))
            self.recvs.append(pltpu.make_async_remote_copy(
                src_ref=src, dst_ref=rows.at[frm], send_sem=send.at[k], recv_sem=recv.at[frm],
                device_id=device(frm), device_id_type=MESH))

    def start(self):
        self.own = None
        if self.own_sem is not None:
            self.own = pltpu.make_async_copy(self.src, self.rows.at[self.me], self.own_sem)
            self.own.start()
        for copy in self.sends:
            copy.start()

    def finish(self, out):
        if self.own is not None:
            self.own.wait()
        for copy in self.recvs:
            copy.wait_recv()
        acc = self.rows[0]
        for j in range(1, self.n):
            acc = acc + self.rows[j]
        for copy in self.sends:
            copy.wait_send()
        out[...] = acc


def window(initial, adjoint_seed, porosity, cell_type, region, n_regions):
    n_ax, n_az = lax.axis_size("ax"), lax.axis_size("az")
    nq, ca, ct, nr = initial.shape
    pop = jax.ShapeDtypeStruct(initial.shape, jnp.float32)
    cells = jax.ShapeDtypeStruct(porosity.shape, jnp.float32)
    vmem = pltpu.VMEM
    f32, i32 = jnp.float32, jnp.int32
    scratch = (
        [vmem(initial.shape, f32), vmem(initial.shape, f32), vmem(porosity.shape, f32),
         vmem((1,) + cell_type.shape, i32), vmem(region.shape, i32), pltpu.SemaphoreType.DMA((5,))]

        + [vmem((nq, ca, ct, nr), f32) for _ in range(8)]
        + [vmem((ca, ct, nr), f32)]
        + [vmem((4, nq, 1, ct, nr), f32), vmem((4, nq, 1, ct, nr), f32),
           vmem((4, nq, ca + 2, 1, nr), f32), vmem((4, nq, ca + 2, 1, nr), f32)]
        + [vmem((1, 1, ct, nr), i32), vmem((1, 1, ct, nr), i32),
           vmem((1, ca + 2, 1, nr), i32), vmem((1, ca + 2, 1, nr), i32)]
        + [pltpu.SemaphoreType.DMA((4, NPIECE)), pltpu.SemaphoreType.DMA((4, NPIECE)),
           pltpu.SemaphoreType.DMA((len(FLAG_PIECES),)), pltpu.SemaphoreType.DMA((len(FLAG_PIECES),))]
        + [vmem((1, n_regions), f32), vmem((n_az, 1, n_regions), f32), vmem((n_ax, 1, n_regions), f32),
           pltpu.SemaphoreType.DMA((n_az,)), pltpu.SemaphoreType.DMA((n_az,)),
           pltpu.SemaphoreType.DMA((n_ax,)), pltpu.SemaphoreType.DMA((n_ax,)),
           pltpu.SemaphoreType.DMA((2,))]
    )
    final, adj, sens, tot = pl.pallas_call(
        functools.partial(_window_kernel, n_ax, n_az),
        out_shape=(pop, pop, cells, jax.ShapeDtypeStruct((1, n_regions), f32)),
        in_specs=[pl.BlockSpec(memory_space=pltpu.HBM)] * 5,
        out_specs=(pl.BlockSpec(memory_space=vmem),) * 4,
        scratch_shapes=scratch,
        compiler_params=pltpu.CompilerParams(collective_id=1, has_side_effects=True,
                                             vmem_limit_bytes=67043328),
    )(initial, adjoint_seed, porosity, cell_type.reshape((1,) + cell_type.shape), region)
    return final, adj, sens, tot


def shards(initial, adjoint_seed, porosity, cell_type, region):
    n_regions = lax.axis_size("ax") * lax.axis_size("az") // 4
    final, adjoint, sensitivity, totals = window(
        initial, adjoint_seed, porosity, cell_type, region, n_regions)
    totals = totals.reshape(-1)
    return (final, adjoint, sensitivity, totals)


def solution(mesh):
    return jax.shard_map(
        shards,
        mesh=mesh,
        in_specs=(
            P(None, "ax", "az", None),
            P(None, "ax", "az", None),
            P("ax", "az", None),
            P("ax", "az", None),
            P("ax", "az", None),
        ),
        out_specs=(P(None, "ax", "az", None), P(None, "ax", "az", None), P("ax", "az", None), P()),
        check_vma=False,
    )
```

```python
import functools

import numpy as np

import jax
import jax.numpy as jnp
from jax import lax
from jax.experimental import pallas as pl
from jax.experimental.pallas import tpu as pltpu
from jax.sharding import PartitionSpec as P

MESH = pl.DeviceIdType.MESH

VELOCITY = [
    (0, 0, 0),
    (1, 0, 0),
    (-1, 0, 0),
    (0, 1, 0),
    (0, -1, 0),
    (0, 0, 1),
    (0, 0, -1),
    (1, 1, 0),
    (-1, -1, 0),
    (1, -1, 0),
    (-1, 1, 0),
    (1, 0, 1),
    (-1, 0, -1),
    (1, 0, -1),
    (-1, 0, 1),
    (0, 1, 1),
    (0, -1, -1),
    (0, 1, -1),
    (0, -1, 1),
]
OPPOSITE = [0, 2, 1, 4, 3, 6, 5, 8, 7, 10, 9, 12, 11, 14, 13, 16, 15, 18, 17]
WEIGHTS = [1.0 / 3.0] + [1.0 / 18.0] * 6 + [1.0 / 36.0] * 12
INLET_SPEED = (0.05, 0.05, 0.0)
NQ = 19
TILE = 8


def _inflow_constants():
    w = np.array(WEIGHTS, np.float32)
    u = np.array(INLET_SPEED, np.float32)
    c = np.array(VELOCITY, np.float32)
    proj = (c * u[None, :]).sum(1, dtype=np.float32).astype(np.float32)
    usq = np.float32((u * u).sum(dtype=np.float32))
    one = np.float32(1.0)
    val = w * one * (one + np.float32(3.0) * proj + np.float32(4.5) * proj * proj - np.float32(1.5) * usq)
    return [float(v) for v in val.astype(np.float32)]


INFLOW = _inflow_constants()


def _combo(values, coeffs):
    acc = None
    for v, c in zip(values, coeffs):
        if c == 0:
            continue
        term = v if c == 1 else (-v if c == -1 else c * v)
        acc = term if acc is None else acc + term
    return acc


def _equilibrium(rho, u):
    usq = u[0] * u[0] + u[1] * u[1] + u[2] * u[2]
    out = []
    for q in range(NQ):
        p = _combo(u, VELOCITY[q])
        if p is None:
            inner = 1.0 - 1.5 * usq
        else:
            inner = 1.0 + 3.0 * p + 4.5 * p * p - 1.5 * usq
        out.append(WEIGHTS[q] * rho * inner)
    return out


def _collide(f, porous, types, regions, with_grad=False):
    rho = f[0]
    for q in range(1, NQ):
        rho = rho + f[q]
    u = [_combo(f, [VELOCITY[q][k] for q in range(NQ)]) / rho for k in range(3)]
    feq = _equilibrium(rho, u)
    g = [f[q] - feq[q] for q in range(NQ)]
    moments = []
    for a, b in ((0, 0), (1, 1), (2, 2), (0, 1), (0, 2), (1, 2)):
        moments.append(_combo(g, [VELOCITY[q][a] * VELOCITY[q][b] for q in range(NQ)]))
    stress_sq = (
        moments[0] * moments[0]
        + moments[1] * moments[1]
        + moments[2] * moments[2]
        + 2.0 * (moments[3] * moments[3] + moments[4] * moments[4] + moments[5] * moments[5])
    )
    shear = 1.5 * jnp.sqrt(stress_sq + 0.0001) / rho
    viscous = 0.02 * (shear + 0.01) ** (0.7 - 1.0)
    relax = 0.5 + 3.0 * viscous
    design = jnp.where(regions > 0, 1.0, 0.0).astype(jnp.float32)
    damp = porous * design
    outflow = _equilibrium(jnp.ones_like(rho), u)
    inlet = types == 2
    outlet = types == 3
    out = []
    for q in range(NQ):
        relaxed = f[q] - g[q] / relax - damp * (feq[q] - WEIGHTS[q] * rho)
        out.append(jnp.where(inlet, INFLOW[q], jnp.where(outlet, outflow[q], relaxed)))
    if not with_grad:
        return out
    fixed = jnp.logical_or(inlet, outlet)
    grad = [jnp.where(fixed, 0.0, -design * (feq[q] - WEIGHTS[q] * rho)) for q in range(NQ)]
    return out, grad


def _pieces(sign):
    out = []
    for q in range(NQ):
        oa, ot = sign * VELOCITY[q][0], sign * VELOCITY[q][1]
        if oa != 0:
            out.append((q, "a", oa, ot))
        if ot != 0:
            out.append((q, "t", oa, ot))
        if oa != 0 and ot != 0:
            out.append((q, "c", oa, ot))
    return out


FLAG_PIECES = [
    (0, "a", 1, 0),
    (0, "a", -1, 0),
    (0, "t", 0, 1),
    (0, "t", 0, -1),
    (0, "c", 1, 1),
    (0, "c", 1, -1),
    (0, "c", -1, 1),
    (0, "c", -1, -1),
]
NPIECE = 24


class Halo:
    def __init__(self, a_lo, a_hi, t_lo, t_hi):
        self.a_lo, self.a_hi, self.t_lo, self.t_hi = a_lo, a_hi, t_lo, t_hi


def _piece_refs(piece, field, halo, ca, ct):
    q, kind, oa, ot = piece
    a_face = ca - 1 if oa == -1 else 0
    t_face = ct - 1 if ot == -1 else 0
    if kind == "a":
        src = field.at[q, pl.ds(a_face, 1)]
        dst = (halo.a_lo if oa == -1 else halo.a_hi).at[q]
        move = (-oa, 0)
    elif kind == "t":
        src = field.at[q, :, pl.ds(t_face, 1)]
        dst = (halo.t_lo if ot == -1 else halo.t_hi).at[q, pl.ds(1, ca)]
        move = (0, -ot)
    else:
        src = field.at[q, pl.ds(a_face, 1), pl.ds(t_face, 1)]
        slot = 0 if oa == -1 else ca + 1
        dst = (halo.t_lo if ot == -1 else halo.t_hi).at[q, pl.ds(slot, 1)]
        move = (-oa, -ot)
    return src, dst, move


class Exchange:
    def __init__(self, pieces, field, halo, send_sem, recv_sem, pos, sizes, ca, ct):
        self.items = []
        me_ax, me_az = pos
        n_ax, n_az = sizes
        for i, piece in enumerate(pieces):
            src, dst, (da, dt) = _piece_refs(piece, field, halo, ca, ct)
            to_ax = me_ax + da
            from_ax = me_ax - da
            to_dev = (to_ax, lax.rem(me_az + dt + n_az, n_az))
            from_dev = (from_ax, lax.rem(me_az - dt + n_az, n_az))
            send = pltpu.make_async_remote_copy(
                src_ref=src, dst_ref=dst, send_sem=send_sem.at[i], recv_sem=recv_sem.at[i],
                device_id=to_dev, device_id_type=MESH)
            recv = pltpu.make_async_remote_copy(
                src_ref=src, dst_ref=dst, send_sem=send_sem.at[i], recv_sem=recv_sem.at[i],
                device_id=from_dev, device_id_type=MESH)
            send_ok = jnp.logical_and(to_ax >= 0, to_ax < n_ax) if da != 0 else None
            recv_ok = jnp.logical_and(from_ax >= 0, from_ax < n_ax) if da != 0 else None
            self.items.append((send, recv, send_ok, recv_ok))

    @staticmethod
    def _maybe(ok, fn):
        if ok is None:
            fn()
        else:
            pl.when(ok)(fn)

    def start(self):
        for send, _, ok, _ in self.items:
            self._maybe(ok, send.start)

    def wait_recv(self):
        for _, recv, _, ok in self.items:
            self._maybe(ok, recv.wait_recv)

    def wait_send(self):
        for send, _, ok, _ in self.items:
            self._maybe(ok, send.wait_send)


def _shift(own, halo, q, a, oa, ot, orr, lo_ok, hi_ok, ca, ct, nr, zero_r):
    ae = a + oa
    ok = None
    if ae < 0:
        slab = halo.a_lo[q, 0]
        ok = lo_ok
    elif ae >= ca:
        slab = halo.a_hi[q, 0]
        ok = hi_ok
    else:
        slab = own[q, ae]
    if ot != 0:
        rows = lax.broadcasted_iota(jnp.int32, (ct, nr), 0)
        if ot == -1:
            edge = halo.t_lo[q, ae + 1]
            slab = jnp.where(rows == 0, edge, pltpu.roll(slab, 1, 0))
        else:
            edge = halo.t_hi[q, ae + 1]
            slab = jnp.where(rows == ct - 1, edge, pltpu.roll(slab, ct - 1, 0))
    if orr != 0:
        lanes = lax.broadcasted_iota(jnp.int32, (ct, nr), 1)
        if orr == -1:
            slab = jnp.where(lanes == 0, zero_r, pltpu.roll(slab, 1, 1))
        else:
            slab = jnp.where(lanes == nr - 1, zero_r, pltpu.roll(slab, nr - 1, 1))
    if ok is not None:
        slab = jnp.where(ok, slab, zero_r)
    return slab


def _window_kernel(
    n_ax, n_az,
    init_hbm, seed_hbm, por_hbm, type_hbm, reg_hbm,
    final_ref, adj_ref, sens_ref, tot_ref,
    init_ref, seed_ref, por_ref, type_ref, reg_ref, load_sem,
    post0, state1, back1, post1, adj1, back0, gpor, fmask, sens1,
    pop_a_lo, pop_a_hi, pop_t_lo, pop_t_hi,
    ty_a_lo, ty_a_hi, ty_t_lo, ty_t_hi,
    send_sem, recv_sem, ty_send, ty_recv,
    part_ref, row_a, row_b, send_a, recv_a, send_b, recv_b, local,
):
    loads = [
        pltpu.make_async_copy(src, dst, load_sem.at[i])
        for i, (src, dst) in enumerate(
            ((type_hbm, type_ref), (seed_hbm, seed_ref), (init_hbm, init_ref),
             (por_hbm, por_ref), (reg_hbm, reg_ref)))
    ]
    for copy in loads:
        copy.start()
    _, ca, ct, nr = init_ref.shape
    me_ax, me_az = lax.axis_index("ax"), lax.axis_index("az")
    lo_ok = me_ax > 0
    hi_ok = me_ax < n_ax - 1
    pos, sizes = (me_ax, me_az), (n_ax, n_az)

    barrier = pltpu.get_barrier_semaphore()
    up_az, dn_az = lax.rem(me_az + 1, n_az), lax.rem(me_az + n_az - 1, n_az)
    for k in range(1, n_az):
        pl.semaphore_signal(barrier, 1, device_id=(me_ax, lax.rem(me_az + k, n_az)), device_id_type=MESH)
    for k in range(1, n_ax):
        pl.semaphore_signal(barrier, 1, device_id=(lax.rem(me_ax + k, n_ax), me_az), device_id_type=MESH)
    for ok, other in ((lo_ok, me_ax - 1), (hi_ok, me_ax + 1)):
        @pl.when(ok)
        def _():
            for dz in (up_az, dn_az):
                pl.semaphore_signal(barrier, 1, device_id=(other, dz), device_id_type=MESH)
    count = (n_az - 1) + (n_ax - 1) + 2 * (lo_ok.astype(jnp.int32) + hi_ok.astype(jnp.int32))
    for copy in loads:
        copy.wait()

    def halo(k):
        return Halo(pop_a_lo.at[k], pop_a_hi.at[k], pop_t_lo.at[k], pop_t_hi.at[k])

    ty_halo = Halo(ty_a_lo, ty_a_hi, ty_t_lo, ty_t_hi)
    ex_types = Exchange(FLAG_PIECES, type_ref, ty_halo, ty_send, ty_recv, pos, sizes, ca, ct)
    ex_seed = Exchange(_pieces(1), seed_ref, halo(0), send_sem.at[0], recv_sem.at[0], pos, sizes, ca, ct)

    steps = ca * (ct // TILE)

    def tile_at(i):
        a = i // (ct // TILE)
        t0 = pl.multiple_of((i % (ct // TILE)) * TILE, TILE)
        return a, pl.ds(t0, TILE)

    def load(ref, a, ts):
        return [ref[q, a, ts, :] for q in range(NQ)]

    def store(ref, a, ts, vals):
        for q in range(NQ):
            ref[q, a, ts, :] = vals[q]

    def collide_loop(src, dst, grad_dst):
        def body(i, carry):
            a, ts = tile_at(i)
            out, grad = _collide(load(src, a, ts), por_ref[a, ts, :], type_ref[0, a, ts, :],
                                 reg_ref[a, ts, :], with_grad=True)
            store(dst, a, ts, out)
            store(grad_dst, a, ts, grad)
            return carry
        lax.fori_loop(0, steps, body, 0)

    def vjp_loop(at, upstream, primal_dst, grad_dst, sens_dst):
        def body(i, carry):
            a, ts = tile_at(i)
            types = type_ref[0, a, ts, :]
            regions = reg_ref[a, ts, :]
            out, pullback = jax.vjp(
                lambda f, p: _collide(f, p, types, regions), load(at, a, ts), por_ref[a, ts, :])
            if primal_dst is not None:
                store(primal_dst, a, ts, out)
            d_f, d_p = pullback(load(upstream, a, ts))
            store(grad_dst, a, ts, d_f)
            if sens_dst is not None:
                sens_dst[a, ts, :] = d_p
            return carry
        lax.fori_loop(0, steps, body, 0)

    zero = jnp.zeros((ct, nr), jnp.float32)

    def flag_shift(a, oa, ot, orr):
        if oa == 0 and ot == 0 and orr == 0:
            own = type_ref[0, a]
            return jnp.where(own != 1, 1.0, 0.0).astype(jnp.float32)
        ty = _shift(type_ref, ty_halo, 0, a, oa, ot, orr, lo_ok, hi_ok, ca, ct, nr, jnp.ones((ct, nr), jnp.int32))
        return jnp.where(ty != 1, 1.0, 0.0).astype(jnp.float32)

    def fill_masks():
        for a in range(ca):
            for q in range(NQ):
                c = VELOCITY[q]
                fmask[q, a] = flag_shift(a, -c[0], -c[1], -c[2])

    def stream(post, hal, dst):
        for a in range(ca):
            for q in range(NQ):
                c = VELOCITY[q]
                moved = _shift(post, hal, q, a, -c[0], -c[1], -c[2], lo_ok, hi_ok, ca, ct, nr, zero)
                ok = fmask[q, a] > 0
                dst[q, a] = jnp.where(ok, moved, post[OPPOSITE[q], a])

    def stream_adjoint(adj, hal, dst):
        for a in range(ca):
            centre = fmask[0, a]
            for q in range(NQ):
                c = VELOCITY[q]
                ahead = _shift(adj, hal, q, a, c[0], c[1], c[2], lo_ok, hi_ok, ca, ct, nr, zero)
                blocked = 1.0 - fmask[OPPOSITE[q], a]
                dst[q, a] = centre * ahead + blocked * adj[OPPOSITE[q], a]

    collide_loop(init_ref, post0, gpor)
    pl.semaphore_wait(barrier, count)
    ex_post0 = Exchange(_pieces(-1), post0, halo(1), send_sem.at[1], recv_sem.at[1], pos, sizes, ca, ct)
    ex_types.start()
    ex_post0.start()
    ex_seed.start()
    ex_types.wait_recv()
    fill_masks()
    ex_post0.wait_recv()
    stream(post0, halo(1), state1)
    ex_seed.wait_recv()
    stream_adjoint(seed_ref, halo(0), back1)
    vjp_loop(state1, back1, post1, adj1, sens1)
    ex_post1 = Exchange(_pieces(-1), post1, halo(2), send_sem.at[2], recv_sem.at[2], pos, sizes, ca, ct)
    ex_adj1 = Exchange(_pieces(1), adj1, halo(3), send_sem.at[3], recv_sem.at[3], pos, sizes, ca, ct)
    ex_adj1.start()
    ex_post1.start()
    ex_adj1.wait_recv()
    stream_adjoint(adj1, halo(3), back0)
    for a in range(ca):
        sens0 = back0[0, a] * gpor[0, a]
        for q in range(1, NQ):
            sens0 = sens0 + back0[q, a] * gpor[q, a]
        sens_ref[a] = sens1[a] + sens0

    total = jnp.zeros((1, 1), jnp.float32)
    rid = jnp.zeros((1, 1), jnp.int32)
    for a in range(ca):
        reg = reg_ref[a]
        total = total + jnp.sum(jnp.where(reg > 0, sens_ref[a], 0.0), keepdims=True)
        rid = jnp.maximum(rid, jnp.max(reg, keepdims=True))
    labels = lax.broadcasted_iota(jnp.int32, part_ref.shape, 1) + 1
    part_ref[...] = jnp.where(labels == rid, total, 0.0)
    first = _TotalsStage(part_ref, row_a, send_a, recv_a, local.at[0], me_az, n_az,
                         lambda j: (me_ax, j))
    first.start()

    vjp_loop(init_ref, back0, None, adj_ref, None)

    first.finish(part_ref)
    own = pltpu.make_async_copy(part_ref, row_b.at[me_ax], local.at[1])
    own.start()
    own.wait()
    second = _TotalsStage(row_b.at[me_ax], row_b, send_b, recv_b, None, me_ax, n_ax,
                          lambda j: (j, me_az))
    second.start()
    ex_post1.wait_recv()
    stream(post1, halo(2), final_ref)
    second.finish(tot_ref)

    for ex in (ex_types, ex_seed, ex_post0, ex_post1, ex_adj1):
        ex.wait_send()


class _TotalsStage:
    def __init__(self, src, rows, send, recv, own_sem, me, n, device):
        self.src, self.rows, self.own_sem, self.me, self.n = src, rows, own_sem, me, n
        self.sends, self.recvs = [], []
        for k in range(1, n):
            to, frm = lax.rem(me + k, n), lax.rem(me + n - k, n)
            self.sends.append(pltpu.make_async_remote_copy(
                src_ref=src, dst_ref=rows.at[me], send_sem=send.at[k], recv_sem=recv.at[me],
                device_id=device(to), device_id_type=MESH))
            self.recvs.append(pltpu.make_async_remote_copy(
                src_ref=src, dst_ref=rows.at[frm], send_sem=send.at[k], recv_sem=recv.at[frm],
                device_id=device(frm), device_id_type=MESH))

    def start(self):
        self.own = None
        if self.own_sem is not None:
            self.own = pltpu.make_async_copy(self.src, self.rows.at[self.me], self.own_sem)
            self.own.start()
        for copy in self.sends:
            copy.start()

    def finish(self, out):
        if self.own is not None:
            self.own.wait()
        for copy in self.recvs:
            copy.wait_recv()
        acc = self.rows[0]
        for j in range(1, self.n):
            acc = acc + self.rows[j]
        for copy in self.sends:
            copy.wait_send()
        out[...] = acc


def window(initial, adjoint_seed, porosity, cell_type, region, n_regions):
    n_ax, n_az = lax.axis_size("ax"), lax.axis_size("az")
    nq, ca, ct, nr = initial.shape
    pop = jax.ShapeDtypeStruct(initial.shape, jnp.float32)
    cells = jax.ShapeDtypeStruct(porosity.shape, jnp.float32)
    vmem = pltpu.VMEM
    f32, i32 = jnp.float32, jnp.int32
    scratch = (
        [vmem(initial.shape, f32), vmem(initial.shape, f32), vmem(porosity.shape, f32),
         vmem((1,) + cell_type.shape, i32), vmem(region.shape, i32), pltpu.SemaphoreType.DMA((5,))]

        + [vmem((nq, ca, ct, nr), f32) for _ in range(8)]
        + [vmem((ca, ct, nr), f32)]
        + [vmem((4, nq, 1, ct, nr), f32), vmem((4, nq, 1, ct, nr), f32),
           vmem((4, nq, ca + 2, 1, nr), f32), vmem((4, nq, ca + 2, 1, nr), f32)]
        + [vmem((1, 1, ct, nr), i32), vmem((1, 1, ct, nr), i32),
           vmem((1, ca + 2, 1, nr), i32), vmem((1, ca + 2, 1, nr), i32)]
        + [pltpu.SemaphoreType.DMA((4, NPIECE)), pltpu.SemaphoreType.DMA((4, NPIECE)),
           pltpu.SemaphoreType.DMA((len(FLAG_PIECES),)), pltpu.SemaphoreType.DMA((len(FLAG_PIECES),))]
        + [vmem((1, n_regions), f32), vmem((n_az, 1, n_regions), f32), vmem((n_ax, 1, n_regions), f32),
           pltpu.SemaphoreType.DMA((n_az,)), pltpu.SemaphoreType.DMA((n_az,)),
           pltpu.SemaphoreType.DMA((n_ax,)), pltpu.SemaphoreType.DMA((n_ax,)),
           pltpu.SemaphoreType.DMA((2,))]
    )
    final, adj, sens, tot = pl.pallas_call(
        functools.partial(_window_kernel, n_ax, n_az),
        out_shape=(pop, pop, cells, jax.ShapeDtypeStruct((1, n_regions), f32)),
        in_specs=[pl.BlockSpec(memory_space=pltpu.HBM)] * 5,
        out_specs=(pl.BlockSpec(memory_space=vmem),) * 4,
        scratch_shapes=scratch,
        compiler_params=pltpu.CompilerParams(collective_id=1, has_side_effects=True,
                                             vmem_limit_bytes=67043328),
    )(initial, adjoint_seed, porosity, cell_type.reshape((1,) + cell_type.shape), region)
    return final, adj, sens, tot


def shards(initial, adjoint_seed, porosity, cell_type, region):
    n_regions = lax.axis_size("ax") * lax.axis_size("az") // 4
    final, adjoint, sensitivity, totals = window(
        initial, adjoint_seed, porosity, cell_type, region, n_regions)
    totals = totals.reshape(-1)
    return (final, adjoint, sensitivity, totals)


def solution(mesh):
    return jax.shard_map(
        shards,
        mesh=mesh,
        in_specs=(
            P(None, "ax", "az", None),
            P(None, "ax", "az", None),
            P("ax", "az", None),
            P("ax", "az", None),
            P("ax", "az", None),
        ),
        out_specs=(P(None, "ax", "az", None), P(None, "ax", "az", None), P("ax", "az", None), P()),
        check_vma=False,
    )
```

```python
import functools

import numpy as np

import jax
import jax.numpy as jnp
from jax import lax
from jax.experimental import pallas as pl
from jax.experimental.pallas import tpu as pltpu
from jax.sharding import PartitionSpec as P

MESH = pl.DeviceIdType.MESH

VELOCITY = [
    (0, 0, 0),
    (1, 0, 0),
    (-1, 0, 0),
    (0, 1, 0),
    (0, -1, 0),
    (0, 0, 1),
    (0, 0, -1),
    (1, 1, 0),
    (-1, -1, 0),
    (1, -1, 0),
    (-1, 1, 0),
    (1, 0, 1),
    (-1, 0, -1),
    (1, 0, -1),
    (-1, 0, 1),
    (0, 1, 1),
    (0, -1, -1),
    (0, 1, -1),
    (0, -1, 1),
]
OPPOSITE = [0, 2, 1, 4, 3, 6, 5, 8, 7, 10, 9, 12, 11, 14, 13, 16, 15, 18, 17]
WEIGHTS = [1.0 / 3.0] + [1.0 / 18.0] * 6 + [1.0 / 36.0] * 12
INLET_SPEED = (0.05, 0.05, 0.0)
NQ = 19
TILE = 8


def _inflow_constants():
    w = np.array(WEIGHTS, np.float32)
    u = np.array(INLET_SPEED, np.float32)
    c = np.array(VELOCITY, np.float32)
    proj = (c * u[None, :]).sum(1, dtype=np.float32).astype(np.float32)
    usq = np.float32((u * u).sum(dtype=np.float32))
    one = np.float32(1.0)
    val = w * one * (one + np.float32(3.0) * proj + np.float32(4.5) * proj * proj - np.float32(1.5) * usq)
    return [float(v) for v in val.astype(np.float32)]


INFLOW = _inflow_constants()


def _combo(values, coeffs):
    acc = None
    for v, c in zip(values, coeffs):
        if c == 0:
            continue
        term = v if c == 1 else (-v if c == -1 else c * v)
        acc = term if acc is None else acc + term
    return acc


def _equilibrium(rho, u):
    usq = u[0] * u[0] + u[1] * u[1] + u[2] * u[2]
    out = []
    for q in range(NQ):
        p = _combo(u, VELOCITY[q])
        if p is None:
            inner = 1.0 - 1.5 * usq
        else:
            inner = 1.0 + 3.0 * p + 4.5 * p * p - 1.5 * usq
        out.append(WEIGHTS[q] * rho * inner)
    return out


def _collide(f, porous, types, regions, with_grad=False):
    rho = f[0]
    for q in range(1, NQ):
        rho = rho + f[q]
    u = [_combo(f, [VELOCITY[q][k] for q in range(NQ)]) / rho for k in range(3)]
    feq = _equilibrium(rho, u)
    g = [f[q] - feq[q] for q in range(NQ)]
    moments = []
    for a, b in ((0, 0), (1, 1), (2, 2), (0, 1), (0, 2), (1, 2)):
        moments.append(_combo(g, [VELOCITY[q][a] * VELOCITY[q][b] for q in range(NQ)]))
    stress_sq = (
        moments[0] * moments[0]
        + moments[1] * moments[1]
        + moments[2] * moments[2]
        + 2.0 * (moments[3] * moments[3] + moments[4] * moments[4] + moments[5] * moments[5])
    )
    shear = 1.5 * jnp.sqrt(stress_sq + 0.0001) / rho
    viscous = 0.02 * (shear + 0.01) ** (0.7 - 1.0)
    relax = 0.5 + 3.0 * viscous
    design = jnp.where(regions > 0, 1.0, 0.0).astype(jnp.float32)
    damp = porous * design
    outflow = _equilibrium(jnp.ones_like(rho), u)
    inlet = types == 2
    outlet = types == 3
    out = []
    for q in range(NQ):
        relaxed = f[q] - g[q] / relax - damp * (feq[q] - WEIGHTS[q] * rho)
        out.append(jnp.where(inlet, INFLOW[q], jnp.where(outlet, outflow[q], relaxed)))
    if not with_grad:
        return out
    fixed = jnp.logical_or(inlet, outlet)
    grad = [jnp.where(fixed, 0.0, -design * (feq[q] - WEIGHTS[q] * rho)) for q in range(NQ)]
    return out, grad


def _pieces(sign):
    out = []
    for q in range(NQ):
        oa, ot = sign * VELOCITY[q][0], sign * VELOCITY[q][1]
        if oa != 0:
            out.append((q, "a", oa, ot))
        if ot != 0:
            out.append((q, "t", oa, ot))
        if oa != 0 and ot != 0:
            out.append((q, "c", oa, ot))
    return out


FLAG_PIECES = [
    (0, "a", 1, 0),
    (0, "a", -1, 0),
    (0, "t", 0, 1),
    (0, "t", 0, -1),
    (0, "c", 1, 1),
    (0, "c", 1, -1),
    (0, "c", -1, 1),
    (0, "c", -1, -1),
]
NPIECE = 24


class Halo:
    def __init__(self, a_lo, a_hi, t_lo, t_hi):
        self.a_lo, self.a_hi, self.t_lo, self.t_hi = a_lo, a_hi, t_lo, t_hi


def _piece_refs(piece, field, halo, ca, ct):
    q, kind, oa, ot = piece
    a_face = ca - 1 if oa == -1 else 0
    t_face = ct - 1 if ot == -1 else 0
    if kind == "a":
        src = field.at[q, pl.ds(a_face, 1)]
        dst = (halo.a_lo if oa == -1 else halo.a_hi).at[q]
        move = (-oa, 0)
    elif kind == "t":
        src = field.at[q, :, pl.ds(t_face, 1)]
        dst = (halo.t_lo if ot == -1 else halo.t_hi).at[q, pl.ds(1, ca)]
        move = (0, -ot)
    else:
        src = field.at[q, pl.ds(a_face, 1), pl.ds(t_face, 1)]
        slot = 0 if oa == -1 else ca + 1
        dst = (halo.t_lo if ot == -1 else halo.t_hi).at[q, pl.ds(slot, 1)]
        move = (-oa, -ot)
    return src, dst, move


class Exchange:
    def __init__(self, pieces, field, halo, send_sem, recv_sem, pos, sizes, ca, ct):
        self.items = []
        me_ax, me_az = pos
        n_ax, n_az = sizes
        for i, piece in enumerate(pieces):
            src, dst, (da, dt) = _piece_refs(piece, field, halo, ca, ct)
            to_ax = me_ax + da
            from_ax = me_ax - da
            to_dev = (to_ax, lax.rem(me_az + dt + n_az, n_az))
            from_dev = (from_ax, lax.rem(me_az - dt + n_az, n_az))
            send = pltpu.make_async_remote_copy(
                src_ref=src, dst_ref=dst, send_sem=send_sem.at[i], recv_sem=recv_sem.at[i],
                device_id=to_dev, device_id_type=MESH)
            recv = pltpu.make_async_remote_copy(
                src_ref=src, dst_ref=dst, send_sem=send_sem.at[i], recv_sem=recv_sem.at[i],
                device_id=from_dev, device_id_type=MESH)
            send_ok = jnp.logical_and(to_ax >= 0, to_ax < n_ax) if da != 0 else None
            recv_ok = jnp.logical_and(from_ax >= 0, from_ax < n_ax) if da != 0 else None
            self.items.append((send, recv, send_ok, recv_ok))

    @staticmethod
    def _maybe(ok, fn):
        if ok is None:
            fn()
        else:
            pl.when(ok)(fn)

    def start(self):
        for send, _, ok, _ in self.items:
            self._maybe(ok, send.start)

    def wait_recv(self):
        for _, recv, _, ok in self.items:
            self._maybe(ok, recv.wait_recv)

    def wait_send(self):
        for send, _, ok, _ in self.items:
            self._maybe(ok, send.wait_send)


def _shift(own, halo, q, a, oa, ot, orr, lo_ok, hi_ok, ca, ct, nr, zero_r):
    ae = a + oa
    ok = None
    if ae < 0:
        slab = halo.a_lo[q, 0]
        ok = lo_ok
    elif ae >= ca:
        slab = halo.a_hi[q, 0]
        ok = hi_ok
    else:
        slab = own[q, ae]
    if ot != 0:
        rows = lax.broadcasted_iota(jnp.int32, (ct, nr), 0)
        if ot == -1:
            edge = halo.t_lo[q, ae + 1]
            slab = jnp.where(rows == 0, edge, pltpu.roll(slab, 1, 0))
        else:
            edge = halo.t_hi[q, ae + 1]
            slab = jnp.where(rows == ct - 1, edge, pltpu.roll(slab, ct - 1, 0))
    if orr != 0:
        lanes = lax.broadcasted_iota(jnp.int32, (ct, nr), 1)
        if orr == -1:
            slab = jnp.where(lanes == 0, zero_r, pltpu.roll(slab, 1, 1))
        else:
            slab = jnp.where(lanes == nr - 1, zero_r, pltpu.roll(slab, nr - 1, 1))
    if ok is not None:
        slab = jnp.where(ok, slab, zero_r)
    return slab


def _window_kernel(
    n_ax, n_az,
    init_hbm, seed_hbm, por_hbm, type_hbm, reg_hbm,
    final_ref, adj_ref, sens_ref, tot_ref,
    init_ref, seed_ref, por_ref, type_ref, reg_ref, load_sem,
    post0, state1, back1, post1, adj1, back0, gpor, fmask, sens1,
    pop_a_lo, pop_a_hi, pop_t_lo, pop_t_hi,
    ty_a_lo, ty_a_hi, ty_t_lo, ty_t_hi,
    send_sem, recv_sem, ty_send, ty_recv,
    part_ref, row_a, row_b, send_a, recv_a, send_b, recv_b, local,
):
    loads = [
        pltpu.make_async_copy(src, dst, load_sem.at[i])
        for i, (src, dst) in enumerate(
            ((type_hbm, type_ref), (seed_hbm, seed_ref), (init_hbm, init_ref),
             (por_hbm, por_ref), (reg_hbm, reg_ref)))
    ]
    for copy in loads:
        copy.start()
    _, ca, ct, nr = init_ref.shape
    me_ax, me_az = lax.axis_index("ax"), lax.axis_index("az")
    lo_ok = me_ax > 0
    hi_ok = me_ax < n_ax - 1
    pos, sizes = (me_ax, me_az), (n_ax, n_az)

    barrier = pltpu.get_barrier_semaphore()
    up_az, dn_az = lax.rem(me_az + 1, n_az), lax.rem(me_az + n_az - 1, n_az)
    for k in range(1, n_az):
        pl.semaphore_signal(barrier, 1, device_id=(me_ax, lax.rem(me_az + k, n_az)), device_id_type=MESH)
    for k in range(1, n_ax):
        pl.semaphore_signal(barrier, 1, device_id=(lax.rem(me_ax + k, n_ax), me_az), device_id_type=MESH)
    for ok, other in ((lo_ok, me_ax - 1), (hi_ok, me_ax + 1)):
        @pl.when(ok)
        def _():
            for dz in (up_az, dn_az):
                pl.semaphore_signal(barrier, 1, device_id=(other, dz), device_id_type=MESH)
    count = (n_az - 1) + (n_ax - 1) + 2 * (lo_ok.astype(jnp.int32) + hi_ok.astype(jnp.int32))
    for copy in loads:
        copy.wait()

    def halo(k):
        return Halo(pop_a_lo.at[k], pop_a_hi.at[k], pop_t_lo.at[k], pop_t_hi.at[k])

    ty_halo = Halo(ty_a_lo, ty_a_hi, ty_t_lo, ty_t_hi)
    ex_types = Exchange(FLAG_PIECES, type_ref, ty_halo, ty_send, ty_recv, pos, sizes, ca, ct)
    ex_seed = Exchange(_pieces(1), seed_ref, halo(0), send_sem.at[0], recv_sem.at[0], pos, sizes, ca, ct)

    steps = ca * (ct // TILE)

    def tile_at(i):
        a = i // (ct // TILE)
        t0 = pl.multiple_of((i % (ct // TILE)) * TILE, TILE)
        return a, pl.ds(t0, TILE)

    def load(ref, a, ts):
        return [ref[q, a, ts, :] for q in range(NQ)]

    def store(ref, a, ts, vals):
        for q in range(NQ):
            ref[q, a, ts, :] = vals[q]

    def collide_loop(src, dst, grad_dst):
        def body(i, carry):
            a, ts = tile_at(i)
            out, grad = _collide(load(src, a, ts), por_ref[a, ts, :], type_ref[0, a, ts, :],
                                 reg_ref[a, ts, :], with_grad=True)
            store(dst, a, ts, out)
            store(grad_dst, a, ts, grad)
            return carry
        lax.fori_loop(0, steps, body, 0)

    def vjp_loop(at, upstream, primal_dst, grad_dst, sens_dst):
        def body(i, carry):
            a, ts = tile_at(i)
            types = type_ref[0, a, ts, :]
            regions = reg_ref[a, ts, :]
            out, pullback = jax.vjp(
                lambda f, p: _collide(f, p, types, regions), load(at, a, ts), por_ref[a, ts, :])
            if primal_dst is not None:
                store(primal_dst, a, ts, out)
            d_f, d_p = pullback(load(upstream, a, ts))
            store(grad_dst, a, ts, d_f)
            if sens_dst is not None:
                sens_dst[a, ts, :] = d_p
            return carry
        lax.fori_loop(0, steps, body, 0)

    zero = jnp.zeros((ct, nr), jnp.float32)

    def flag_shift(a, oa, ot, orr):
        if oa == 0 and ot == 0 and orr == 0:
            own = type_ref[0, a]
            return jnp.where(own != 1, 1.0, 0.0).astype(jnp.float32)
        ty = _shift(type_ref, ty_halo, 0, a, oa, ot, orr, lo_ok, hi_ok, ca, ct, nr, jnp.ones((ct, nr), jnp.int32))
        return jnp.where(ty != 1, 1.0, 0.0).astype(jnp.float32)

    def fill_masks():
        for a in range(ca):
            for q in range(NQ):
                c = VELOCITY[q]
                fmask[q, a] = flag_shift(a, -c[0], -c[1], -c[2])

    def stream(post, hal, dst):
        for a in range(ca):
            for q in range(NQ):
                c = VELOCITY[q]
                moved = _shift(post, hal, q, a, -c[0], -c[1], -c[2], lo_ok, hi_ok, ca, ct, nr, zero)
                ok = fmask[q, a] > 0
                dst[q, a] = jnp.where(ok, moved, post[OPPOSITE[q], a])

    def stream_adjoint(adj, hal, dst):
        for a in range(ca):
            centre = fmask[0, a]
            for q in range(NQ):
                c = VELOCITY[q]
                ahead = _shift(adj, hal, q, a, c[0], c[1], c[2], lo_ok, hi_ok, ca, ct, nr, zero)
                blocked = 1.0 - fmask[OPPOSITE[q], a]
                dst[q, a] = centre * ahead + blocked * adj[OPPOSITE[q], a]

    collide_loop(init_ref, post0, gpor)
    pl.semaphore_wait(barrier, count)
    ex_post0 = Exchange(_pieces(-1), post0, halo(1), send_sem.at[1], recv_sem.at[1], pos, sizes, ca, ct)
    ex_types.start()
    ex_seed.start()
    ex_post0.start()
    ex_types.wait_recv()
    fill_masks()
    ex_seed.wait_recv()
    stream_adjoint(seed_ref, halo(0), back1)
    ex_post0.wait_recv()
    stream(post0, halo(1), state1)
    vjp_loop(state1, back1, post1, adj1, sens1)
    ex_post1 = Exchange(_pieces(-1), post1, halo(2), send_sem.at[2], recv_sem.at[2], pos, sizes, ca, ct)
    ex_adj1 = Exchange(_pieces(1), adj1, halo(3), send_sem.at[3], recv_sem.at[3], pos, sizes, ca, ct)
    ex_adj1.start()
    ex_post1.start()
    ex_adj1.wait_recv()
    stream_adjoint(adj1, halo(3), back0)
    for a in range(ca):
        sens0 = back0[0, a] * gpor[0, a]
        for q in range(1, NQ):
            sens0 = sens0 + back0[q, a] * gpor[q, a]
        sens_ref[a] = sens1[a] + sens0

    total = jnp.zeros((1, 1), jnp.float32)
    rid = jnp.zeros((1, 1), jnp.int32)
    for a in range(ca):
        reg = reg_ref[a]
        total = total + jnp.sum(jnp.where(reg > 0, sens_ref[a], 0.0), keepdims=True)
        rid = jnp.maximum(rid, jnp.max(reg, keepdims=True))
    labels = lax.broadcasted_iota(jnp.int32, part_ref.shape, 1) + 1
    part_ref[...] = jnp.where(labels == rid, total, 0.0)
    first = _TotalsStage(part_ref, row_a, send_a, recv_a, local.at[0], me_az, n_az,
                         lambda j: (me_ax, j))
    first.start()

    vjp_loop(init_ref, back0, None, adj_ref, None)

    first.finish(part_ref)
    own = pltpu.make_async_copy(part_ref, row_b.at[me_ax], local.at[1])
    own.start()
    own.wait()
    second = _TotalsStage(row_b.at[me_ax], row_b, send_b, recv_b, None, me_ax, n_ax,
                          lambda j: (j, me_az))
    second.start()
    ex_post1.wait_recv()
    stream(post1, halo(2), final_ref)
    second.finish(tot_ref)

    for ex in (ex_types, ex_seed, ex_post0, ex_post1, ex_adj1):
        ex.wait_send()


class _TotalsStage:
    def __init__(self, src, rows, send, recv, own_sem, me, n, device):
        self.src, self.rows, self.own_sem, self.me, self.n = src, rows, own_sem, me, n
        self.sends, self.recvs = [], []
        for k in range(1, n):
            to, frm = lax.rem(me + k, n), lax.rem(me + n - k, n)
            self.sends.append(pltpu.make_async_remote_copy(
                src_ref=src, dst_ref=rows.at[me], send_sem=send.at[k], recv_sem=recv.at[me],
                device_id=device(to), device_id_type=MESH))
            self.recvs.append(pltpu.make_async_remote_copy(
                src_ref=src, dst_ref=rows.at[frm], send_sem=send.at[k], recv_sem=recv.at[frm],
                device_id=device(frm), device_id_type=MESH))

    def start(self):
        self.own = None
        if self.own_sem is not None:
            self.own = pltpu.make_async_copy(self.src, self.rows.at[self.me], self.own_sem)
            self.own.start()
        for copy in self.sends:
            copy.start()

    def finish(self, out):
        if self.own is not None:
            self.own.wait()
        for copy in self.recvs:
            copy.wait_recv()
        acc = self.rows[0]
        for j in range(1, self.n):
            acc = acc + self.rows[j]
        for copy in self.sends:
            copy.wait_send()
        out[...] = acc


def window(initial, adjoint_seed, porosity, cell_type, region, n_regions):
    n_ax, n_az = lax.axis_size("ax"), lax.axis_size("az")
    nq, ca, ct, nr = initial.shape
    pop = jax.ShapeDtypeStruct(initial.shape, jnp.float32)
    cells = jax.ShapeDtypeStruct(porosity.shape, jnp.float32)
    vmem = pltpu.VMEM
    f32, i32 = jnp.float32, jnp.int32
    scratch = (
        [vmem(initial.shape, f32), vmem(initial.shape, f32), vmem(porosity.shape, f32),
         vmem((1,) + cell_type.shape, i32), vmem(region.shape, i32), pltpu.SemaphoreType.DMA((5,))]

        + [vmem((nq, ca, ct, nr), f32) for _ in range(8)]
        + [vmem((ca, ct, nr), f32)]
        + [vmem((4, nq, 1, ct, nr), f32), vmem((4, nq, 1, ct, nr), f32),
           vmem((4, nq, ca + 2, 1, nr), f32), vmem((4, nq, ca + 2, 1, nr), f32)]
        + [vmem((1, 1, ct, nr), i32), vmem((1, 1, ct, nr), i32),
           vmem((1, ca + 2, 1, nr), i32), vmem((1, ca + 2, 1, nr), i32)]
        + [pltpu.SemaphoreType.DMA((4, NPIECE)), pltpu.SemaphoreType.DMA((4, NPIECE)),
           pltpu.SemaphoreType.DMA((len(FLAG_PIECES),)), pltpu.SemaphoreType.DMA((len(FLAG_PIECES),))]
        + [vmem((1, n_regions), f32), vmem((n_az, 1, n_regions), f32), vmem((n_ax, 1, n_regions), f32),
           pltpu.SemaphoreType.DMA((n_az,)), pltpu.SemaphoreType.DMA((n_az,)),
           pltpu.SemaphoreType.DMA((n_ax,)), pltpu.SemaphoreType.DMA((n_ax,)),
           pltpu.SemaphoreType.DMA((2,))]
    )
    final, adj, sens, tot = pl.pallas_call(
        functools.partial(_window_kernel, n_ax, n_az),
        out_shape=(pop, pop, cells, jax.ShapeDtypeStruct((1, n_regions), f32)),
        in_specs=[pl.BlockSpec(memory_space=pltpu.HBM)] * 5,
        out_specs=(pl.BlockSpec(memory_space=vmem),) * 4,
        scratch_shapes=scratch,
        compiler_params=pltpu.CompilerParams(collective_id=1, has_side_effects=True,
                                             vmem_limit_bytes=67043328),
    )(initial, adjoint_seed, porosity, cell_type.reshape((1,) + cell_type.shape), region)
    return final, adj, sens, tot


def shards(initial, adjoint_seed, porosity, cell_type, region):
    n_regions = lax.axis_size("ax") * lax.axis_size("az") // 4
    final, adjoint, sensitivity, totals = window(
        initial, adjoint_seed, porosity, cell_type, region, n_regions)
    totals = totals.reshape(-1)
    return (final, adjoint, sensitivity, totals)


def solution(mesh):
    return jax.shard_map(
        shards,
        mesh=mesh,
        in_specs=(
            P(None, "ax", "az", None),
            P(None, "ax", "az", None),
            P("ax", "az", None),
            P("ax", "az", None),
            P("ax", "az", None),
        ),
        out_specs=(P(None, "ax", "az", None), P(None, "ax", "az", None), P("ax", "az", None), P()),
        check_vma=False,
    )
```

```python
import functools

import numpy as np

import jax
import jax.numpy as jnp
from jax import lax
from jax.experimental import pallas as pl
from jax.experimental.pallas import tpu as pltpu
from jax.sharding import PartitionSpec as P

MESH = pl.DeviceIdType.MESH

VELOCITY = [
    (0, 0, 0),
    (1, 0, 0),
    (-1, 0, 0),
    (0, 1, 0),
    (0, -1, 0),
    (0, 0, 1),
    (0, 0, -1),
    (1, 1, 0),
    (-1, -1, 0),
    (1, -1, 0),
    (-1, 1, 0),
    (1, 0, 1),
    (-1, 0, -1),
    (1, 0, -1),
    (-1, 0, 1),
    (0, 1, 1),
    (0, -1, -1),
    (0, 1, -1),
    (0, -1, 1),
]
OPPOSITE = [0, 2, 1, 4, 3, 6, 5, 8, 7, 10, 9, 12, 11, 14, 13, 16, 15, 18, 17]
WEIGHTS = [1.0 / 3.0] + [1.0 / 18.0] * 6 + [1.0 / 36.0] * 12
INLET_SPEED = (0.05, 0.05, 0.0)
NQ = 19
TILE = 8
LANES = 128


def _inflow_constants():
    w = np.array(WEIGHTS, np.float32)
    u = np.array(INLET_SPEED, np.float32)
    c = np.array(VELOCITY, np.float32)
    proj = (c * u[None, :]).sum(1, dtype=np.float32).astype(np.float32)
    usq = np.float32((u * u).sum(dtype=np.float32))
    one = np.float32(1.0)
    val = w * one * (one + np.float32(3.0) * proj + np.float32(4.5) * proj * proj - np.float32(1.5) * usq)
    return [float(v) for v in val.astype(np.float32)]


INFLOW = _inflow_constants()


def _combo(values, coeffs):
    acc = None
    for v, c in zip(values, coeffs):
        if c == 0:
            continue
        term = v if c == 1 else (-v if c == -1 else c * v)
        acc = term if acc is None else acc + term
    return acc


def _equilibrium(rho, u):
    usq = u[0] * u[0] + u[1] * u[1] + u[2] * u[2]
    out = []
    for q in range(NQ):
        p = _combo(u, VELOCITY[q])
        if p is None:
            inner = 1.0 - 1.5 * usq
        else:
            inner = 1.0 + 3.0 * p + 4.5 * p * p - 1.5 * usq
        out.append(WEIGHTS[q] * rho * inner)
    return out


def _collide(f, porous, types, regions, with_grad=False):
    rho = f[0]
    for q in range(1, NQ):
        rho = rho + f[q]
    u = [_combo(f, [VELOCITY[q][k] for q in range(NQ)]) / rho for k in range(3)]
    feq = _equilibrium(rho, u)
    g = [f[q] - feq[q] for q in range(NQ)]
    moments = []
    for a, b in ((0, 0), (1, 1), (2, 2), (0, 1), (0, 2), (1, 2)):
        moments.append(_combo(g, [VELOCITY[q][a] * VELOCITY[q][b] for q in range(NQ)]))
    stress_sq = (
        moments[0] * moments[0]
        + moments[1] * moments[1]
        + moments[2] * moments[2]
        + 2.0 * (moments[3] * moments[3] + moments[4] * moments[4] + moments[5] * moments[5])
    )
    shear = 1.5 * jnp.sqrt(stress_sq + 0.0001) / rho
    viscous = 0.02 * (shear + 0.01) ** (0.7 - 1.0)
    relax = 0.5 + 3.0 * viscous
    design = jnp.where(regions > 0, 1.0, 0.0).astype(jnp.float32)
    damp = porous * design
    outflow = _equilibrium(jnp.ones_like(rho), u)
    inlet = types == 2
    outlet = types == 3
    out = []
    for q in range(NQ):
        relaxed = f[q] - g[q] / relax - damp * (feq[q] - WEIGHTS[q] * rho)
        out.append(jnp.where(inlet, INFLOW[q], jnp.where(outlet, outflow[q], relaxed)))
    if not with_grad:
        return out
    fixed = jnp.logical_or(inlet, outlet)
    grad = [jnp.where(fixed, 0.0, -design * (feq[q] - WEIGHTS[q] * rho)) for q in range(NQ)]
    return out, grad


def _pieces(sign):
    out = []
    for q in range(NQ):
        oa, ot = sign * VELOCITY[q][0], sign * VELOCITY[q][1]
        if oa != 0:
            out.append((q, "a", oa, ot))
        if ot != 0:
            out.append((q, "t", oa, ot))
        if oa != 0 and ot != 0:
            out.append((q, "c", oa, ot))
    return out


FLAG_PIECES = [
    (0, "a", 1, 0),
    (0, "a", -1, 0),
    (0, "t", 0, 1),
    (0, "t", 0, -1),
    (0, "c", 1, 1),
    (0, "c", 1, -1),
    (0, "c", -1, 1),
    (0, "c", -1, -1),
]
NPIECE = 24


class Halo:
    def __init__(self, a_lo, a_hi, t_lo, t_hi):
        self.a_lo, self.a_hi, self.t_lo, self.t_hi = a_lo, a_hi, t_lo, t_hi


def _piece_refs(piece, field, halo, ca, ct):
    q, kind, oa, ot = piece
    a_face = ca - 1 if oa == -1 else 0
    t_face = ct - 1 if ot == -1 else 0
    if kind == "a":
        src = field.at[q, pl.ds(a_face, 1)]
        dst = (halo.a_lo if oa == -1 else halo.a_hi).at[q]
        move = (-oa, 0)
    elif kind == "t":
        src = field.at[q, :, pl.ds(t_face, 1)]
        dst = (halo.t_lo if ot == -1 else halo.t_hi).at[q, pl.ds(1, ca)]
        move = (0, -ot)
    else:
        src = field.at[q, pl.ds(a_face, 1), pl.ds(t_face, 1)]
        slot = 0 if oa == -1 else ca + 1
        dst = (halo.t_lo if ot == -1 else halo.t_hi).at[q, pl.ds(slot, 1)]
        move = (-oa, -ot)
    return src, dst, move


class Exchange:
    def __init__(self, pieces, field, halo, send_sem, recv_sem, pos, sizes, ca, ct):
        self.items = []
        me_ax, me_az = pos
        n_ax, n_az = sizes
        for i, piece in enumerate(pieces):
            src, dst, (da, dt) = _piece_refs(piece, field, halo, ca, ct)
            to_ax = me_ax + da
            from_ax = me_ax - da
            to_dev = (to_ax, lax.rem(me_az + dt + n_az, n_az))
            from_dev = (from_ax, lax.rem(me_az - dt + n_az, n_az))
            send = pltpu.make_async_remote_copy(
                src_ref=src, dst_ref=dst, send_sem=send_sem.at[i], recv_sem=recv_sem.at[i],
                device_id=to_dev, device_id_type=MESH)
            recv = pltpu.make_async_remote_copy(
                src_ref=src, dst_ref=dst, send_sem=send_sem.at[i], recv_sem=recv_sem.at[i],
                device_id=from_dev, device_id_type=MESH)
            send_ok = jnp.logical_and(to_ax >= 0, to_ax < n_ax) if da != 0 else None
            recv_ok = jnp.logical_and(from_ax >= 0, from_ax < n_ax) if da != 0 else None
            self.items.append((send, recv, send_ok, recv_ok))

    @staticmethod
    def _maybe(ok, fn):
        if ok is None:
            fn()
        else:
            pl.when(ok)(fn)

    def start(self):
        for send, _, ok, _ in self.items:
            self._maybe(ok, send.start)

    def wait_recv(self):
        for _, recv, _, ok in self.items:
            self._maybe(ok, recv.wait_recv)

    def wait_send(self):
        for send, _, ok, _ in self.items:
            self._maybe(ok, send.wait_send)


def _shift(own, halo, q, a, oa, ot, orr, lo_ok, hi_ok, ca, ct, nr, zero_r):
    ae = a + oa
    ok = None
    if ae < 0:
        slab = halo.a_lo[q, 0]
        ok = lo_ok
    elif ae >= ca:
        slab = halo.a_hi[q, 0]
        ok = hi_ok
    else:
        slab = own[q, ae]
    if ot != 0:
        rows = lax.broadcasted_iota(jnp.int32, (ct, nr), 0)
        if ot == -1:
            edge = halo.t_lo[q, ae + 1]
            slab = jnp.where(rows == 0, edge, pltpu.roll(slab, 1, 0))
        else:
            edge = halo.t_hi[q, ae + 1]
            slab = jnp.where(rows == ct - 1, edge, pltpu.roll(slab, ct - 1, 0))
    if orr != 0:
        lanes = lax.broadcasted_iota(jnp.int32, (ct, nr), 1)
        if orr == -1:
            slab = jnp.where(lanes == 0, zero_r, pltpu.roll(slab, 1, 1))
        else:
            slab = jnp.where(lanes == nr - 1, zero_r, pltpu.roll(slab, nr - 1, 1))
    if ok is not None:
        slab = jnp.where(ok, slab, zero_r)
    return slab


def _window_kernel(
    n_ax, n_az,
    init_hbm, seed_hbm, por_hbm, type_hbm, reg_hbm,
    final_ref, adj_ref, sens_ref, tot_ref,
    init_ref, seed_ref, por_ref, type_ref, reg_ref, load_sem,
    post0, state1, back1, post1, adj1, back0, gpor, fmask, sens1,
    pop_a_lo, pop_a_hi, pop_t_lo, pop_t_hi,
    ty_a_lo, ty_a_hi, ty_t_lo, ty_t_hi,
    send_sem, recv_sem, ty_send, ty_recv,
    part_ref, row_a, row_b, send_a, recv_a, send_b, recv_b, local,
):
    loads = [
        pltpu.make_async_copy(src, dst, load_sem.at[i])
        for i, (src, dst) in enumerate(
            ((type_hbm, type_ref), (seed_hbm, seed_ref), (init_hbm, init_ref),
             (por_hbm, por_ref), (reg_hbm, reg_ref)))
    ]
    for copy in loads:
        copy.start()
    _, ca, ct, nr = init_ref.shape
    me_ax, me_az = lax.axis_index("ax"), lax.axis_index("az")
    lo_ok = me_ax > 0
    hi_ok = me_ax < n_ax - 1
    pos, sizes = (me_ax, me_az), (n_ax, n_az)

    barrier = pltpu.get_barrier_semaphore()
    up_az, dn_az = lax.rem(me_az + 1, n_az), lax.rem(me_az + n_az - 1, n_az)
    for k in range(1, n_az):
        pl.semaphore_signal(barrier, 1, device_id=(me_ax, lax.rem(me_az + k, n_az)), device_id_type=MESH)
    for k in range(1, n_ax):
        pl.semaphore_signal(barrier, 1, device_id=(lax.rem(me_ax + k, n_ax), me_az), device_id_type=MESH)
    for ok, other in ((lo_ok, me_ax - 1), (hi_ok, me_ax + 1)):
        @pl.when(ok)
        def _():
            for dz in (up_az, dn_az):
                pl.semaphore_signal(barrier, 1, device_id=(other, dz), device_id_type=MESH)
    count = (n_az - 1) + (n_ax - 1) + 2 * (lo_ok.astype(jnp.int32) + hi_ok.astype(jnp.int32))
    for copy in loads:
        copy.wait()

    def halo(k):
        return Halo(pop_a_lo.at[k], pop_a_hi.at[k], pop_t_lo.at[k], pop_t_hi.at[k])

    ty_halo = Halo(ty_a_lo, ty_a_hi, ty_t_lo, ty_t_hi)
    ex_types = Exchange(FLAG_PIECES, type_ref, ty_halo, ty_send, ty_recv, pos, sizes, ca, ct)
    ex_seed = Exchange(_pieces(1), seed_ref, halo(0), send_sem.at[0], recv_sem.at[0], pos, sizes, ca, ct)

    n_t, n_l = ct // TILE, nr // LANES
    steps = ca * n_t * n_l

    def tile_at(i):
        a = i // (n_t * n_l)
        t0 = pl.multiple_of(((i // n_l) % n_t) * TILE, TILE)
        l0 = pl.multiple_of((i % n_l) * LANES, LANES)
        return a, (pl.ds(t0, TILE), pl.ds(l0, LANES))

    def load(ref, a, ts):
        return [ref[q, a, ts[0], ts[1]] for q in range(NQ)]

    def store(ref, a, ts, vals):
        for q in range(NQ):
            ref[q, a, ts[0], ts[1]] = vals[q]

    def collide_loop(src, dst, grad_dst):
        def body(i, carry):
            a, ts = tile_at(i)
            out, grad = _collide(load(src, a, ts), por_ref[a, ts[0], ts[1]], type_ref[0, a, ts[0], ts[1]],
                                 reg_ref[a, ts[0], ts[1]], with_grad=True)
            store(dst, a, ts, out)
            store(grad_dst, a, ts, grad)
            return carry
        lax.fori_loop(0, steps, body, 0)

    def vjp_loop(at, upstream, primal_dst, grad_dst, sens_dst):
        def body(i, carry):
            a, ts = tile_at(i)
            types = type_ref[0, a, ts[0], ts[1]]
            regions = reg_ref[a, ts[0], ts[1]]
            out, pullback = jax.vjp(
                lambda f, p: _collide(f, p, types, regions), load(at, a, ts), por_ref[a, ts[0], ts[1]])
            if primal_dst is not None:
                store(primal_dst, a, ts, out)
            d_f, d_p = pullback(load(upstream, a, ts))
            store(grad_dst, a, ts, d_f)
            if sens_dst is not None:
                sens_dst[a, ts[0], ts[1]] = d_p
            return carry
        lax.fori_loop(0, steps, body, 0)

    zero = jnp.zeros((ct, nr), jnp.float32)

    def flag_shift(a, oa, ot, orr):
        if oa == 0 and ot == 0 and orr == 0:
            own = type_ref[0, a]
            return jnp.where(own != 1, 1.0, 0.0).astype(jnp.float32)
        ty = _shift(type_ref, ty_halo, 0, a, oa, ot, orr, lo_ok, hi_ok, ca, ct, nr, jnp.ones((ct, nr), jnp.int32))
        return jnp.where(ty != 1, 1.0, 0.0).astype(jnp.float32)

    def fill_masks():
        for a in range(ca):
            for q in range(NQ):
                c = VELOCITY[q]
                fmask[q, a] = flag_shift(a, -c[0], -c[1], -c[2])

    def stream(post, hal, dst):
        for a in range(ca):
            for q in range(NQ):
                c = VELOCITY[q]
                moved = _shift(post, hal, q, a, -c[0], -c[1], -c[2], lo_ok, hi_ok, ca, ct, nr, zero)
                ok = fmask[q, a] > 0
                dst[q, a] = jnp.where(ok, moved, post[OPPOSITE[q], a])

    def stream_adjoint(adj, hal, dst):
        for a in range(ca):
            centre = fmask[0, a]
            for q in range(NQ):
                c = VELOCITY[q]
                ahead = _shift(adj, hal, q, a, c[0], c[1], c[2], lo_ok, hi_ok, ca, ct, nr, zero)
                blocked = 1.0 - fmask[OPPOSITE[q], a]
                dst[q, a] = centre * ahead + blocked * adj[OPPOSITE[q], a]

    collide_loop(init_ref, post0, gpor)
    pl.semaphore_wait(barrier, count)
    ex_post0 = Exchange(_pieces(-1), post0, halo(1), send_sem.at[1], recv_sem.at[1], pos, sizes, ca, ct)
    ex_types.start()
    ex_seed.start()
    ex_post0.start()
    ex_types.wait_recv()
    fill_masks()
    ex_seed.wait_recv()
    stream_adjoint(seed_ref, halo(0), back1)
    ex_post0.wait_recv()
    stream(post0, halo(1), state1)
    vjp_loop(state1, back1, post1, adj1, sens1)
    ex_post1 = Exchange(_pieces(-1), post1, halo(2), send_sem.at[2], recv_sem.at[2], pos, sizes, ca, ct)
    ex_adj1 = Exchange(_pieces(1), adj1, halo(3), send_sem.at[3], recv_sem.at[3], pos, sizes, ca, ct)
    ex_adj1.start()
    ex_post1.start()
    ex_adj1.wait_recv()
    stream_adjoint(adj1, halo(3), back0)
    for a in range(ca):
        sens0 = back0[0, a] * gpor[0, a]
        for q in range(1, NQ):
            sens0 = sens0 + back0[q, a] * gpor[q, a]
        sens_ref[a] = sens1[a] + sens0

    total = jnp.zeros((1, 1), jnp.float32)
    rid = jnp.zeros((1, 1), jnp.int32)
    for a in range(ca):
        reg = reg_ref[a]
        total = total + jnp.sum(jnp.where(reg > 0, sens_ref[a], 0.0), keepdims=True)
        rid = jnp.maximum(rid, jnp.max(reg, keepdims=True))
    labels = lax.broadcasted_iota(jnp.int32, part_ref.shape, 1) + 1
    part_ref[...] = jnp.where(labels == rid, total, 0.0)
    first = _TotalsStage(part_ref, row_a, send_a, recv_a, local.at[0], me_az, n_az,
                         lambda j: (me_ax, j))
    first.start()

    vjp_loop(init_ref, back0, None, adj_ref, None)

    first.finish(part_ref)
    own = pltpu.make_async_copy(part_ref, row_b.at[me_ax], local.at[1])
    own.start()
    own.wait()
    second = _TotalsStage(row_b.at[me_ax], row_b, send_b, recv_b, None, me_ax, n_ax,
                          lambda j: (j, me_az))
    second.start()
    ex_post1.wait_recv()
    stream(post1, halo(2), final_ref)
    second.finish(tot_ref)

    for ex in (ex_types, ex_seed, ex_post0, ex_post1, ex_adj1):
        ex.wait_send()


class _TotalsStage:
    def __init__(self, src, rows, send, recv, own_sem, me, n, device):
        self.src, self.rows, self.own_sem, self.me, self.n = src, rows, own_sem, me, n
        self.sends, self.recvs = [], []
        for k in range(1, n):
            to, frm = lax.rem(me + k, n), lax.rem(me + n - k, n)
            self.sends.append(pltpu.make_async_remote_copy(
                src_ref=src, dst_ref=rows.at[me], send_sem=send.at[k], recv_sem=recv.at[me],
                device_id=device(to), device_id_type=MESH))
            self.recvs.append(pltpu.make_async_remote_copy(
                src_ref=src, dst_ref=rows.at[frm], send_sem=send.at[k], recv_sem=recv.at[frm],
                device_id=device(frm), device_id_type=MESH))

    def start(self):
        self.own = None
        if self.own_sem is not None:
            self.own = pltpu.make_async_copy(self.src, self.rows.at[self.me], self.own_sem)
            self.own.start()
        for copy in self.sends:
            copy.start()

    def finish(self, out):
        if self.own is not None:
            self.own.wait()
        for copy in self.recvs:
            copy.wait_recv()
        acc = self.rows[0]
        for j in range(1, self.n):
            acc = acc + self.rows[j]
        for copy in self.sends:
            copy.wait_send()
        out[...] = acc


def window(initial, adjoint_seed, porosity, cell_type, region, n_regions):
    n_ax, n_az = lax.axis_size("ax"), lax.axis_size("az")
    nq, ca, ct, nr = initial.shape
    pop = jax.ShapeDtypeStruct(initial.shape, jnp.float32)
    cells = jax.ShapeDtypeStruct(porosity.shape, jnp.float32)
    vmem = pltpu.VMEM
    f32, i32 = jnp.float32, jnp.int32
    scratch = (
        [vmem(initial.shape, f32), vmem(initial.shape, f32), vmem(porosity.shape, f32),
         vmem((1,) + cell_type.shape, i32), vmem(region.shape, i32), pltpu.SemaphoreType.DMA((5,))]

        + [vmem((nq, ca, ct, nr), f32) for _ in range(8)]
        + [vmem((ca, ct, nr), f32)]
        + [vmem((4, nq, 1, ct, nr), f32), vmem((4, nq, 1, ct, nr), f32),
           vmem((4, nq, ca + 2, 1, nr), f32), vmem((4, nq, ca + 2, 1, nr), f32)]
        + [vmem((1, 1, ct, nr), i32), vmem((1, 1, ct, nr), i32),
           vmem((1, ca + 2, 1, nr), i32), vmem((1, ca + 2, 1, nr), i32)]
        + [pltpu.SemaphoreType.DMA((4, NPIECE)), pltpu.SemaphoreType.DMA((4, NPIECE)),
           pltpu.SemaphoreType.DMA((len(FLAG_PIECES),)), pltpu.SemaphoreType.DMA((len(FLAG_PIECES),))]
        + [vmem((1, n_regions), f32), vmem((n_az, 1, n_regions), f32), vmem((n_ax, 1, n_regions), f32),
           pltpu.SemaphoreType.DMA((n_az,)), pltpu.SemaphoreType.DMA((n_az,)),
           pltpu.SemaphoreType.DMA((n_ax,)), pltpu.SemaphoreType.DMA((n_ax,)),
           pltpu.SemaphoreType.DMA((2,))]
    )
    final, adj, sens, tot = pl.pallas_call(
        functools.partial(_window_kernel, n_ax, n_az),
        out_shape=(pop, pop, cells, jax.ShapeDtypeStruct((1, n_regions), f32)),
        in_specs=[pl.BlockSpec(memory_space=pltpu.HBM)] * 5,
        out_specs=(pl.BlockSpec(memory_space=vmem),) * 4,
        scratch_shapes=scratch,
        compiler_params=pltpu.CompilerParams(collective_id=1, has_side_effects=True,
                                             vmem_limit_bytes=67043328),
    )(initial, adjoint_seed, porosity, cell_type.reshape((1,) + cell_type.shape), region)
    return final, adj, sens, tot


def shards(initial, adjoint_seed, porosity, cell_type, region):
    n_regions = lax.axis_size("ax") * lax.axis_size("az") // 4
    final, adjoint, sensitivity, totals = window(
        initial, adjoint_seed, porosity, cell_type, region, n_regions)
    totals = totals.reshape(-1)
    return (final, adjoint, sensitivity, totals)


def solution(mesh):
    return jax.shard_map(
        shards,
        mesh=mesh,
        in_specs=(
            P(None, "ax", "az", None),
            P(None, "ax", "az", None),
            P("ax", "az", None),
            P("ax", "az", None),
            P("ax", "az", None),
        ),
        out_specs=(P(None, "ax", "az", None), P(None, "ax", "az", None), P("ax", "az", None), P()),
        check_vma=False,
    )
```

```python
import functools

import numpy as np

import jax
import jax.numpy as jnp
from jax import lax
from jax.experimental import pallas as pl
from jax.experimental.pallas import tpu as pltpu
from jax.sharding import PartitionSpec as P

MESH = pl.DeviceIdType.MESH

VELOCITY = [
    (0, 0, 0),
    (1, 0, 0),
    (-1, 0, 0),
    (0, 1, 0),
    (0, -1, 0),
    (0, 0, 1),
    (0, 0, -1),
    (1, 1, 0),
    (-1, -1, 0),
    (1, -1, 0),
    (-1, 1, 0),
    (1, 0, 1),
    (-1, 0, -1),
    (1, 0, -1),
    (-1, 0, 1),
    (0, 1, 1),
    (0, -1, -1),
    (0, 1, -1),
    (0, -1, 1),
]
OPPOSITE = [0, 2, 1, 4, 3, 6, 5, 8, 7, 10, 9, 12, 11, 14, 13, 16, 15, 18, 17]
WEIGHTS = [1.0 / 3.0] + [1.0 / 18.0] * 6 + [1.0 / 36.0] * 12
INLET_SPEED = (0.05, 0.05, 0.0)
NQ = 19
TILE = 8


def _inflow_constants():
    w = np.array(WEIGHTS, np.float32)
    u = np.array(INLET_SPEED, np.float32)
    c = np.array(VELOCITY, np.float32)
    proj = (c * u[None, :]).sum(1, dtype=np.float32).astype(np.float32)
    usq = np.float32((u * u).sum(dtype=np.float32))
    one = np.float32(1.0)
    val = w * one * (one + np.float32(3.0) * proj + np.float32(4.5) * proj * proj - np.float32(1.5) * usq)
    return [float(v) for v in val.astype(np.float32)]


INFLOW = _inflow_constants()


def _combo(values, coeffs):
    acc = None
    for v, c in zip(values, coeffs):
        if c == 0:
            continue
        term = v if c == 1 else (-v if c == -1 else c * v)
        acc = term if acc is None else acc + term
    return acc


def _equilibrium(rho, u):
    usq = u[0] * u[0] + u[1] * u[1] + u[2] * u[2]
    out = []
    for q in range(NQ):
        p = _combo(u, VELOCITY[q])
        if p is None:
            inner = 1.0 - 1.5 * usq
        else:
            inner = 1.0 + 3.0 * p + 4.5 * p * p - 1.5 * usq
        out.append(WEIGHTS[q] * rho * inner)
    return out


def _collide(f, porous, types, regions, with_grad=False):
    rho = f[0]
    for q in range(1, NQ):
        rho = rho + f[q]
    u = [_combo(f, [VELOCITY[q][k] for q in range(NQ)]) / rho for k in range(3)]
    feq = _equilibrium(rho, u)
    g = [f[q] - feq[q] for q in range(NQ)]
    moments = []
    for a, b in ((0, 0), (1, 1), (2, 2), (0, 1), (0, 2), (1, 2)):
        moments.append(_combo(g, [VELOCITY[q][a] * VELOCITY[q][b] for q in range(NQ)]))
    stress_sq = (
        moments[0] * moments[0]
        + moments[1] * moments[1]
        + moments[2] * moments[2]
        + 2.0 * (moments[3] * moments[3] + moments[4] * moments[4] + moments[5] * moments[5])
    )
    shear = 1.5 * jnp.sqrt(stress_sq + 0.0001) / rho
    viscous = 0.02 * (shear + 0.01) ** (0.7 - 1.0)
    relax = 0.5 + 3.0 * viscous
    design = jnp.where(regions > 0, 1.0, 0.0).astype(jnp.float32)
    damp = porous * design
    outflow = _equilibrium(jnp.ones_like(rho), u)
    inlet = types == 2
    outlet = types == 3
    out = []
    for q in range(NQ):
        relaxed = f[q] - g[q] / relax - damp * (feq[q] - WEIGHTS[q] * rho)
        out.append(jnp.where(inlet, INFLOW[q], jnp.where(outlet, outflow[q], relaxed)))
    if not with_grad:
        return out
    fixed = jnp.logical_or(inlet, outlet)
    grad = [jnp.where(fixed, 0.0, -design * (feq[q] - WEIGHTS[q] * rho)) for q in range(NQ)]
    return out, grad


def _pieces(sign):
    out = []
    for q in range(NQ):
        oa, ot = sign * VELOCITY[q][0], sign * VELOCITY[q][1]
        if oa != 0:
            out.append((q, "a", oa, ot))
        if ot != 0:
            out.append((q, "t", oa, ot))
        if oa != 0 and ot != 0:
            out.append((q, "c", oa, ot))
    return out


FLAG_PIECES = [
    (0, "a", 1, 0),
    (0, "a", -1, 0),
    (0, "t", 0, 1),
    (0, "t", 0, -1),
    (0, "c", 1, 1),
    (0, "c", 1, -1),
    (0, "c", -1, 1),
    (0, "c", -1, -1),
]
NPIECE = 24


class Halo:
    def __init__(self, a_lo, a_hi, t_lo, t_hi):
        self.a_lo, self.a_hi, self.t_lo, self.t_hi = a_lo, a_hi, t_lo, t_hi


def _piece_refs(piece, field, halo, ca, ct):
    q, kind, oa, ot = piece
    a_face = ca - 1 if oa == -1 else 0
    t_face = ct - 1 if ot == -1 else 0
    if kind == "a":
        src = field.at[q, pl.ds(a_face, 1)]
        dst = (halo.a_lo if oa == -1 else halo.a_hi).at[q]
        move = (-oa, 0)
    elif kind == "t":
        src = field.at[q, :, pl.ds(t_face, 1)]
        dst = (halo.t_lo if ot == -1 else halo.t_hi).at[q, pl.ds(1, ca)]
        move = (0, -ot)
    else:
        src = field.at[q, pl.ds(a_face, 1), pl.ds(t_face, 1)]
        slot = 0 if oa == -1 else ca + 1
        dst = (halo.t_lo if ot == -1 else halo.t_hi).at[q, pl.ds(slot, 1)]
        move = (-oa, -ot)
    return src, dst, move


class Exchange:
    def __init__(self, pieces, field, halo, send_sem, recv_sem, pos, sizes, ca, ct):
        self.items = []
        me_ax, me_az = pos
        n_ax, n_az = sizes
        for i, piece in enumerate(pieces):
            src, dst, (da, dt) = _piece_refs(piece, field, halo, ca, ct)
            to_ax = me_ax + da
            from_ax = me_ax - da
            to_dev = (to_ax, lax.rem(me_az + dt + n_az, n_az))
            from_dev = (from_ax, lax.rem(me_az - dt + n_az, n_az))
            send = pltpu.make_async_remote_copy(
                src_ref=src, dst_ref=dst, send_sem=send_sem.at[i], recv_sem=recv_sem.at[i],
                device_id=to_dev, device_id_type=MESH)
            recv = pltpu.make_async_remote_copy(
                src_ref=src, dst_ref=dst, send_sem=send_sem.at[i], recv_sem=recv_sem.at[i],
                device_id=from_dev, device_id_type=MESH)
            send_ok = jnp.logical_and(to_ax >= 0, to_ax < n_ax) if da != 0 else None
            recv_ok = jnp.logical_and(from_ax >= 0, from_ax < n_ax) if da != 0 else None
            self.items.append((send, recv, send_ok, recv_ok))

    @staticmethod
    def _maybe(ok, fn):
        if ok is None:
            fn()
        else:
            pl.when(ok)(fn)

    def start(self):
        for send, _, ok, _ in self.items:
            self._maybe(ok, send.start)

    def wait_recv(self):
        for _, recv, _, ok in self.items:
            self._maybe(ok, recv.wait_recv)

    def wait_send(self):
        for send, _, ok, _ in self.items:
            self._maybe(ok, send.wait_send)


def _shift(own, halo, q, a, oa, ot, orr, lo_ok, hi_ok, ca, ct, nr, zero_r):
    ae = a + oa
    ok = None
    if ae < 0:
        slab = halo.a_lo[q, 0]
        ok = lo_ok
    elif ae >= ca:
        slab = halo.a_hi[q, 0]
        ok = hi_ok
    else:
        slab = own[q, ae]
    if ot != 0:
        rows = lax.broadcasted_iota(jnp.int32, (ct, nr), 0)
        if ot == -1:
            edge = halo.t_lo[q, ae + 1]
            slab = jnp.where(rows == 0, edge, pltpu.roll(slab, 1, 0))
        else:
            edge = halo.t_hi[q, ae + 1]
            slab = jnp.where(rows == ct - 1, edge, pltpu.roll(slab, ct - 1, 0))
    if orr != 0:
        lanes = lax.broadcasted_iota(jnp.int32, (ct, nr), 1)
        if orr == -1:
            slab = jnp.where(lanes == 0, zero_r, pltpu.roll(slab, 1, 1))
        else:
            slab = jnp.where(lanes == nr - 1, zero_r, pltpu.roll(slab, nr - 1, 1))
    if ok is not None:
        slab = jnp.where(ok, slab, zero_r)
    return slab


def _window_kernel(
    n_ax, n_az,
    init_hbm, seed_hbm, por_hbm, type_hbm, reg_hbm,
    final_ref, adj_ref, sens_ref, tot_ref,
    init_ref, seed_ref, por_ref, type_ref, reg_ref, load_sem,
    post0, state1, back1, post1, adj1, back0, gpor, fmask, sens1,
    pop_a_lo, pop_a_hi, pop_t_lo, pop_t_hi,
    ty_a_lo, ty_a_hi, ty_t_lo, ty_t_hi,
    send_sem, recv_sem, ty_send, ty_recv,
    part_ref, row_a, row_b, send_a, recv_a, send_b, recv_b, local,
):
    loads = [
        pltpu.make_async_copy(src, dst, load_sem.at[i])
        for i, (src, dst) in enumerate(
            ((type_hbm, type_ref), (seed_hbm, seed_ref), (init_hbm, init_ref),
             (por_hbm, por_ref), (reg_hbm, reg_ref)))
    ]
    for copy in loads:
        copy.start()
    _, ca, ct, nr = init_ref.shape
    me_ax, me_az = lax.axis_index("ax"), lax.axis_index("az")
    lo_ok = me_ax > 0
    hi_ok = me_ax < n_ax - 1
    pos, sizes = (me_ax, me_az), (n_ax, n_az)

    barrier = pltpu.get_barrier_semaphore()
    up_az, dn_az = lax.rem(me_az + 1, n_az), lax.rem(me_az + n_az - 1, n_az)
    for k in range(1, n_az):
        pl.semaphore_signal(barrier, 1, device_id=(me_ax, lax.rem(me_az + k, n_az)), device_id_type=MESH)
    for k in range(1, n_ax):
        pl.semaphore_signal(barrier, 1, device_id=(lax.rem(me_ax + k, n_ax), me_az), device_id_type=MESH)
    for ok, other in ((lo_ok, me_ax - 1), (hi_ok, me_ax + 1)):
        @pl.when(ok)
        def _():
            for dz in (up_az, dn_az):
                pl.semaphore_signal(barrier, 1, device_id=(other, dz), device_id_type=MESH)
    count = (n_az - 1) + (n_ax - 1) + 2 * (lo_ok.astype(jnp.int32) + hi_ok.astype(jnp.int32))
    for copy in loads:
        copy.wait()

    def halo(k):
        return Halo(pop_a_lo.at[k], pop_a_hi.at[k], pop_t_lo.at[k], pop_t_hi.at[k])

    ty_halo = Halo(ty_a_lo, ty_a_hi, ty_t_lo, ty_t_hi)
    ex_types = Exchange(FLAG_PIECES, type_ref, ty_halo, ty_send, ty_recv, pos, sizes, ca, ct)
    ex_seed = Exchange(_pieces(1), seed_ref, halo(0), send_sem.at[0], recv_sem.at[0], pos, sizes, ca, ct)

    steps = ca * (ct // TILE)

    def tile_at(i):
        a = i // (ct // TILE)
        t0 = pl.multiple_of((i % (ct // TILE)) * TILE, TILE)
        return a, pl.ds(t0, TILE)

    def load(ref, a, ts):
        return [ref[q, a, ts, :] for q in range(NQ)]

    def store(ref, a, ts, vals):
        for q in range(NQ):
            ref[q, a, ts, :] = vals[q]

    def collide_loop(src, dst, grad_dst):
        def body(i, carry):
            a, ts = tile_at(i)
            out, grad = _collide(load(src, a, ts), por_ref[a, ts, :], type_ref[0, a, ts, :],
                                 reg_ref[a, ts, :], with_grad=True)
            store(dst, a, ts, out)
            store(grad_dst, a, ts, grad)
            return carry
        lax.fori_loop(0, steps, body, 0, unroll=True)

    def vjp_loop(at, upstream, primal_dst, grad_dst, sens_dst):
        def body(i, carry):
            a, ts = tile_at(i)
            types = type_ref[0, a, ts, :]
            regions = reg_ref[a, ts, :]
            out, pullback = jax.vjp(
                lambda f, p: _collide(f, p, types, regions), load(at, a, ts), por_ref[a, ts, :])
            if primal_dst is not None:
                store(primal_dst, a, ts, out)
            d_f, d_p = pullback(load(upstream, a, ts))
            store(grad_dst, a, ts, d_f)
            if sens_dst is not None:
                sens_dst[a, ts, :] = d_p
            return carry
        lax.fori_loop(0, steps, body, 0, unroll=True)

    zero = jnp.zeros((ct, nr), jnp.float32)

    def flag_shift(a, oa, ot, orr):
        if oa == 0 and ot == 0 and orr == 0:
            own = type_ref[0, a]
            return jnp.where(own != 1, 1.0, 0.0).astype(jnp.float32)
        ty = _shift(type_ref, ty_halo, 0, a, oa, ot, orr, lo_ok, hi_ok, ca, ct, nr, jnp.ones((ct, nr), jnp.int32))
        return jnp.where(ty != 1, 1.0, 0.0).astype(jnp.float32)

    def fill_masks():
        for a in range(ca):
            for q in range(NQ):
                c = VELOCITY[q]
                fmask[q, a] = flag_shift(a, -c[0], -c[1], -c[2])

    def stream(post, hal, dst):
        for a in range(ca):
            for q in range(NQ):
                c = VELOCITY[q]
                moved = _shift(post, hal, q, a, -c[0], -c[1], -c[2], lo_ok, hi_ok, ca, ct, nr, zero)
                ok = fmask[q, a] > 0
                dst[q, a] = jnp.where(ok, moved, post[OPPOSITE[q], a])

    def stream_adjoint(adj, hal, dst):
        for a in range(ca):
            centre = fmask[0, a]
            for q in range(NQ):
                c = VELOCITY[q]
                ahead = _shift(adj, hal, q, a, c[0], c[1], c[2], lo_ok, hi_ok, ca, ct, nr, zero)
                blocked = 1.0 - fmask[OPPOSITE[q], a]
                dst[q, a] = centre * ahead + blocked * adj[OPPOSITE[q], a]

    collide_loop(init_ref, post0, gpor)
    pl.semaphore_wait(barrier, count)
    ex_post0 = Exchange(_pieces(-1), post0, halo(1), send_sem.at[1], recv_sem.at[1], pos, sizes, ca, ct)
    ex_types.start()
    ex_post0.start()
    ex_seed.start()
    ex_types.wait_recv()
    fill_masks()
    ex_post0.wait_recv()
    stream(post0, halo(1), state1)
    ex_seed.wait_recv()
    stream_adjoint(seed_ref, halo(0), back1)
    vjp_loop(state1, back1, post1, adj1, sens1)
    ex_post1 = Exchange(_pieces(-1), post1, halo(2), send_sem.at[2], recv_sem.at[2], pos, sizes, ca, ct)
    ex_adj1 = Exchange(_pieces(1), adj1, halo(3), send_sem.at[3], recv_sem.at[3], pos, sizes, ca, ct)
    ex_adj1.start()
    ex_post1.start()
    ex_adj1.wait_recv()
    stream_adjoint(adj1, halo(3), back0)
    for a in range(ca):
        sens0 = back0[0, a] * gpor[0, a]
        for q in range(1, NQ):
            sens0 = sens0 + back0[q, a] * gpor[q, a]
        sens_ref[a] = sens1[a] + sens0

    total = jnp.zeros((1, 1), jnp.float32)
    rid = jnp.zeros((1, 1), jnp.int32)
    for a in range(ca):
        reg = reg_ref[a]
        total = total + jnp.sum(jnp.where(reg > 0, sens_ref[a], 0.0), keepdims=True)
        rid = jnp.maximum(rid, jnp.max(reg, keepdims=True))
    labels = lax.broadcasted_iota(jnp.int32, part_ref.shape, 1) + 1
    part_ref[...] = jnp.where(labels == rid, total, 0.0)
    first = _TotalsStage(part_ref, row_a, send_a, recv_a, local.at[0], me_az, n_az,
                         lambda j: (me_ax, j))
    first.start()

    vjp_loop(init_ref, back0, None, adj_ref, None)
    ex_post1.wait_recv()
    stream(post1, halo(2), final_ref)

    first.finish(part_ref)
    own = pltpu.make_async_copy(part_ref, row_b.at[me_ax], local.at[1])
    own.start()
    own.wait()
    second = _TotalsStage(row_b.at[me_ax], row_b, send_b, recv_b, None, me_ax, n_ax,
                          lambda j: (j, me_az))
    second.start()
    second.finish(tot_ref)

    for ex in (ex_types, ex_seed, ex_post0, ex_post1, ex_adj1):
        ex.wait_send()


class _TotalsStage:
    def __init__(self, src, rows, send, recv, own_sem, me, n, device):
        self.src, self.rows, self.own_sem, self.me, self.n = src, rows, own_sem, me, n
        self.sends, self.recvs = [], []
        for k in range(1, n):
            to, frm = lax.rem(me + k, n), lax.rem(me + n - k, n)
            self.sends.append(pltpu.make_async_remote_copy(
                src_ref=src, dst_ref=rows.at[me], send_sem=send.at[k], recv_sem=recv.at[me],
                device_id=device(to), device_id_type=MESH))
            self.recvs.append(pltpu.make_async_remote_copy(
                src_ref=src, dst_ref=rows.at[frm], send_sem=send.at[k], recv_sem=recv.at[frm],
                device_id=device(frm), device_id_type=MESH))

    def start(self):
        self.own = None
        if self.own_sem is not None:
            self.own = pltpu.make_async_copy(self.src, self.rows.at[self.me], self.own_sem)
            self.own.start()
        for copy in self.sends:
            copy.start()

    def finish(self, out):
        if self.own is not None:
            self.own.wait()
        for copy in self.recvs:
            copy.wait_recv()
        acc = self.rows[0]
        for j in range(1, self.n):
            acc = acc + self.rows[j]
        for copy in self.sends:
            copy.wait_send()
        out[...] = acc


def window(initial, adjoint_seed, porosity, cell_type, region, n_regions):
    n_ax, n_az = lax.axis_size("ax"), lax.axis_size("az")
    nq, ca, ct, nr = initial.shape
    pop = jax.ShapeDtypeStruct(initial.shape, jnp.float32)
    cells = jax.ShapeDtypeStruct(porosity.shape, jnp.float32)
    vmem = pltpu.VMEM
    f32, i32 = jnp.float32, jnp.int32
    scratch = (
        [vmem(initial.shape, f32), vmem(initial.shape, f32), vmem(porosity.shape, f32),
         vmem((1,) + cell_type.shape, i32), vmem(region.shape, i32), pltpu.SemaphoreType.DMA((5,))]

        + [vmem((nq, ca, ct, nr), f32) for _ in range(8)]
        + [vmem((ca, ct, nr), f32)]
        + [vmem((4, nq, 1, ct, nr), f32), vmem((4, nq, 1, ct, nr), f32),
           vmem((4, nq, ca + 2, 1, nr), f32), vmem((4, nq, ca + 2, 1, nr), f32)]
        + [vmem((1, 1, ct, nr), i32), vmem((1, 1, ct, nr), i32),
           vmem((1, ca + 2, 1, nr), i32), vmem((1, ca + 2, 1, nr), i32)]
        + [pltpu.SemaphoreType.DMA((4, NPIECE)), pltpu.SemaphoreType.DMA((4, NPIECE)),
           pltpu.SemaphoreType.DMA((len(FLAG_PIECES),)), pltpu.SemaphoreType.DMA((len(FLAG_PIECES),))]
        + [vmem((1, n_regions), f32), vmem((n_az, 1, n_regions), f32), vmem((n_ax, 1, n_regions), f32),
           pltpu.SemaphoreType.DMA((n_az,)), pltpu.SemaphoreType.DMA((n_az,)),
           pltpu.SemaphoreType.DMA((n_ax,)), pltpu.SemaphoreType.DMA((n_ax,)),
           pltpu.SemaphoreType.DMA((2,))]
    )
    final, adj, sens, tot = pl.pallas_call(
        functools.partial(_window_kernel, n_ax, n_az),
        out_shape=(pop, pop, cells, jax.ShapeDtypeStruct((1, n_regions), f32)),
        in_specs=[pl.BlockSpec(memory_space=pltpu.HBM)] * 5,
        out_specs=(pl.BlockSpec(memory_space=vmem),) * 4,
        scratch_shapes=scratch,
        compiler_params=pltpu.CompilerParams(collective_id=1, has_side_effects=True,
                                             vmem_limit_bytes=67043328),
    )(initial, adjoint_seed, porosity, cell_type.reshape((1,) + cell_type.shape), region)
    return final, adj, sens, tot


def shards(initial, adjoint_seed, porosity, cell_type, region):
    n_regions = lax.axis_size("ax") * lax.axis_size("az") // 4
    final, adjoint, sensitivity, totals = window(
        initial, adjoint_seed, porosity, cell_type, region, n_regions)
    totals = totals.reshape(-1)
    return (final, adjoint, sensitivity, totals)


def solution(mesh):
    return jax.shard_map(
        shards,
        mesh=mesh,
        in_specs=(
            P(None, "ax", "az", None),
            P(None, "ax", "az", None),
            P("ax", "az", None),
            P("ax", "az", None),
            P("ax", "az", None),
        ),
        out_specs=(P(None, "ax", "az", None), P(None, "ax", "az", None), P("ax", "az", None), P()),
        check_vma=False,
    )
```

```python
import functools

import numpy as np

import jax
import jax.numpy as jnp
from jax import lax
from jax.experimental import pallas as pl
from jax.experimental.pallas import tpu as pltpu
from jax.sharding import PartitionSpec as P

MESH = pl.DeviceIdType.MESH

VELOCITY = [
    (0, 0, 0),
    (1, 0, 0),
    (-1, 0, 0),
    (0, 1, 0),
    (0, -1, 0),
    (0, 0, 1),
    (0, 0, -1),
    (1, 1, 0),
    (-1, -1, 0),
    (1, -1, 0),
    (-1, 1, 0),
    (1, 0, 1),
    (-1, 0, -1),
    (1, 0, -1),
    (-1, 0, 1),
    (0, 1, 1),
    (0, -1, -1),
    (0, 1, -1),
    (0, -1, 1),
]
OPPOSITE = [0, 2, 1, 4, 3, 6, 5, 8, 7, 10, 9, 12, 11, 14, 13, 16, 15, 18, 17]
WEIGHTS = [1.0 / 3.0] + [1.0 / 18.0] * 6 + [1.0 / 36.0] * 12
INLET_SPEED = (0.05, 0.05, 0.0)
NQ = 19
TILE = 8


def _inflow_constants():
    w = np.array(WEIGHTS, np.float32)
    u = np.array(INLET_SPEED, np.float32)
    c = np.array(VELOCITY, np.float32)
    proj = (c * u[None, :]).sum(1, dtype=np.float32).astype(np.float32)
    usq = np.float32((u * u).sum(dtype=np.float32))
    one = np.float32(1.0)
    val = w * one * (one + np.float32(3.0) * proj + np.float32(4.5) * proj * proj - np.float32(1.5) * usq)
    return [float(v) for v in val.astype(np.float32)]


INFLOW = _inflow_constants()


def _combo(values, coeffs):
    acc = None
    for v, c in zip(values, coeffs):
        if c == 0:
            continue
        term = v if c == 1 else (-v if c == -1 else c * v)
        acc = term if acc is None else acc + term
    return acc


def _equilibrium(rho, u):
    usq = u[0] * u[0] + u[1] * u[1] + u[2] * u[2]
    out = []
    for q in range(NQ):
        p = _combo(u, VELOCITY[q])
        if p is None:
            inner = 1.0 - 1.5 * usq
        else:
            inner = 1.0 + 3.0 * p + 4.5 * p * p - 1.5 * usq
        out.append(WEIGHTS[q] * rho * inner)
    return out


def _collide(f, porous, types, regions, with_grad=False):
    rho = f[0]
    for q in range(1, NQ):
        rho = rho + f[q]
    u = [_combo(f, [VELOCITY[q][k] for q in range(NQ)]) / rho for k in range(3)]
    feq = _equilibrium(rho, u)
    g = [f[q] - feq[q] for q in range(NQ)]
    moments = []
    for a, b in ((0, 0), (1, 1), (2, 2), (0, 1), (0, 2), (1, 2)):
        moments.append(_combo(g, [VELOCITY[q][a] * VELOCITY[q][b] for q in range(NQ)]))
    stress_sq = (
        moments[0] * moments[0]
        + moments[1] * moments[1]
        + moments[2] * moments[2]
        + 2.0 * (moments[3] * moments[3] + moments[4] * moments[4] + moments[5] * moments[5])
    )
    shear = 1.5 * jnp.sqrt(stress_sq + 0.0001) / rho
    viscous = 0.02 * (shear + 0.01) ** (0.7 - 1.0)
    relax = 0.5 + 3.0 * viscous
    design = jnp.where(regions > 0, 1.0, 0.0).astype(jnp.float32)
    damp = porous * design
    outflow = _equilibrium(jnp.ones_like(rho), u)
    inlet = types == 2
    outlet = types == 3
    out = []
    for q in range(NQ):
        relaxed = f[q] - g[q] / relax - damp * (feq[q] - WEIGHTS[q] * rho)
        out.append(jnp.where(inlet, INFLOW[q], jnp.where(outlet, outflow[q], relaxed)))
    if not with_grad:
        return out
    fixed = jnp.logical_or(inlet, outlet)
    grad = [jnp.where(fixed, 0.0, -design * (feq[q] - WEIGHTS[q] * rho)) for q in range(NQ)]
    return out, grad


def _pieces(sign):
    out = []
    for q in range(NQ):
        oa, ot = sign * VELOCITY[q][0], sign * VELOCITY[q][1]
        if oa != 0:
            out.append((q, "a", oa, ot))
        if ot != 0:
            out.append((q, "t", oa, ot))
        if oa != 0 and ot != 0:
            out.append((q, "c", oa, ot))
    return out


FLAG_PIECES = [
    (0, "a", 1, 0),
    (0, "a", -1, 0),
    (0, "t", 0, 1),
    (0, "t", 0, -1),
    (0, "c", 1, 1),
    (0, "c", 1, -1),
    (0, "c", -1, 1),
    (0, "c", -1, -1),
]
NPIECE = 24


class Halo:
    def __init__(self, a_lo, a_hi, t_lo, t_hi):
        self.a_lo, self.a_hi, self.t_lo, self.t_hi = a_lo, a_hi, t_lo, t_hi


def _piece_refs(piece, field, halo, ca, ct):
    q, kind, oa, ot = piece
    a_face = ca - 1 if oa == -1 else 0
    t_face = ct - 1 if ot == -1 else 0
    if kind == "a":
        src = field.at[q, pl.ds(a_face, 1)]
        dst = (halo.a_lo if oa == -1 else halo.a_hi).at[q]
        move = (-oa, 0)
    elif kind == "t":
        src = field.at[q, :, pl.ds(t_face, 1)]
        dst = (halo.t_lo if ot == -1 else halo.t_hi).at[q, pl.ds(1, ca)]
        move = (0, -ot)
    else:
        src = field.at[q, pl.ds(a_face, 1), pl.ds(t_face, 1)]
        slot = 0 if oa == -1 else ca + 1
        dst = (halo.t_lo if ot == -1 else halo.t_hi).at[q, pl.ds(slot, 1)]
        move = (-oa, -ot)
    return src, dst, move


class Exchange:
    def __init__(self, pieces, field, halo, send_sem, recv_sem, pos, sizes, ca, ct):
        self.items = []
        me_ax, me_az = pos
        n_ax, n_az = sizes
        for i, piece in enumerate(pieces):
            src, dst, (da, dt) = _piece_refs(piece, field, halo, ca, ct)
            to_ax = me_ax + da
            from_ax = me_ax - da
            to_dev = (to_ax, lax.rem(me_az + dt + n_az, n_az))
            from_dev = (from_ax, lax.rem(me_az - dt + n_az, n_az))
            send = pltpu.make_async_remote_copy(
                src_ref=src, dst_ref=dst, send_sem=send_sem.at[i], recv_sem=recv_sem.at[i],
                device_id=to_dev, device_id_type=MESH)
            recv = pltpu.make_async_remote_copy(
                src_ref=src, dst_ref=dst, send_sem=send_sem.at[i], recv_sem=recv_sem.at[i],
                device_id=from_dev, device_id_type=MESH)
            send_ok = jnp.logical_and(to_ax >= 0, to_ax < n_ax) if da != 0 else None
            recv_ok = jnp.logical_and(from_ax >= 0, from_ax < n_ax) if da != 0 else None
            self.items.append((send, recv, send_ok, recv_ok))

    @staticmethod
    def _maybe(ok, fn):
        if ok is None:
            fn()
        else:
            pl.when(ok)(fn)

    def start(self):
        for send, _, ok, _ in self.items:
            self._maybe(ok, send.start)

    def wait_recv(self):
        for _, recv, _, ok in self.items:
            self._maybe(ok, recv.wait_recv)

    def wait_send(self):
        for send, _, ok, _ in self.items:
            self._maybe(ok, send.wait_send)


def _shift(own, halo, q, a, oa, ot, orr, lo_ok, hi_ok, ca, ct, nr, zero_r):
    ae = a + oa
    ok = None
    if ae < 0:
        slab = halo.a_lo[q, 0]
        ok = lo_ok
    elif ae >= ca:
        slab = halo.a_hi[q, 0]
        ok = hi_ok
    else:
        slab = own[q, ae]
    if ot != 0:
        rows = lax.broadcasted_iota(jnp.int32, (ct, nr), 0)
        if ot == -1:
            edge = halo.t_lo[q, ae + 1]
            slab = jnp.where(rows == 0, edge, pltpu.roll(slab, 1, 0))
        else:
            edge = halo.t_hi[q, ae + 1]
            slab = jnp.where(rows == ct - 1, edge, pltpu.roll(slab, ct - 1, 0))
    if orr != 0:
        lanes = lax.broadcasted_iota(jnp.int32, (ct, nr), 1)
        if orr == -1:
            slab = jnp.where(lanes == 0, zero_r, pltpu.roll(slab, 1, 1))
        else:
            slab = jnp.where(lanes == nr - 1, zero_r, pltpu.roll(slab, nr - 1, 1))
    if ok is not None:
        slab = jnp.where(ok, slab, zero_r)
    return slab


def _window_kernel(
    n_ax, n_az,
    init_hbm, seed_hbm, por_hbm, type_hbm, reg_hbm,
    final_ref, adj_ref, sens_ref, tot_ref,
    init_ref, seed_ref, por_ref, type_ref, reg_ref, load_sem,
    post0, state1, back1, post1, adj1, back0, gpor, fmask, sens1,
    pop_a_lo, pop_a_hi, pop_t_lo, pop_t_hi,
    ty_a_lo, ty_a_hi, ty_t_lo, ty_t_hi,
    send_sem, recv_sem, ty_send, ty_recv,
    part_ref, row_a, row_b, send_a, recv_a, send_b, recv_b, local,
):
    loads = [
        pltpu.make_async_copy(src, dst, load_sem.at[i])
        for i, (src, dst) in enumerate(
            ((type_hbm, type_ref), (seed_hbm, seed_ref), (init_hbm, init_ref),
             (por_hbm, por_ref), (reg_hbm, reg_ref)))
    ]
    for copy in loads:
        copy.start()
    _, ca, ct, nr = init_ref.shape
    me_ax, me_az = lax.axis_index("ax"), lax.axis_index("az")
    lo_ok = me_ax > 0
    hi_ok = me_ax < n_ax - 1
    pos, sizes = (me_ax, me_az), (n_ax, n_az)

    barrier = pltpu.get_barrier_semaphore()
    up_az, dn_az = lax.rem(me_az + 1, n_az), lax.rem(me_az + n_az - 1, n_az)
    for k in range(1, n_az):
        peer = me_az + k
        peer = jnp.where(peer >= n_az, peer - n_az, peer)
        pl.semaphore_signal(barrier, 1, device_id=(me_ax, peer), device_id_type=MESH)
    for k in range(1, n_ax):
        peer = me_ax + k
        peer = jnp.where(peer >= n_ax, peer - n_ax, peer)
        pl.semaphore_signal(barrier, 1, device_id=(peer, me_az), device_id_type=MESH)
    for ok, other in ((lo_ok, me_ax - 1), (hi_ok, me_ax + 1)):
        @pl.when(ok)
        def _():
            for dz in (up_az, dn_az):
                pl.semaphore_signal(barrier, 1, device_id=(other, dz), device_id_type=MESH)
    count = (n_az - 1) + (n_ax - 1) + 2 * (lo_ok.astype(jnp.int32) + hi_ok.astype(jnp.int32))
    for copy in loads[:1] + loads[2:]:
        copy.wait()

    def halo(k):
        return Halo(pop_a_lo.at[k], pop_a_hi.at[k], pop_t_lo.at[k], pop_t_hi.at[k])

    ty_halo = Halo(ty_a_lo, ty_a_hi, ty_t_lo, ty_t_hi)
    ex_types = Exchange(FLAG_PIECES, type_ref, ty_halo, ty_send, ty_recv, pos, sizes, ca, ct)
    ex_seed = Exchange(_pieces(1), seed_ref, halo(0), send_sem.at[0], recv_sem.at[0], pos, sizes, ca, ct)

    steps = ca * (ct // TILE)

    def tile_at(i):
        a = i // (ct // TILE)
        t0 = pl.multiple_of((i % (ct // TILE)) * TILE, TILE)
        return a, pl.ds(t0, TILE)

    def load(ref, a, ts):
        return [ref[q, a, ts, :] for q in range(NQ)]

    def store(ref, a, ts, vals):
        for q in range(NQ):
            ref[q, a, ts, :] = vals[q]

    def collide_loop(src, dst, grad_dst):
        def body(i, carry):
            a, ts = tile_at(i)
            out, grad = _collide(load(src, a, ts), por_ref[a, ts, :], type_ref[0, a, ts, :],
                                 reg_ref[a, ts, :], with_grad=True)
            store(dst, a, ts, out)
            store(grad_dst, a, ts, grad)
            return carry
        lax.fori_loop(0, steps, body, 0)

    def vjp_loop(at, upstream, primal_dst, grad_dst, sens_dst):
        def body(i, carry):
            a, ts = tile_at(i)
            types = type_ref[0, a, ts, :]
            regions = reg_ref[a, ts, :]
            out, pullback = jax.vjp(
                lambda f, p: _collide(f, p, types, regions), load(at, a, ts), por_ref[a, ts, :])
            if primal_dst is not None:
                store(primal_dst, a, ts, out)
            d_f, d_p = pullback(load(upstream, a, ts))
            store(grad_dst, a, ts, d_f)
            if sens_dst is not None:
                sens_dst[a, ts, :] = d_p
            return carry
        lax.fori_loop(0, steps, body, 0)

    zero = jnp.zeros((ct, nr), jnp.float32)

    def flag_shift(a, oa, ot, orr):
        if oa == 0 and ot == 0 and orr == 0:
            own = type_ref[0, a]
            return jnp.where(own != 1, 1.0, 0.0).astype(jnp.float32)
        ty = _shift(type_ref, ty_halo, 0, a, oa, ot, orr, lo_ok, hi_ok, ca, ct, nr, jnp.ones((ct, nr), jnp.int32))
        return jnp.where(ty != 1, 1.0, 0.0).astype(jnp.float32)

    def fill_masks():
        for a in range(ca):
            for q in range(NQ):
                c = VELOCITY[q]
                fmask[q, a] = flag_shift(a, -c[0], -c[1], -c[2])

    def stream(post, hal, dst):
        for a in range(ca):
            for q in range(NQ):
                c = VELOCITY[q]
                moved = _shift(post, hal, q, a, -c[0], -c[1], -c[2], lo_ok, hi_ok, ca, ct, nr, zero)
                ok = fmask[q, a] > 0
                dst[q, a] = jnp.where(ok, moved, post[OPPOSITE[q], a])

    def stream_adjoint(adj, hal, dst):
        for a in range(ca):
            centre = fmask[0, a]
            for q in range(NQ):
                c = VELOCITY[q]
                ahead = _shift(adj, hal, q, a, c[0], c[1], c[2], lo_ok, hi_ok, ca, ct, nr, zero)
                blocked = 1.0 - fmask[OPPOSITE[q], a]
                dst[q, a] = centre * ahead + blocked * adj[OPPOSITE[q], a]

    collide_loop(init_ref, post0, gpor)
    loads[1].wait()
    pl.semaphore_wait(barrier, count)
    ex_post0 = Exchange(_pieces(-1), post0, halo(1), send_sem.at[1], recv_sem.at[1], pos, sizes, ca, ct)
    ex_types.start()
    ex_post0.start()
    ex_seed.start()
    ex_types.wait_recv()
    fill_masks()
    ex_post0.wait_recv()
    stream(post0, halo(1), state1)
    ex_seed.wait_recv()
    stream_adjoint(seed_ref, halo(0), back1)
    vjp_loop(state1, back1, post1, adj1, sens1)
    ex_post1 = Exchange(_pieces(-1), post1, halo(2), send_sem.at[2], recv_sem.at[2], pos, sizes, ca, ct)
    ex_adj1 = Exchange(_pieces(1), adj1, halo(3), send_sem.at[3], recv_sem.at[3], pos, sizes, ca, ct)
    ex_adj1.start()
    ex_post1.start()
    ex_adj1.wait_recv()
    stream_adjoint(adj1, halo(3), back0)
    for a in range(ca):
        sens0 = back0[0, a] * gpor[0, a]
        for q in range(1, NQ):
            sens0 = sens0 + back0[q, a] * gpor[q, a]
        sens_ref[a] = sens1[a] + sens0

    total = jnp.zeros((1, 1), jnp.float32)
    rid = jnp.zeros((1, 1), jnp.int32)
    for a in range(ca):
        reg = reg_ref[a]
        total = total + jnp.sum(jnp.where(reg > 0, sens_ref[a], 0.0), keepdims=True)
        rid = jnp.maximum(rid, jnp.max(reg, keepdims=True))
    labels = lax.broadcasted_iota(jnp.int32, part_ref.shape, 1) + 1
    part_ref[...] = jnp.where(labels == rid, total, 0.0)
    first = _TotalsStage(part_ref, row_a, send_a, recv_a, local.at[0], me_az, n_az,
                         lambda j: (me_ax, j))
    first.start()

    vjp_loop(init_ref, back0, None, adj_ref, None)
    ex_post1.wait_recv()
    stream(post1, halo(2), final_ref)

    first.finish(part_ref)
    own = pltpu.make_async_copy(part_ref, row_b.at[me_ax], local.at[1])
    own.start()
    own.wait()
    second = _TotalsStage(row_b.at[me_ax], row_b, send_b, recv_b, None, me_ax, n_ax,
                          lambda j: (j, me_az))
    second.start()
    second.finish(tot_ref)

    for ex in (ex_types, ex_seed, ex_post0, ex_post1, ex_adj1):
        ex.wait_send()


class _TotalsStage:
    def __init__(self, src, rows, send, recv, own_sem, me, n, device):
        self.src, self.rows, self.own_sem, self.me, self.n = src, rows, own_sem, me, n
        self.sends, self.recvs = [], []
        for k in range(1, n):
            to, frm = lax.rem(me + k, n), lax.rem(me + n - k, n)
            self.sends.append(pltpu.make_async_remote_copy(
                src_ref=src, dst_ref=rows.at[me], send_sem=send.at[k], recv_sem=recv.at[me],
                device_id=device(to), device_id_type=MESH))
            self.recvs.append(pltpu.make_async_remote_copy(
                src_ref=src, dst_ref=rows.at[frm], send_sem=send.at[k], recv_sem=recv.at[frm],
                device_id=device(frm), device_id_type=MESH))

    def start(self):
        self.own = None
        if self.own_sem is not None:
            self.own = pltpu.make_async_copy(self.src, self.rows.at[self.me], self.own_sem)
            self.own.start()
        for copy in self.sends:
            copy.start()

    def finish(self, out):
        if self.own is not None:
            self.own.wait()
        for copy in self.recvs:
            copy.wait_recv()
        acc = self.rows[0]
        for j in range(1, self.n):
            acc = acc + self.rows[j]
        for copy in self.sends:
            copy.wait_send()
        out[...] = acc


def window(initial, adjoint_seed, porosity, cell_type, region, n_regions):
    n_ax, n_az = lax.axis_size("ax"), lax.axis_size("az")
    nq, ca, ct, nr = initial.shape
    pop = jax.ShapeDtypeStruct(initial.shape, jnp.float32)
    cells = jax.ShapeDtypeStruct(porosity.shape, jnp.float32)
    vmem = pltpu.VMEM
    f32, i32 = jnp.float32, jnp.int32
    scratch = (
        [vmem(initial.shape, f32), vmem(initial.shape, f32), vmem(porosity.shape, f32),
         vmem((1,) + cell_type.shape, i32), vmem(region.shape, i32), pltpu.SemaphoreType.DMA((5,))]

        + [vmem((nq, ca, ct, nr), f32) for _ in range(8)]
        + [vmem((ca, ct, nr), f32)]
        + [vmem((4, nq, 1, ct, nr), f32), vmem((4, nq, 1, ct, nr), f32),
           vmem((4, nq, ca + 2, 1, nr), f32), vmem((4, nq, ca + 2, 1, nr), f32)]
        + [vmem((1, 1, ct, nr), i32), vmem((1, 1, ct, nr), i32),
           vmem((1, ca + 2, 1, nr), i32), vmem((1, ca + 2, 1, nr), i32)]
        + [pltpu.SemaphoreType.DMA((4, NPIECE)), pltpu.SemaphoreType.DMA((4, NPIECE)),
           pltpu.SemaphoreType.DMA((len(FLAG_PIECES),)), pltpu.SemaphoreType.DMA((len(FLAG_PIECES),))]
        + [vmem((1, n_regions), f32), vmem((n_az, 1, n_regions), f32), vmem((n_ax, 1, n_regions), f32),
           pltpu.SemaphoreType.DMA((n_az,)), pltpu.SemaphoreType.DMA((n_az,)),
           pltpu.SemaphoreType.DMA((n_ax,)), pltpu.SemaphoreType.DMA((n_ax,)),
           pltpu.SemaphoreType.DMA((2,))]
    )
    final, adj, sens, tot = pl.pallas_call(
        functools.partial(_window_kernel, n_ax, n_az),
        out_shape=(pop, pop, cells, jax.ShapeDtypeStruct((1, n_regions), f32)),
        in_specs=[pl.BlockSpec(memory_space=pltpu.HBM)] * 5,
        out_specs=(pl.BlockSpec(memory_space=vmem),) * 4,
        scratch_shapes=scratch,
        compiler_params=pltpu.CompilerParams(collective_id=1, has_side_effects=True,
                                             vmem_limit_bytes=67043328),
    )(initial, adjoint_seed, porosity, cell_type.reshape((1,) + cell_type.shape), region)
    return final, adj, sens, tot


def shards(initial, adjoint_seed, porosity, cell_type, region):
    n_regions = lax.axis_size("ax") * lax.axis_size("az") // 4
    final, adjoint, sensitivity, totals = window(
        initial, adjoint_seed, porosity, cell_type, region, n_regions)
    totals = totals.reshape(-1)
    return (final, adjoint, sensitivity, totals)


def solution(mesh):
    return jax.shard_map(
        shards,
        mesh=mesh,
        in_specs=(
            P(None, "ax", "az", None),
            P(None, "ax", "az", None),
            P("ax", "az", None),
            P("ax", "az", None),
            P("ax", "az", None),
        ),
        out_specs=(P(None, "ax", "az", None), P(None, "ax", "az", None), P("ax", "az", None), P()),
        check_vma=False,
    )
```

```python
import functools

import numpy as np

import jax
import jax.numpy as jnp
from jax import lax
from jax.experimental import pallas as pl
from jax.experimental.pallas import tpu as pltpu
from jax.sharding import PartitionSpec as P

MESH = pl.DeviceIdType.MESH

VELOCITY = [
    (0, 0, 0),
    (1, 0, 0),
    (-1, 0, 0),
    (0, 1, 0),
    (0, -1, 0),
    (0, 0, 1),
    (0, 0, -1),
    (1, 1, 0),
    (-1, -1, 0),
    (1, -1, 0),
    (-1, 1, 0),
    (1, 0, 1),
    (-1, 0, -1),
    (1, 0, -1),
    (-1, 0, 1),
    (0, 1, 1),
    (0, -1, -1),
    (0, 1, -1),
    (0, -1, 1),
]
OPPOSITE = [0, 2, 1, 4, 3, 6, 5, 8, 7, 10, 9, 12, 11, 14, 13, 16, 15, 18, 17]
WEIGHTS = [1.0 / 3.0] + [1.0 / 18.0] * 6 + [1.0 / 36.0] * 12
INLET_SPEED = (0.05, 0.05, 0.0)
NQ = 19
TILE = 8


def _inflow_constants():
    w = np.array(WEIGHTS, np.float32)
    u = np.array(INLET_SPEED, np.float32)
    c = np.array(VELOCITY, np.float32)
    proj = (c * u[None, :]).sum(1, dtype=np.float32).astype(np.float32)
    usq = np.float32((u * u).sum(dtype=np.float32))
    one = np.float32(1.0)
    val = w * one * (one + np.float32(3.0) * proj + np.float32(4.5) * proj * proj - np.float32(1.5) * usq)
    return [float(v) for v in val.astype(np.float32)]


INFLOW = _inflow_constants()


def _combo(values, coeffs):
    acc = None
    for v, c in zip(values, coeffs):
        if c == 0:
            continue
        term = v if c == 1 else (-v if c == -1 else c * v)
        acc = term if acc is None else acc + term
    return acc


def _equilibrium(rho, u):
    usq = u[0] * u[0] + u[1] * u[1] + u[2] * u[2]
    out = []
    for q in range(NQ):
        p = _combo(u, VELOCITY[q])
        if p is None:
            inner = 1.0 - 1.5 * usq
        else:
            inner = 1.0 + 3.0 * p + 4.5 * p * p - 1.5 * usq
        out.append(WEIGHTS[q] * rho * inner)
    return out


def _collide(f, porous, types, regions, with_grad=False):
    rho = f[0]
    for q in range(1, NQ):
        rho = rho + f[q]
    u = [_combo(f, [VELOCITY[q][k] for q in range(NQ)]) / rho for k in range(3)]
    feq = _equilibrium(rho, u)
    g = [f[q] - feq[q] for q in range(NQ)]
    moments = []
    for a, b in ((0, 0), (1, 1), (2, 2), (0, 1), (0, 2), (1, 2)):
        moments.append(_combo(g, [VELOCITY[q][a] * VELOCITY[q][b] for q in range(NQ)]))
    stress_sq = (
        moments[0] * moments[0]
        + moments[1] * moments[1]
        + moments[2] * moments[2]
        + 2.0 * (moments[3] * moments[3] + moments[4] * moments[4] + moments[5] * moments[5])
    )
    shear = 1.5 * jnp.sqrt(stress_sq + 0.0001) / rho
    viscous = 0.02 * (shear + 0.01) ** (0.7 - 1.0)
    relax = 0.5 + 3.0 * viscous
    design = jnp.where(regions > 0, 1.0, 0.0).astype(jnp.float32)
    damp = porous * design
    outflow = _equilibrium(jnp.ones_like(rho), u)
    inlet = types == 2
    outlet = types == 3
    out = []
    for q in range(NQ):
        relaxed = f[q] - g[q] / relax - damp * (feq[q] - WEIGHTS[q] * rho)
        out.append(jnp.where(inlet, INFLOW[q], jnp.where(outlet, outflow[q], relaxed)))
    if not with_grad:
        return out
    fixed = jnp.logical_or(inlet, outlet)
    grad = [jnp.where(fixed, 0.0, -design * (feq[q] - WEIGHTS[q] * rho)) for q in range(NQ)]
    return out, grad


def _pieces(sign):
    out = []
    for q in range(NQ):
        oa, ot = sign * VELOCITY[q][0], sign * VELOCITY[q][1]
        if oa != 0:
            out.append((q, "a", oa, ot))
        if ot != 0:
            out.append((q, "t", oa, ot))
        if oa != 0 and ot != 0:
            out.append((q, "c", oa, ot))
    return out


FLAG_PIECES = [
    (0, "a", 1, 0),
    (0, "a", -1, 0),
    (0, "t", 0, 1),
    (0, "t", 0, -1),
    (0, "c", 1, 1),
    (0, "c", 1, -1),
    (0, "c", -1, 1),
    (0, "c", -1, -1),
]
NPIECE = 24


class Halo:
    def __init__(self, a_lo, a_hi, t_lo, t_hi):
        self.a_lo, self.a_hi, self.t_lo, self.t_hi = a_lo, a_hi, t_lo, t_hi


def _piece_refs(piece, field, halo, ca, ct):
    q, kind, oa, ot = piece
    a_face = ca - 1 if oa == -1 else 0
    t_face = ct - 1 if ot == -1 else 0
    if kind == "a":
        src = field.at[q, pl.ds(a_face, 1)]
        dst = (halo.a_lo if oa == -1 else halo.a_hi).at[q]
        move = (-oa, 0)
    elif kind == "t":
        src = field.at[q, :, pl.ds(t_face, 1)]
        dst = (halo.t_lo if ot == -1 else halo.t_hi).at[q, pl.ds(1, ca)]
        move = (0, -ot)
    else:
        src = field.at[q, pl.ds(a_face, 1), pl.ds(t_face, 1)]
        slot = 0 if oa == -1 else ca + 1
        dst = (halo.t_lo if ot == -1 else halo.t_hi).at[q, pl.ds(slot, 1)]
        move = (-oa, -ot)
    return src, dst, move


class Exchange:
    def __init__(self, pieces, field, halo, send_sem, recv_sem, pos, sizes, ca, ct):
        self.items = []
        self.pieces = pieces
        me_ax, me_az = pos
        n_ax, n_az = sizes
        for i, piece in enumerate(pieces):
            src, dst, (da, dt) = _piece_refs(piece, field, halo, ca, ct)
            to_ax = me_ax + da
            from_ax = me_ax - da
            to_dev = (to_ax, lax.rem(me_az + dt + n_az, n_az))
            from_dev = (from_ax, lax.rem(me_az - dt + n_az, n_az))
            send = pltpu.make_async_remote_copy(
                src_ref=src, dst_ref=dst, send_sem=send_sem.at[i], recv_sem=recv_sem.at[i],
                device_id=to_dev, device_id_type=MESH)
            recv = pltpu.make_async_remote_copy(
                src_ref=src, dst_ref=dst, send_sem=send_sem.at[i], recv_sem=recv_sem.at[i],
                device_id=from_dev, device_id_type=MESH)
            send_ok = jnp.logical_and(to_ax >= 0, to_ax < n_ax) if da != 0 else None
            recv_ok = jnp.logical_and(from_ax >= 0, from_ax < n_ax) if da != 0 else None
            self.items.append((send, recv, send_ok, recv_ok))

    @staticmethod
    def _maybe(ok, fn):
        if ok is None:
            fn()
        else:
            pl.when(ok)(fn)

    def start(self):
        for send, _, ok, _ in self.items:
            self._maybe(ok, send.start)

    def wait_recv(self, part=None):
        for (send, recv, _, ok), piece in zip(self.items, self.pieces):
            low = piece[1] == "t" or piece[2] == -1
            if part is None or (part == 0) == low:
                self._maybe(ok, recv.wait_recv)

    def wait_send(self):
        for send, _, ok, _ in self.items:
            self._maybe(ok, send.wait_send)


def _shift(own, halo, q, a, oa, ot, orr, lo_ok, hi_ok, ca, ct, nr, zero_r):
    ae = a + oa
    ok = None
    if ae < 0:
        slab = halo.a_lo[q, 0]
        ok = lo_ok
    elif ae >= ca:
        slab = halo.a_hi[q, 0]
        ok = hi_ok
    else:
        slab = own[q, ae]
    if ot != 0:
        rows = lax.broadcasted_iota(jnp.int32, (ct, nr), 0)
        if ot == -1:
            edge = halo.t_lo[q, ae + 1]
            slab = jnp.where(rows == 0, edge, pltpu.roll(slab, 1, 0))
        else:
            edge = halo.t_hi[q, ae + 1]
            slab = jnp.where(rows == ct - 1, edge, pltpu.roll(slab, ct - 1, 0))
    if orr != 0:
        lanes = lax.broadcasted_iota(jnp.int32, (ct, nr), 1)
        if orr == -1:
            slab = jnp.where(lanes == 0, zero_r, pltpu.roll(slab, 1, 1))
        else:
            slab = jnp.where(lanes == nr - 1, zero_r, pltpu.roll(slab, nr - 1, 1))
    if ok is not None:
        slab = jnp.where(ok, slab, zero_r)
    return slab


def _window_kernel(
    n_ax, n_az,
    init_hbm, seed_hbm, por_hbm, type_hbm, reg_hbm,
    final_ref, adj_ref, sens_ref, tot_ref,
    init_ref, seed_ref, por_ref, type_ref, reg_ref, load_sem,
    post0, state1, back1, post1, adj1, back0, gpor, fmask, sens1,
    pop_a_lo, pop_a_hi, pop_t_lo, pop_t_hi,
    ty_a_lo, ty_a_hi, ty_t_lo, ty_t_hi,
    send_sem, recv_sem, ty_send, ty_recv,
    part_ref, row_a, row_b, send_a, recv_a, send_b, recv_b, local,
):
    loads = [
        pltpu.make_async_copy(src, dst, load_sem.at[i])
        for i, (src, dst) in enumerate(
            ((type_hbm, type_ref), (seed_hbm, seed_ref), (init_hbm, init_ref),
             (por_hbm, por_ref), (reg_hbm, reg_ref)))
    ]
    for copy in loads:
        copy.start()
    _, ca, ct, nr = init_ref.shape
    me_ax, me_az = lax.axis_index("ax"), lax.axis_index("az")
    lo_ok = me_ax > 0
    hi_ok = me_ax < n_ax - 1
    pos, sizes = (me_ax, me_az), (n_ax, n_az)

    barrier = pltpu.get_barrier_semaphore()
    up_az, dn_az = lax.rem(me_az + 1, n_az), lax.rem(me_az + n_az - 1, n_az)
    for k in range(1, n_az):
        peer = me_az + k
        peer = jnp.where(peer >= n_az, peer - n_az, peer)
        pl.semaphore_signal(barrier, 1, device_id=(me_ax, peer), device_id_type=MESH)
    for k in range(1, n_ax):
        peer = me_ax + k
        peer = jnp.where(peer >= n_ax, peer - n_ax, peer)
        pl.semaphore_signal(barrier, 1, device_id=(peer, me_az), device_id_type=MESH)
    for ok, other in ((lo_ok, me_ax - 1), (hi_ok, me_ax + 1)):
        @pl.when(ok)
        def _():
            for dz in (up_az, dn_az):
                pl.semaphore_signal(barrier, 1, device_id=(other, dz), device_id_type=MESH)
    count = (n_az - 1) + (n_ax - 1) + 2 * (lo_ok.astype(jnp.int32) + hi_ok.astype(jnp.int32))
    for copy in loads[:1] + loads[2:]:
        copy.wait()

    def halo(k):
        return Halo(pop_a_lo.at[k], pop_a_hi.at[k], pop_t_lo.at[k], pop_t_hi.at[k])

    ty_halo = Halo(ty_a_lo, ty_a_hi, ty_t_lo, ty_t_hi)
    ex_types = Exchange(FLAG_PIECES, type_ref, ty_halo, ty_send, ty_recv, pos, sizes, ca, ct)
    ex_seed = Exchange(_pieces(1), seed_ref, halo(0), send_sem.at[0], recv_sem.at[0], pos, sizes, ca, ct)

    steps = ca * (ct // TILE)

    def tile_at(i):
        a = i // (ct // TILE)
        t0 = pl.multiple_of((i % (ct // TILE)) * TILE, TILE)
        return a, pl.ds(t0, TILE)

    def load(ref, a, ts):
        return [ref[q, a, ts, :] for q in range(NQ)]

    def store(ref, a, ts, vals):
        for q in range(NQ):
            ref[q, a, ts, :] = vals[q]

    def collide_loop(src, dst, grad_dst):
        def body(i, carry):
            a, ts = tile_at(i)
            out, grad = _collide(load(src, a, ts), por_ref[a, ts, :], type_ref[0, a, ts, :],
                                 reg_ref[a, ts, :], with_grad=True)
            store(dst, a, ts, out)
            store(grad_dst, a, ts, grad)
            return carry
        lax.fori_loop(0, steps, body, 0)

    def vjp_loop(at, upstream, primal_dst, grad_dst, sens_dst):
        def body(i, carry):
            a, ts = tile_at(i)
            types = type_ref[0, a, ts, :]
            regions = reg_ref[a, ts, :]
            out, pullback = jax.vjp(
                lambda f, p: _collide(f, p, types, regions), load(at, a, ts), por_ref[a, ts, :])
            if primal_dst is not None:
                store(primal_dst, a, ts, out)
            d_f, d_p = pullback(load(upstream, a, ts))
            store(grad_dst, a, ts, d_f)
            if sens_dst is not None:
                sens_dst[a, ts, :] = d_p
            return carry
        lax.fori_loop(0, steps, body, 0)

    zero = jnp.zeros((ct, nr), jnp.float32)

    def flag_shift(a, oa, ot, orr):
        if oa == 0 and ot == 0 and orr == 0:
            own = type_ref[0, a]
            return jnp.where(own != 1, 1.0, 0.0).astype(jnp.float32)
        ty = _shift(type_ref, ty_halo, 0, a, oa, ot, orr, lo_ok, hi_ok, ca, ct, nr, jnp.ones((ct, nr), jnp.int32))
        return jnp.where(ty != 1, 1.0, 0.0).astype(jnp.float32)

    def fill_masks():
        for a in range(ca):
            for q in range(NQ):
                c = VELOCITY[q]
                fmask[q, a] = flag_shift(a, -c[0], -c[1], -c[2])

    def stream(post, hal, dst, rows=None):
        for a in rows if rows is not None else range(ca):
            for q in range(NQ):
                c = VELOCITY[q]
                moved = _shift(post, hal, q, a, -c[0], -c[1], -c[2], lo_ok, hi_ok, ca, ct, nr, zero)
                ok = fmask[q, a] > 0
                dst[q, a] = jnp.where(ok, moved, post[OPPOSITE[q], a])

    def stream_adjoint(adj, hal, dst, rows=None):
        for a in rows if rows is not None else range(ca):
            centre = fmask[0, a]
            for q in range(NQ):
                c = VELOCITY[q]
                ahead = _shift(adj, hal, q, a, c[0], c[1], c[2], lo_ok, hi_ok, ca, ct, nr, zero)
                blocked = 1.0 - fmask[OPPOSITE[q], a]
                dst[q, a] = centre * ahead + blocked * adj[OPPOSITE[q], a]

    collide_loop(init_ref, post0, gpor)
    loads[1].wait()
    pl.semaphore_wait(barrier, count)
    ex_post0 = Exchange(_pieces(-1), post0, halo(1), send_sem.at[1], recv_sem.at[1], pos, sizes, ca, ct)
    ex_types.start()
    ex_post0.start()
    ex_seed.start()
    ex_types.wait_recv()
    fill_masks()
    ex_post0.wait_recv(0)
    stream(post0, halo(1), state1, [0])
    ex_post0.wait_recv(1)
    stream(post0, halo(1), state1, range(1, ca))
    ex_seed.wait_recv()
    stream_adjoint(seed_ref, halo(0), back1)
    vjp_loop(state1, back1, post1, adj1, sens1)
    ex_post1 = Exchange(_pieces(-1), post1, halo(2), send_sem.at[2], recv_sem.at[2], pos, sizes, ca, ct)
    ex_adj1 = Exchange(_pieces(1), adj1, halo(3), send_sem.at[3], recv_sem.at[3], pos, sizes, ca, ct)
    ex_adj1.start()
    ex_post1.start()
    ex_adj1.wait_recv(0)
    stream_adjoint(adj1, halo(3), back0, [0])
    ex_adj1.wait_recv(1)
    stream_adjoint(adj1, halo(3), back0, range(1, ca))
    for a in range(ca):
        sens0 = back0[0, a] * gpor[0, a]
        for q in range(1, NQ):
            sens0 = sens0 + back0[q, a] * gpor[q, a]
        sens_ref[a] = sens1[a] + sens0

    total = jnp.zeros((1, 1), jnp.float32)
    rid = jnp.zeros((1, 1), jnp.int32)
    for a in range(ca):
        reg = reg_ref[a]
        total = total + jnp.sum(jnp.where(reg > 0, sens_ref[a], 0.0), keepdims=True)
        rid = jnp.maximum(rid, jnp.max(reg, keepdims=True))
    labels = lax.broadcasted_iota(jnp.int32, part_ref.shape, 1) + 1
    part_ref[...] = jnp.where(labels == rid, total, 0.0)
    first = _TotalsStage(part_ref, row_a, send_a, recv_a, local.at[0], me_az, n_az,
                         lambda j: (me_ax, j))
    first.start()

    vjp_loop(init_ref, back0, None, adj_ref, None)
    ex_post1.wait_recv()
    stream(post1, halo(2), final_ref)

    first.finish(part_ref)
    own = pltpu.make_async_copy(part_ref, row_b.at[me_ax], local.at[1])
    own.start()
    own.wait()
    second = _TotalsStage(row_b.at[me_ax], row_b, send_b, recv_b, None, me_ax, n_ax,
                          lambda j: (j, me_az))
    second.start()
    second.finish(tot_ref)

    for ex in (ex_types, ex_seed, ex_post0, ex_post1, ex_adj1):
        ex.wait_send()


class _TotalsStage:
    def __init__(self, src, rows, send, recv, own_sem, me, n, device):
        self.src, self.rows, self.own_sem, self.me, self.n = src, rows, own_sem, me, n
        self.sends, self.recvs = [], []
        for k in range(1, n):
            to, frm = lax.rem(me + k, n), lax.rem(me + n - k, n)
            self.sends.append(pltpu.make_async_remote_copy(
                src_ref=src, dst_ref=rows.at[me], send_sem=send.at[k], recv_sem=recv.at[me],
                device_id=device(to), device_id_type=MESH))
            self.recvs.append(pltpu.make_async_remote_copy(
                src_ref=src, dst_ref=rows.at[frm], send_sem=send.at[k], recv_sem=recv.at[frm],
                device_id=device(frm), device_id_type=MESH))

    def start(self):
        self.own = None
        if self.own_sem is not None:
            self.own = pltpu.make_async_copy(self.src, self.rows.at[self.me], self.own_sem)
            self.own.start()
        for copy in self.sends:
            copy.start()

    def finish(self, out):
        if self.own is not None:
            self.own.wait()
        for copy in self.recvs:
            copy.wait_recv()
        acc = self.rows[0]
        for j in range(1, self.n):
            acc = acc + self.rows[j]
        for copy in self.sends:
            copy.wait_send()
        out[...] = acc


def window(initial, adjoint_seed, porosity, cell_type, region, n_regions):
    n_ax, n_az = lax.axis_size("ax"), lax.axis_size("az")
    nq, ca, ct, nr = initial.shape
    pop = jax.ShapeDtypeStruct(initial.shape, jnp.float32)
    cells = jax.ShapeDtypeStruct(porosity.shape, jnp.float32)
    vmem = pltpu.VMEM
    f32, i32 = jnp.float32, jnp.int32
    scratch = (
        [vmem(initial.shape, f32), vmem(initial.shape, f32), vmem(porosity.shape, f32),
         vmem((1,) + cell_type.shape, i32), vmem(region.shape, i32), pltpu.SemaphoreType.DMA((5,))]

        + [vmem((nq, ca, ct, nr), f32) for _ in range(8)]
        + [vmem((ca, ct, nr), f32)]
        + [vmem((4, nq, 1, ct, nr), f32), vmem((4, nq, 1, ct, nr), f32),
           vmem((4, nq, ca + 2, 1, nr), f32), vmem((4, nq, ca + 2, 1, nr), f32)]
        + [vmem((1, 1, ct, nr), i32), vmem((1, 1, ct, nr), i32),
           vmem((1, ca + 2, 1, nr), i32), vmem((1, ca + 2, 1, nr), i32)]
        + [pltpu.SemaphoreType.DMA((4, NPIECE)), pltpu.SemaphoreType.DMA((4, NPIECE)),
           pltpu.SemaphoreType.DMA((len(FLAG_PIECES),)), pltpu.SemaphoreType.DMA((len(FLAG_PIECES),))]
        + [vmem((1, n_regions), f32), vmem((n_az, 1, n_regions), f32), vmem((n_ax, 1, n_regions), f32),
           pltpu.SemaphoreType.DMA((n_az,)), pltpu.SemaphoreType.DMA((n_az,)),
           pltpu.SemaphoreType.DMA((n_ax,)), pltpu.SemaphoreType.DMA((n_ax,)),
           pltpu.SemaphoreType.DMA((2,))]
    )
    final, adj, sens, tot = pl.pallas_call(
        functools.partial(_window_kernel, n_ax, n_az),
        out_shape=(pop, pop, cells, jax.ShapeDtypeStruct((1, n_regions), f32)),
        in_specs=[pl.BlockSpec(memory_space=pltpu.HBM)] * 5,
        out_specs=(pl.BlockSpec(memory_space=vmem),) * 4,
        scratch_shapes=scratch,
        compiler_params=pltpu.CompilerParams(collective_id=1, has_side_effects=True,
                                             vmem_limit_bytes=67043328),
    )(initial, adjoint_seed, porosity, cell_type.reshape((1,) + cell_type.shape), region)
    return final, adj, sens, tot


def shards(initial, adjoint_seed, porosity, cell_type, region):
    n_regions = lax.axis_size("ax") * lax.axis_size("az") // 4
    final, adjoint, sensitivity, totals = window(
        initial, adjoint_seed, porosity, cell_type, region, n_regions)
    totals = totals.reshape(-1)
    return (final, adjoint, sensitivity, totals)


def solution(mesh):
    return jax.shard_map(
        shards,
        mesh=mesh,
        in_specs=(
            P(None, "ax", "az", None),
            P(None, "ax", "az", None),
            P("ax", "az", None),
            P("ax", "az", None),
            P("ax", "az", None),
        ),
        out_specs=(P(None, "ax", "az", None), P(None, "ax", "az", None), P("ax", "az", None), P()),
        check_vma=False,
    )
```

```python
import functools

import numpy as np

import jax
import jax.numpy as jnp
from jax import lax
from jax.experimental import pallas as pl
from jax.experimental.pallas import tpu as pltpu
from jax.sharding import PartitionSpec as P

MESH = pl.DeviceIdType.MESH

VELOCITY = [
    (0, 0, 0),
    (1, 0, 0),
    (-1, 0, 0),
    (0, 1, 0),
    (0, -1, 0),
    (0, 0, 1),
    (0, 0, -1),
    (1, 1, 0),
    (-1, -1, 0),
    (1, -1, 0),
    (-1, 1, 0),
    (1, 0, 1),
    (-1, 0, -1),
    (1, 0, -1),
    (-1, 0, 1),
    (0, 1, 1),
    (0, -1, -1),
    (0, 1, -1),
    (0, -1, 1),
]
OPPOSITE = [0, 2, 1, 4, 3, 6, 5, 8, 7, 10, 9, 12, 11, 14, 13, 16, 15, 18, 17]
WEIGHTS = [1.0 / 3.0] + [1.0 / 18.0] * 6 + [1.0 / 36.0] * 12
INLET_SPEED = (0.05, 0.05, 0.0)
NQ = 19
TILE = 8


def _inflow_constants():
    w = np.array(WEIGHTS, np.float32)
    u = np.array(INLET_SPEED, np.float32)
    c = np.array(VELOCITY, np.float32)
    proj = (c * u[None, :]).sum(1, dtype=np.float32).astype(np.float32)
    usq = np.float32((u * u).sum(dtype=np.float32))
    one = np.float32(1.0)
    val = w * one * (one + np.float32(3.0) * proj + np.float32(4.5) * proj * proj - np.float32(1.5) * usq)
    return [float(v) for v in val.astype(np.float32)]


INFLOW = _inflow_constants()


def _combo(values, coeffs):
    acc = None
    for v, c in zip(values, coeffs):
        if c == 0:
            continue
        term = v if c == 1 else (-v if c == -1 else c * v)
        acc = term if acc is None else acc + term
    return acc


def _equilibrium(rho, u):
    usq = u[0] * u[0] + u[1] * u[1] + u[2] * u[2]
    out = []
    for q in range(NQ):
        p = _combo(u, VELOCITY[q])
        if p is None:
            inner = 1.0 - 1.5 * usq
        else:
            inner = 1.0 + 3.0 * p + 4.5 * p * p - 1.5 * usq
        out.append(WEIGHTS[q] * rho * inner)
    return out


def _collide(f, porous, types, regions, with_grad=False):
    rho = f[0]
    for q in range(1, NQ):
        rho = rho + f[q]
    u = [_combo(f, [VELOCITY[q][k] for q in range(NQ)]) / rho for k in range(3)]
    feq = _equilibrium(rho, u)
    g = [f[q] - feq[q] for q in range(NQ)]
    moments = []
    for a, b in ((0, 0), (1, 1), (2, 2), (0, 1), (0, 2), (1, 2)):
        moments.append(_combo(g, [VELOCITY[q][a] * VELOCITY[q][b] for q in range(NQ)]))
    stress_sq = (
        moments[0] * moments[0]
        + moments[1] * moments[1]
        + moments[2] * moments[2]
        + 2.0 * (moments[3] * moments[3] + moments[4] * moments[4] + moments[5] * moments[5])
    )
    shear = 1.5 * jnp.sqrt(stress_sq + 0.0001) / rho
    viscous = 0.02 * (shear + 0.01) ** (0.7 - 1.0)
    relax = 0.5 + 3.0 * viscous
    design = jnp.where(regions > 0, 1.0, 0.0).astype(jnp.float32)
    damp = porous * design
    outflow = _equilibrium(jnp.ones_like(rho), u)
    inlet = types == 2
    outlet = types == 3
    out = []
    for q in range(NQ):
        relaxed = f[q] - g[q] / relax - damp * (feq[q] - WEIGHTS[q] * rho)
        out.append(jnp.where(inlet, INFLOW[q], jnp.where(outlet, outflow[q], relaxed)))
    if not with_grad:
        return out
    fixed = jnp.logical_or(inlet, outlet)
    grad = [jnp.where(fixed, 0.0, -design * (feq[q] - WEIGHTS[q] * rho)) for q in range(NQ)]
    return out, grad


def _pieces(sign):
    out = []
    for q in range(NQ):
        oa, ot = sign * VELOCITY[q][0], sign * VELOCITY[q][1]
        if oa != 0:
            out.append((q, "a", oa, ot))
        if ot != 0:
            out.append((q, "t", oa, ot))
        if oa != 0 and ot != 0:
            out.append((q, "c", oa, ot))
    return out


FLAG_PIECES = [
    (0, "a", 1, 0),
    (0, "a", -1, 0),
    (0, "t", 0, 1),
    (0, "t", 0, -1),
    (0, "c", 1, 1),
    (0, "c", 1, -1),
    (0, "c", -1, 1),
    (0, "c", -1, -1),
]
NPIECE = 24


class Halo:
    def __init__(self, a_lo, a_hi, t_lo, t_hi):
        self.a_lo, self.a_hi, self.t_lo, self.t_hi = a_lo, a_hi, t_lo, t_hi


def _piece_refs(piece, field, halo, ca, ct):
    q, kind, oa, ot = piece
    a_face = ca - 1 if oa == -1 else 0
    t_face = ct - 1 if ot == -1 else 0
    if kind == "a":
        src = field.at[q, pl.ds(a_face, 1)]
        dst = (halo.a_lo if oa == -1 else halo.a_hi).at[q]
        move = (-oa, 0)
    elif kind == "t":
        src = field.at[q, :, pl.ds(t_face, 1)]
        dst = (halo.t_lo if ot == -1 else halo.t_hi).at[q, pl.ds(1, ca)]
        move = (0, -ot)
    else:
        src = field.at[q, pl.ds(a_face, 1), pl.ds(t_face, 1)]
        slot = 0 if oa == -1 else ca + 1
        dst = (halo.t_lo if ot == -1 else halo.t_hi).at[q, pl.ds(slot, 1)]
        move = (-oa, -ot)
    return src, dst, move


class Exchange:
    def __init__(self, pieces, field, halo, send_sem, recv_sem, pos, sizes, ca, ct):
        self.items = []
        self.pieces = pieces
        me_ax, me_az = pos
        n_ax, n_az = sizes
        for i, piece in enumerate(pieces):
            src, dst, (da, dt) = _piece_refs(piece, field, halo, ca, ct)
            to_ax = me_ax + da
            from_ax = me_ax - da
            to_dev = (to_ax, lax.rem(me_az + dt + n_az, n_az))
            from_dev = (from_ax, lax.rem(me_az - dt + n_az, n_az))
            send = pltpu.make_async_remote_copy(
                src_ref=src, dst_ref=dst, send_sem=send_sem.at[i], recv_sem=recv_sem.at[i],
                device_id=to_dev, device_id_type=MESH)
            recv = pltpu.make_async_remote_copy(
                src_ref=src, dst_ref=dst, send_sem=send_sem.at[i], recv_sem=recv_sem.at[i],
                device_id=from_dev, device_id_type=MESH)
            send_ok = jnp.logical_and(to_ax >= 0, to_ax < n_ax) if da != 0 else None
            recv_ok = jnp.logical_and(from_ax >= 0, from_ax < n_ax) if da != 0 else None
            self.items.append((send, recv, send_ok, recv_ok))

    @staticmethod
    def _maybe(ok, fn):
        if ok is None:
            fn()
        else:
            pl.when(ok)(fn)

    def start(self):
        for send, _, ok, _ in self.items:
            self._maybe(ok, send.start)

    def wait_recv(self, part=None):
        for (send, recv, _, ok), piece in zip(self.items, self.pieces):
            low = piece[1] == "t" or piece[2] == -1
            if part is None or (part == 0) == low:
                self._maybe(ok, recv.wait_recv)

    def wait_send(self):
        for send, _, ok, _ in self.items:
            self._maybe(ok, send.wait_send)


def _shift(own, halo, q, a, oa, ot, orr, lo_ok, hi_ok, ca, ct, nr, zero_r):
    ae = a + oa
    ok = None
    if ae < 0:
        slab = halo.a_lo[q, 0]
        ok = lo_ok
    elif ae >= ca:
        slab = halo.a_hi[q, 0]
        ok = hi_ok
    else:
        slab = own[q, ae]
    if ot != 0:
        rows = lax.broadcasted_iota(jnp.int32, (ct, nr), 0)
        if ot == -1:
            edge = halo.t_lo[q, ae + 1]
            slab = jnp.where(rows == 0, edge, pltpu.roll(slab, 1, 0))
        else:
            edge = halo.t_hi[q, ae + 1]
            slab = jnp.where(rows == ct - 1, edge, pltpu.roll(slab, ct - 1, 0))
    if orr != 0:
        lanes = lax.broadcasted_iota(jnp.int32, (ct, nr), 1)
        if orr == -1:
            slab = jnp.where(lanes == 0, zero_r, pltpu.roll(slab, 1, 1))
        else:
            slab = jnp.where(lanes == nr - 1, zero_r, pltpu.roll(slab, nr - 1, 1))
    if ok is not None:
        slab = jnp.where(ok, slab, zero_r)
    return slab


def _window_kernel(
    n_ax, n_az,
    init_hbm, seed_hbm, por_hbm, type_hbm, reg_hbm,
    final_ref, adj_ref, sens_ref, tot_ref,
    init_ref, seed_ref, por_ref, type_ref, reg_ref, load_sem,
    post0, state1, back1, post1, adj1, back0, gpor, fmask, sens1,
    pop_a_lo, pop_a_hi, pop_t_lo, pop_t_hi,
    ty_a_lo, ty_a_hi, ty_t_lo, ty_t_hi,
    send_sem, recv_sem, ty_send, ty_recv,
    part_ref, row_a, row_b, send_a, recv_a, send_b, recv_b, local,
):
    loads = [
        pltpu.make_async_copy(src, dst, load_sem.at[i])
        for i, (src, dst) in enumerate(
            ((type_hbm, type_ref), (seed_hbm, seed_ref), (init_hbm, init_ref),
             (por_hbm, por_ref), (reg_hbm, reg_ref)))
    ]
    for copy in loads:
        copy.start()
    _, ca, ct, nr = init_ref.shape
    me_ax, me_az = lax.axis_index("ax"), lax.axis_index("az")
    lo_ok = me_ax > 0
    hi_ok = me_ax < n_ax - 1
    pos, sizes = (me_ax, me_az), (n_ax, n_az)

    barrier = pltpu.get_barrier_semaphore()
    up_az, dn_az = lax.rem(me_az + 1, n_az), lax.rem(me_az + n_az - 1, n_az)
    for k in range(1, n_az):
        peer = me_az + k
        peer = jnp.where(peer >= n_az, peer - n_az, peer)
        pl.semaphore_signal(barrier, 1, device_id=(me_ax, peer), device_id_type=MESH)
    for k in range(1, n_ax):
        peer = me_ax + k
        peer = jnp.where(peer >= n_ax, peer - n_ax, peer)
        pl.semaphore_signal(barrier, 1, device_id=(peer, me_az), device_id_type=MESH)
    for ok, other in ((lo_ok, me_ax - 1), (hi_ok, me_ax + 1)):
        @pl.when(ok)
        def _():
            for dz in (up_az, dn_az):
                pl.semaphore_signal(barrier, 1, device_id=(other, dz), device_id_type=MESH)
    count = (n_az - 1) + (n_ax - 1) + 2 * (lo_ok.astype(jnp.int32) + hi_ok.astype(jnp.int32))
    for copy in loads[:1] + loads[2:]:
        copy.wait()

    def halo(k):
        return Halo(pop_a_lo.at[k], pop_a_hi.at[k], pop_t_lo.at[k], pop_t_hi.at[k])

    ty_halo = Halo(ty_a_lo, ty_a_hi, ty_t_lo, ty_t_hi)
    ex_types = Exchange(FLAG_PIECES, type_ref, ty_halo, ty_send, ty_recv, pos, sizes, ca, ct)
    ex_seed = Exchange(_pieces(1), seed_ref, halo(0), send_sem.at[0], recv_sem.at[0], pos, sizes, ca, ct)

    steps = ca * (ct // TILE)

    def tile_at(i):
        a = i // (ct // TILE)
        t0 = pl.multiple_of((i % (ct // TILE)) * TILE, TILE)
        return a, pl.ds(t0, TILE)

    def load(ref, a, ts):
        return [ref[q, a, ts, :] for q in range(NQ)]

    def store(ref, a, ts, vals):
        for q in range(NQ):
            ref[q, a, ts, :] = vals[q]

    def collide_loop(src, dst, grad_dst):
        def body(i, carry):
            a, ts = tile_at(i)
            out, grad = _collide(load(src, a, ts), por_ref[a, ts, :], type_ref[0, a, ts, :],
                                 reg_ref[a, ts, :], with_grad=True)
            store(dst, a, ts, out)
            store(grad_dst, a, ts, grad)
            return carry
        lax.fori_loop(0, steps, body, 0)

    def vjp_loop(at, upstream, primal_dst, grad_dst, sens_dst):
        def body(i, carry):
            a, ts = tile_at(i)
            types = type_ref[0, a, ts, :]
            regions = reg_ref[a, ts, :]
            out, pullback = jax.vjp(
                lambda f, p: _collide(f, p, types, regions), load(at, a, ts), por_ref[a, ts, :])
            if primal_dst is not None:
                store(primal_dst, a, ts, out)
            d_f, d_p = pullback(load(upstream, a, ts))
            store(grad_dst, a, ts, d_f)
            if sens_dst is not None:
                sens_dst[a, ts, :] = d_p
            return carry
        lax.fori_loop(0, steps, body, 0)

    zero = jnp.zeros((ct, nr), jnp.float32)

    def flag_shift(a, oa, ot, orr):
        if oa == 0 and ot == 0 and orr == 0:
            own = type_ref[0, a]
            return jnp.where(own != 1, 1.0, 0.0).astype(jnp.float32)
        ty = _shift(type_ref, ty_halo, 0, a, oa, ot, orr, lo_ok, hi_ok, ca, ct, nr, jnp.ones((ct, nr), jnp.int32))
        return jnp.where(ty != 1, 1.0, 0.0).astype(jnp.float32)

    def fill_masks():
        for a in range(ca):
            for q in range(NQ):
                c = VELOCITY[q]
                fmask[q, a] = flag_shift(a, -c[0], -c[1], -c[2])

    def stream(post, hal, dst, rows=None):
        for a in rows if rows is not None else range(ca):
            for q in range(NQ):
                c = VELOCITY[q]
                moved = _shift(post, hal, q, a, -c[0], -c[1], -c[2], lo_ok, hi_ok, ca, ct, nr, zero)
                ok = fmask[q, a] > 0
                dst[q, a] = jnp.where(ok, moved, post[OPPOSITE[q], a])

    def stream_adjoint(adj, hal, dst, rows=None):
        for a in rows if rows is not None else range(ca):
            centre = fmask[0, a]
            for q in range(NQ):
                c = VELOCITY[q]
                ahead = _shift(adj, hal, q, a, c[0], c[1], c[2], lo_ok, hi_ok, ca, ct, nr, zero)
                blocked = 1.0 - fmask[OPPOSITE[q], a]
                dst[q, a] = centre * ahead + blocked * adj[OPPOSITE[q], a]

    collide_loop(init_ref, post0, gpor)
    loads[1].wait()
    pl.semaphore_wait(barrier, count)
    ex_post0 = Exchange(_pieces(-1), post0, halo(1), send_sem.at[1], recv_sem.at[1], pos, sizes, ca, ct)
    ex_types.start()
    ex_post0.start()
    ex_seed.start()
    ex_types.wait_recv()
    fill_masks()
    ex_post0.wait_recv(0)
    stream(post0, halo(1), state1, [0])
    ex_post0.wait_recv(1)
    stream(post0, halo(1), state1, range(1, ca))
    ex_seed.wait_recv()
    stream_adjoint(seed_ref, halo(0), back1)
    vjp_loop(state1, back1, post1, adj1, sens1)
    ex_post1 = Exchange(_pieces(-1), post1, halo(2), send_sem.at[2], recv_sem.at[2], pos, sizes, ca, ct)
    ex_adj1 = Exchange(_pieces(1), adj1, halo(3), send_sem.at[3], recv_sem.at[3], pos, sizes, ca, ct)
    ex_adj1.start()
    ex_post1.start()
    ex_adj1.wait_recv(0)
    stream_adjoint(adj1, halo(3), back0, [0])
    ex_adj1.wait_recv(1)
    stream_adjoint(adj1, halo(3), back0, range(1, ca))
    for a in range(ca):
        sens0 = back0[0, a] * gpor[0, a]
        for q in range(1, NQ):
            sens0 = sens0 + back0[q, a] * gpor[q, a]
        sens_ref[a] = sens1[a] + sens0

    total = jnp.zeros((1, 1), jnp.float32)
    rid = jnp.zeros((1, 1), jnp.int32)
    for a in range(ca):
        reg = reg_ref[a]
        total = total + jnp.sum(jnp.where(reg > 0, sens_ref[a], 0.0), keepdims=True)
        rid = jnp.maximum(rid, jnp.max(reg, keepdims=True))
    labels = lax.broadcasted_iota(jnp.int32, part_ref.shape, 1) + 1
    part_ref[...] = jnp.where(labels == rid, total, 0.0)
    first = _TotalsStage(part_ref, row_b, send_b, recv_b, local.at[0], me_ax, n_ax,
                         lambda j: (j, me_az))
    first.start()

    vjp_loop(init_ref, back0, None, adj_ref, None)
    ex_post1.wait_recv()
    stream(post1, halo(2), final_ref)

    first.finish(part_ref)
    own = pltpu.make_async_copy(part_ref, row_a.at[me_az], local.at[1])
    own.start()
    own.wait()
    second = _TotalsStage(row_a.at[me_az], row_a, send_a, recv_a, None, me_az, n_az,
                          lambda j: (me_ax, j))
    second.start()
    second.finish(tot_ref)

    for ex in (ex_types, ex_seed, ex_post0, ex_post1, ex_adj1):
        ex.wait_send()


class _TotalsStage:
    def __init__(self, src, rows, send, recv, own_sem, me, n, device):
        self.src, self.rows, self.own_sem, self.me, self.n = src, rows, own_sem, me, n
        self.sends, self.recvs = [], []
        for k in range(1, n):
            to, frm = lax.rem(me + k, n), lax.rem(me + n - k, n)
            self.sends.append(pltpu.make_async_remote_copy(
                src_ref=src, dst_ref=rows.at[me], send_sem=send.at[k], recv_sem=recv.at[me],
                device_id=device(to), device_id_type=MESH))
            self.recvs.append(pltpu.make_async_remote_copy(
                src_ref=src, dst_ref=rows.at[frm], send_sem=send.at[k], recv_sem=recv.at[frm],
                device_id=device(frm), device_id_type=MESH))

    def start(self):
        self.own = None
        if self.own_sem is not None:
            self.own = pltpu.make_async_copy(self.src, self.rows.at[self.me], self.own_sem)
            self.own.start()
        for copy in self.sends:
            copy.start()

    def finish(self, out):
        if self.own is not None:
            self.own.wait()
        for copy in self.recvs:
            copy.wait_recv()
        acc = self.rows[0]
        for j in range(1, self.n):
            acc = acc + self.rows[j]
        for copy in self.sends:
            copy.wait_send()
        out[...] = acc


def window(initial, adjoint_seed, porosity, cell_type, region, n_regions):
    n_ax, n_az = lax.axis_size("ax"), lax.axis_size("az")
    nq, ca, ct, nr = initial.shape
    pop = jax.ShapeDtypeStruct(initial.shape, jnp.float32)
    cells = jax.ShapeDtypeStruct(porosity.shape, jnp.float32)
    vmem = pltpu.VMEM
    f32, i32 = jnp.float32, jnp.int32
    scratch = (
        [vmem(initial.shape, f32), vmem(initial.shape, f32), vmem(porosity.shape, f32),
         vmem((1,) + cell_type.shape, i32), vmem(region.shape, i32), pltpu.SemaphoreType.DMA((5,))]

        + [vmem((nq, ca, ct, nr), f32) for _ in range(8)]
        + [vmem((ca, ct, nr), f32)]
        + [vmem((4, nq, 1, ct, nr), f32), vmem((4, nq, 1, ct, nr), f32),
           vmem((4, nq, ca + 2, 1, nr), f32), vmem((4, nq, ca + 2, 1, nr), f32)]
        + [vmem((1, 1, ct, nr), i32), vmem((1, 1, ct, nr), i32),
           vmem((1, ca + 2, 1, nr), i32), vmem((1, ca + 2, 1, nr), i32)]
        + [pltpu.SemaphoreType.DMA((4, NPIECE)), pltpu.SemaphoreType.DMA((4, NPIECE)),
           pltpu.SemaphoreType.DMA((len(FLAG_PIECES),)), pltpu.SemaphoreType.DMA((len(FLAG_PIECES),))]
        + [vmem((1, n_regions), f32), vmem((n_az, 1, n_regions), f32), vmem((n_ax, 1, n_regions), f32),
           pltpu.SemaphoreType.DMA((n_az,)), pltpu.SemaphoreType.DMA((n_az,)),
           pltpu.SemaphoreType.DMA((n_ax,)), pltpu.SemaphoreType.DMA((n_ax,)),
           pltpu.SemaphoreType.DMA((2,))]
    )
    final, adj, sens, tot = pl.pallas_call(
        functools.partial(_window_kernel, n_ax, n_az),
        out_shape=(pop, pop, cells, jax.ShapeDtypeStruct((1, n_regions), f32)),
        in_specs=[pl.BlockSpec(memory_space=pltpu.HBM)] * 5,
        out_specs=(pl.BlockSpec(memory_space=vmem),) * 4,
        scratch_shapes=scratch,
        compiler_params=pltpu.CompilerParams(collective_id=1, has_side_effects=True,
                                             vmem_limit_bytes=67043328),
    )(initial, adjoint_seed, porosity, cell_type.reshape((1,) + cell_type.shape), region)
    return final, adj, sens, tot


def shards(initial, adjoint_seed, porosity, cell_type, region):
    n_regions = lax.axis_size("ax") * lax.axis_size("az") // 4
    final, adjoint, sensitivity, totals = window(
        initial, adjoint_seed, porosity, cell_type, region, n_regions)
    totals = totals.reshape(-1)
    return (final, adjoint, sensitivity, totals)


def solution(mesh):
    return jax.shard_map(
        shards,
        mesh=mesh,
        in_specs=(
            P(None, "ax", "az", None),
            P(None, "ax", "az", None),
            P("ax", "az", None),
            P("ax", "az", None),
            P("ax", "az", None),
        ),
        out_specs=(P(None, "ax", "az", None), P(None, "ax", "az", None), P("ax", "az", None), P()),
        check_vma=False,
    )
```

```python
import functools

import numpy as np

import jax
import jax.numpy as jnp
from jax import lax
from jax.experimental import pallas as pl
from jax.experimental.pallas import tpu as pltpu
from jax.sharding import PartitionSpec as P

MESH = pl.DeviceIdType.MESH

VELOCITY = [
    (0, 0, 0),
    (1, 0, 0),
    (-1, 0, 0),
    (0, 1, 0),
    (0, -1, 0),
    (0, 0, 1),
    (0, 0, -1),
    (1, 1, 0),
    (-1, -1, 0),
    (1, -1, 0),
    (-1, 1, 0),
    (1, 0, 1),
    (-1, 0, -1),
    (1, 0, -1),
    (-1, 0, 1),
    (0, 1, 1),
    (0, -1, -1),
    (0, 1, -1),
    (0, -1, 1),
]
OPPOSITE = [0, 2, 1, 4, 3, 6, 5, 8, 7, 10, 9, 12, 11, 14, 13, 16, 15, 18, 17]
WEIGHTS = [1.0 / 3.0] + [1.0 / 18.0] * 6 + [1.0 / 36.0] * 12
INLET_SPEED = (0.05, 0.05, 0.0)
NQ = 19
TILE = 8


def _inflow_constants():
    w = np.array(WEIGHTS, np.float32)
    u = np.array(INLET_SPEED, np.float32)
    c = np.array(VELOCITY, np.float32)
    proj = (c * u[None, :]).sum(1, dtype=np.float32).astype(np.float32)
    usq = np.float32((u * u).sum(dtype=np.float32))
    one = np.float32(1.0)
    val = w * one * (one + np.float32(3.0) * proj + np.float32(4.5) * proj * proj - np.float32(1.5) * usq)
    return [float(v) for v in val.astype(np.float32)]


INFLOW = _inflow_constants()


def _combo(values, coeffs):
    acc = None
    for v, c in zip(values, coeffs):
        if c == 0:
            continue
        term = v if c == 1 else (-v if c == -1 else c * v)
        acc = term if acc is None else acc + term
    return acc


def _equilibrium(rho, u):
    usq = u[0] * u[0] + u[1] * u[1] + u[2] * u[2]
    out = []
    for q in range(NQ):
        p = _combo(u, VELOCITY[q])
        if p is None:
            inner = 1.0 - 1.5 * usq
        else:
            inner = 1.0 + 3.0 * p + 4.5 * p * p - 1.5 * usq
        out.append(WEIGHTS[q] * rho * inner)
    return out


def _collide(f, porous, types, regions, with_grad=False):
    rho = f[0]
    for q in range(1, NQ):
        rho = rho + f[q]
    u = [_combo(f, [VELOCITY[q][k] for q in range(NQ)]) / rho for k in range(3)]
    feq = _equilibrium(rho, u)
    g = [f[q] - feq[q] for q in range(NQ)]
    moments = []
    for a, b in ((0, 0), (1, 1), (2, 2), (0, 1), (0, 2), (1, 2)):
        moments.append(_combo(g, [VELOCITY[q][a] * VELOCITY[q][b] for q in range(NQ)]))
    stress_sq = (
        moments[0] * moments[0]
        + moments[1] * moments[1]
        + moments[2] * moments[2]
        + 2.0 * (moments[3] * moments[3] + moments[4] * moments[4] + moments[5] * moments[5])
    )
    shear = 1.5 * jnp.sqrt(stress_sq + 0.0001) / rho
    viscous = 0.02 * (shear + 0.01) ** (0.7 - 1.0)
    relax = 0.5 + 3.0 * viscous
    design = jnp.where(regions > 0, 1.0, 0.0).astype(jnp.float32)
    damp = porous * design
    outflow = _equilibrium(jnp.ones_like(rho), u)
    inlet = types == 2
    outlet = types == 3
    out = []
    for q in range(NQ):
        relaxed = f[q] - g[q] / relax - damp * (feq[q] - WEIGHTS[q] * rho)
        out.append(jnp.where(inlet, INFLOW[q], jnp.where(outlet, outflow[q], relaxed)))
    if not with_grad:
        return out
    fixed = jnp.logical_or(inlet, outlet)
    grad = [jnp.where(fixed, 0.0, -design * (feq[q] - WEIGHTS[q] * rho)) for q in range(NQ)]
    return out, grad


def _pieces(sign):
    out = []
    for q in range(NQ):
        oa, ot = sign * VELOCITY[q][0], sign * VELOCITY[q][1]
        if oa != 0:
            out.append((q, "a", oa, ot))
        if ot != 0:
            out.append((q, "t", oa, ot))
        if oa != 0 and ot != 0:
            out.append((q, "c", oa, ot))
    return out


FLAG_PIECES = [
    (0, "a", 1, 0),
    (0, "a", -1, 0),
    (0, "t", 0, 1),
    (0, "t", 0, -1),
    (0, "c", 1, 1),
    (0, "c", 1, -1),
    (0, "c", -1, 1),
    (0, "c", -1, -1),
]
NPIECE = 24


class Halo:
    def __init__(self, a_lo, a_hi, t_lo, t_hi):
        self.a_lo, self.a_hi, self.t_lo, self.t_hi = a_lo, a_hi, t_lo, t_hi


def _piece_refs(piece, field, halo, ca, ct):
    q, kind, oa, ot = piece
    a_face = ca - 1 if oa == -1 else 0
    t_face = ct - 1 if ot == -1 else 0
    if kind == "a":
        src = field.at[q, pl.ds(a_face, 1)]
        dst = (halo.a_lo if oa == -1 else halo.a_hi).at[q]
        move = (-oa, 0)
    elif kind == "t":
        src = field.at[q, :, pl.ds(t_face, 1)]
        dst = (halo.t_lo if ot == -1 else halo.t_hi).at[q, pl.ds(1, ca)]
        move = (0, -ot)
    else:
        src = field.at[q, pl.ds(a_face, 1), pl.ds(t_face, 1)]
        slot = 0 if oa == -1 else ca + 1
        dst = (halo.t_lo if ot == -1 else halo.t_hi).at[q, pl.ds(slot, 1)]
        move = (-oa, -ot)
    return src, dst, move


class Exchange:
    def __init__(self, pieces, field, halo, send_sem, recv_sem, pos, sizes, ca, ct):
        self.items = []
        self.pieces = pieces
        me_ax, me_az = pos
        n_ax, n_az = sizes
        for i, piece in enumerate(pieces):
            src, dst, (da, dt) = _piece_refs(piece, field, halo, ca, ct)
            to_ax = me_ax + da
            from_ax = me_ax - da
            to_dev = (to_ax, lax.rem(me_az + dt + n_az, n_az))
            from_dev = (from_ax, lax.rem(me_az - dt + n_az, n_az))
            send = pltpu.make_async_remote_copy(
                src_ref=src, dst_ref=dst, send_sem=send_sem.at[i], recv_sem=recv_sem.at[i],
                device_id=to_dev, device_id_type=MESH)
            recv = pltpu.make_async_remote_copy(
                src_ref=src, dst_ref=dst, send_sem=send_sem.at[i], recv_sem=recv_sem.at[i],
                device_id=from_dev, device_id_type=MESH)
            send_ok = jnp.logical_and(to_ax >= 0, to_ax < n_ax) if da != 0 else None
            recv_ok = jnp.logical_and(from_ax >= 0, from_ax < n_ax) if da != 0 else None
            self.items.append((send, recv, send_ok, recv_ok))

    @staticmethod
    def _maybe(ok, fn):
        if ok is None:
            fn()
        else:
            pl.when(ok)(fn)

    def start(self):
        for send, _, ok, _ in self.items:
            self._maybe(ok, send.start)

    def wait_recv(self, part=None):
        for (send, recv, _, ok), piece in zip(self.items, self.pieces):
            low = piece[1] == "t" or piece[2] == -1
            if part is None or (part == 0) == low:
                self._maybe(ok, recv.wait_recv)

    def wait_send(self):
        for send, _, ok, _ in self.items:
            self._maybe(ok, send.wait_send)


def _shift(own, halo, q, a, oa, ot, orr, lo_ok, hi_ok, ca, ct, nr, zero_r):
    ae = a + oa
    ok = None
    if ae < 0:
        slab = halo.a_lo[q, 0]
        ok = lo_ok
    elif ae >= ca:
        slab = halo.a_hi[q, 0]
        ok = hi_ok
    else:
        slab = own[q, ae]
    if ot != 0:
        rows = lax.broadcasted_iota(jnp.int32, (ct, nr), 0)
        if ot == -1:
            edge = halo.t_lo[q, ae + 1]
            slab = jnp.where(rows == 0, edge, pltpu.roll(slab, 1, 0))
        else:
            edge = halo.t_hi[q, ae + 1]
            slab = jnp.where(rows == ct - 1, edge, pltpu.roll(slab, ct - 1, 0))
    if orr != 0:
        lanes = lax.broadcasted_iota(jnp.int32, (ct, nr), 1)
        if orr == -1:
            slab = jnp.where(lanes == 0, zero_r, pltpu.roll(slab, 1, 1))
        else:
            slab = jnp.where(lanes == nr - 1, zero_r, pltpu.roll(slab, nr - 1, 1))
    if ok is not None:
        slab = jnp.where(ok, slab, zero_r)
    return slab


def _window_kernel(
    n_ax, n_az,
    init_hbm, seed_hbm, por_hbm, type_hbm, reg_hbm,
    final_ref, adj_ref, sens_ref, tot_ref,
    init_ref, seed_ref, por_ref, type_ref, reg_ref, load_sem,
    post0, state1, back1, post1, adj1, back0, gpor, fmask, sens1,
    pop_a_lo, pop_a_hi, pop_t_lo, pop_t_hi,
    ty_a_lo, ty_a_hi, ty_t_lo, ty_t_hi,
    send_sem, recv_sem, ty_send, ty_recv,
    part_ref, row_a, row_b, send_a, recv_a, send_b, recv_b, local,
):
    loads = [
        pltpu.make_async_copy(src, dst, load_sem.at[i])
        for i, (src, dst) in enumerate(
            ((type_hbm, type_ref), (seed_hbm, seed_ref), (init_hbm, init_ref),
             (por_hbm, por_ref), (reg_hbm, reg_ref)))
    ]
    for copy in loads:
        copy.start()
    _, ca, ct, nr = init_ref.shape
    me_ax, me_az = lax.axis_index("ax"), lax.axis_index("az")
    lo_ok = me_ax > 0
    hi_ok = me_ax < n_ax - 1
    pos, sizes = (me_ax, me_az), (n_ax, n_az)

    barrier = pltpu.get_barrier_semaphore()
    up_az, dn_az = lax.rem(me_az + 1, n_az), lax.rem(me_az + n_az - 1, n_az)
    for k in range(1, n_az):
        peer = me_az + k
        peer = jnp.where(peer >= n_az, peer - n_az, peer)
        pl.semaphore_signal(barrier, 1, device_id=(me_ax, peer), device_id_type=MESH)
    for k in range(1, n_ax):
        peer = me_ax + k
        peer = jnp.where(peer >= n_ax, peer - n_ax, peer)
        pl.semaphore_signal(barrier, 1, device_id=(peer, me_az), device_id_type=MESH)
    for ok, other in ((lo_ok, me_ax - 1), (hi_ok, me_ax + 1)):
        @pl.when(ok)
        def _():
            for dz in (up_az, dn_az):
                pl.semaphore_signal(barrier, 1, device_id=(other, dz), device_id_type=MESH)
    count = (n_az - 1) + (n_ax - 1) + 2 * (lo_ok.astype(jnp.int32) + hi_ok.astype(jnp.int32))
    for copy in loads[:1] + loads[2:]:
        copy.wait()

    def halo(k):
        return Halo(pop_a_lo.at[k], pop_a_hi.at[k], pop_t_lo.at[k], pop_t_hi.at[k])

    ty_halo = Halo(ty_a_lo, ty_a_hi, ty_t_lo, ty_t_hi)
    ex_types = Exchange(FLAG_PIECES, type_ref, ty_halo, ty_send, ty_recv, pos, sizes, ca, ct)
    ex_seed = Exchange(_pieces(1), seed_ref, halo(0), send_sem.at[0], recv_sem.at[0], pos, sizes, ca, ct)

    steps = ca * (ct // TILE)

    def tile_at(i):
        a = i // (ct // TILE)
        t0 = pl.multiple_of((i % (ct // TILE)) * TILE, TILE)
        return a, pl.ds(t0, TILE)

    def load(ref, a, ts):
        return [ref[q, a, ts, :] for q in range(NQ)]

    def store(ref, a, ts, vals):
        for q in range(NQ):
            ref[q, a, ts, :] = vals[q]

    def collide_loop(src, dst, grad_dst):
        def body(i, carry):
            a, ts = tile_at(i)
            out, grad = _collide(load(src, a, ts), por_ref[a, ts, :], type_ref[0, a, ts, :],
                                 reg_ref[a, ts, :], with_grad=True)
            store(dst, a, ts, out)
            store(grad_dst, a, ts, grad)
            return carry
        lax.fori_loop(0, steps, body, 0)

    def vjp_loop(at, upstream, primal_dst, grad_dst, sens_dst):
        def body(i, carry):
            a, ts = tile_at(i)
            types = type_ref[0, a, ts, :]
            regions = reg_ref[a, ts, :]
            out, pullback = jax.vjp(
                lambda f, p: _collide(f, p, types, regions), load(at, a, ts), por_ref[a, ts, :])
            if primal_dst is not None:
                store(primal_dst, a, ts, out)
            d_f, d_p = pullback(load(upstream, a, ts))
            store(grad_dst, a, ts, d_f)
            if sens_dst is not None:
                sens_dst[a, ts, :] = d_p
            return carry
        lax.fori_loop(0, steps, body, 0)

    zero = jnp.zeros((ct, nr), jnp.float32)

    def flag_shift(a, oa, ot, orr):
        if oa == 0 and ot == 0 and orr == 0:
            own = type_ref[0, a]
            return jnp.where(own != 1, 1.0, 0.0).astype(jnp.float32)
        ty = _shift(type_ref, ty_halo, 0, a, oa, ot, orr, lo_ok, hi_ok, ca, ct, nr, jnp.ones((ct, nr), jnp.int32))
        return jnp.where(ty != 1, 1.0, 0.0).astype(jnp.float32)

    def fill_masks():
        for a in range(ca):
            for q in range(NQ):
                c = VELOCITY[q]
                fmask[q, a] = flag_shift(a, -c[0], -c[1], -c[2])

    def stream(post, hal, dst, rows=None):
        for a in rows if rows is not None else range(ca):
            for q in range(NQ):
                c = VELOCITY[q]
                moved = _shift(post, hal, q, a, -c[0], -c[1], -c[2], lo_ok, hi_ok, ca, ct, nr, zero)
                ok = fmask[q, a] > 0
                dst[q, a] = jnp.where(ok, moved, post[OPPOSITE[q], a])

    def stream_adjoint(adj, hal, dst, rows=None):
        for a in rows if rows is not None else range(ca):
            centre = fmask[0, a]
            for q in range(NQ):
                c = VELOCITY[q]
                ahead = _shift(adj, hal, q, a, c[0], c[1], c[2], lo_ok, hi_ok, ca, ct, nr, zero)
                blocked = 1.0 - fmask[OPPOSITE[q], a]
                dst[q, a] = centre * ahead + blocked * adj[OPPOSITE[q], a]

    collide_loop(init_ref, post0, gpor)
    loads[1].wait()
    pl.semaphore_wait(barrier, count)
    ex_post0 = Exchange(_pieces(-1), post0, halo(1), send_sem.at[1], recv_sem.at[1], pos, sizes, ca, ct)
    ex_types.start()
    ex_post0.start()
    ex_seed.start()
    ex_types.wait_recv()
    fill_masks()
    ex_post0.wait_recv(0)
    stream(post0, halo(1), state1, [0])
    ex_post0.wait_recv(1)
    stream(post0, halo(1), state1, range(1, ca))
    ex_seed.wait_recv()
    stream_adjoint(seed_ref, halo(0), back1)
    vjp_loop(state1, back1, post1, adj1, sens1)
    ex_post1 = Exchange(_pieces(-1), post1, halo(2), send_sem.at[2], recv_sem.at[2], pos, sizes, ca, ct)
    ex_adj1 = Exchange(_pieces(1), adj1, halo(3), send_sem.at[3], recv_sem.at[3], pos, sizes, ca, ct)
    ex_adj1.start()
    ex_post1.start()
    ex_adj1.wait_recv(0)
    stream_adjoint(adj1, halo(3), back0, [0])
    ex_adj1.wait_recv(1)
    stream_adjoint(adj1, halo(3), back0, range(1, ca))
    for a in range(ca):
        sens0 = back0[0, a] * gpor[0, a]
        for q in range(1, NQ):
            sens0 = sens0 + back0[q, a] * gpor[q, a]
        sens_ref[a] = sens1[a] + sens0

    total = jnp.zeros((1, 1), jnp.float32)
    rid = jnp.zeros((1, 1), jnp.int32)
    for a in range(ca):
        reg = reg_ref[a]
        total = total + jnp.sum(jnp.where(reg > 0, sens_ref[a], 0.0), keepdims=True)
        rid = jnp.maximum(rid, jnp.max(reg, keepdims=True))
    labels = lax.broadcasted_iota(jnp.int32, part_ref.shape, 1) + 1
    part_ref[...] = jnp.where(labels == rid, total, 0.0)
    first = _TotalsStage(part_ref, row_b, send_b, recv_b, local.at[0], me_ax, n_ax,
                         lambda j: (j, me_az))
    first.start()

    vjp_loop(init_ref, back0, None, adj_ref, None)

    first.finish(part_ref)
    own = pltpu.make_async_copy(part_ref, row_a.at[me_az], local.at[1])
    own.start()
    own.wait()
    second = _TotalsStage(row_a.at[me_az], row_a, send_a, recv_a, None, me_az, n_az,
                          lambda j: (me_ax, j))
    second.start()
    ex_post1.wait_recv()
    stream(post1, halo(2), final_ref)
    second.finish(tot_ref)

    for ex in (ex_types, ex_seed, ex_post0, ex_post1, ex_adj1):
        ex.wait_send()


class _TotalsStage:
    def __init__(self, src, rows, send, recv, own_sem, me, n, device):
        self.src, self.rows, self.own_sem, self.me, self.n = src, rows, own_sem, me, n
        self.sends, self.recvs = [], []
        for k in range(1, n):
            to, frm = lax.rem(me + k, n), lax.rem(me + n - k, n)
            self.sends.append(pltpu.make_async_remote_copy(
                src_ref=src, dst_ref=rows.at[me], send_sem=send.at[k], recv_sem=recv.at[me],
                device_id=device(to), device_id_type=MESH))
            self.recvs.append(pltpu.make_async_remote_copy(
                src_ref=src, dst_ref=rows.at[frm], send_sem=send.at[k], recv_sem=recv.at[frm],
                device_id=device(frm), device_id_type=MESH))

    def start(self):
        self.own = None
        if self.own_sem is not None:
            self.own = pltpu.make_async_copy(self.src, self.rows.at[self.me], self.own_sem)
            self.own.start()
        for copy in self.sends:
            copy.start()

    def finish(self, out):
        if self.own is not None:
            self.own.wait()
        for copy in self.recvs:
            copy.wait_recv()
        acc = self.rows[0]
        for j in range(1, self.n):
            acc = acc + self.rows[j]
        for copy in self.sends:
            copy.wait_send()
        out[...] = acc


def window(initial, adjoint_seed, porosity, cell_type, region, n_regions):
    n_ax, n_az = lax.axis_size("ax"), lax.axis_size("az")
    nq, ca, ct, nr = initial.shape
    pop = jax.ShapeDtypeStruct(initial.shape, jnp.float32)
    cells = jax.ShapeDtypeStruct(porosity.shape, jnp.float32)
    vmem = pltpu.VMEM
    f32, i32 = jnp.float32, jnp.int32
    scratch = (
        [vmem(initial.shape, f32), vmem(initial.shape, f32), vmem(porosity.shape, f32),
         vmem((1,) + cell_type.shape, i32), vmem(region.shape, i32), pltpu.SemaphoreType.DMA((5,))]

        + [vmem((nq, ca, ct, nr), f32) for _ in range(8)]
        + [vmem((ca, ct, nr), f32)]
        + [vmem((4, nq, 1, ct, nr), f32), vmem((4, nq, 1, ct, nr), f32),
           vmem((4, nq, ca + 2, 1, nr), f32), vmem((4, nq, ca + 2, 1, nr), f32)]
        + [vmem((1, 1, ct, nr), i32), vmem((1, 1, ct, nr), i32),
           vmem((1, ca + 2, 1, nr), i32), vmem((1, ca + 2, 1, nr), i32)]
        + [pltpu.SemaphoreType.DMA((4, NPIECE)), pltpu.SemaphoreType.DMA((4, NPIECE)),
           pltpu.SemaphoreType.DMA((len(FLAG_PIECES),)), pltpu.SemaphoreType.DMA((len(FLAG_PIECES),))]
        + [vmem((1, n_regions), f32), vmem((n_az, 1, n_regions), f32), vmem((n_ax, 1, n_regions), f32),
           pltpu.SemaphoreType.DMA((n_az,)), pltpu.SemaphoreType.DMA((n_az,)),
           pltpu.SemaphoreType.DMA((n_ax,)), pltpu.SemaphoreType.DMA((n_ax,)),
           pltpu.SemaphoreType.DMA((2,))]
    )
    final, adj, sens, tot = pl.pallas_call(
        functools.partial(_window_kernel, n_ax, n_az),
        out_shape=(pop, pop, cells, jax.ShapeDtypeStruct((1, n_regions), f32)),
        in_specs=[pl.BlockSpec(memory_space=pltpu.HBM)] * 5,
        out_specs=(pl.BlockSpec(memory_space=vmem),) * 4,
        scratch_shapes=scratch,
        compiler_params=pltpu.CompilerParams(collective_id=1, has_side_effects=True,
                                             vmem_limit_bytes=67043328),
    )(initial, adjoint_seed, porosity, cell_type.reshape((1,) + cell_type.shape), region)
    return final, adj, sens, tot


def shards(initial, adjoint_seed, porosity, cell_type, region):
    n_regions = lax.axis_size("ax") * lax.axis_size("az") // 4
    final, adjoint, sensitivity, totals = window(
        initial, adjoint_seed, porosity, cell_type, region, n_regions)
    totals = totals.reshape(-1)
    return (final, adjoint, sensitivity, totals)


def solution(mesh):
    return jax.shard_map(
        shards,
        mesh=mesh,
        in_specs=(
            P(None, "ax", "az", None),
            P(None, "ax", "az", None),
            P("ax", "az", None),
            P("ax", "az", None),
            P("ax", "az", None),
        ),
        out_specs=(P(None, "ax", "az", None), P(None, "ax", "az", None), P("ax", "az", None), P()),
        check_vma=False,
    )
```
